256 devices in a mesh: expert: 64 (over y, z_hi, x, core), tensor: 4 (over z_lo).
Axes of the slice: x: 4, y: 4, z: 8 (z_hi: 2, z_lo: 4; z = z_hi * 4 + z_lo), core: 2. Of those that a mesh axis runs over, the one named last changes fastest.
Arguments:
- tokens: bfloat16 [8192, 2048], P('expert'), may hold values from -6 to 6
- expert_ids: int32 [8192, 8], P('expert'), may hold values from 0 to 127, as said below
- gate_values: float32 [8192, 8], P('expert'), may hold values from 0.25 to 1
- hot_ids: int32 [4], replicated, may hold values from 0 to 127, as said below
- w_gate: bfloat16 [128, 768, 2048], P('expert', 'tensor'), may hold values from -0.125 to 0.125
- w_up: bfloat16 [128, 768, 2048], P('expert', 'tensor'), may hold values from -0.125 to 0.125
- w_down: bfloat16 [128, 768, 2048], P('expert', 'tensor'), may hold values from -0.21875 to 0.21875
Outputs:
- mixed: bfloat16 [8192, 2048], P('expert', 'tensor')
The draws below stay inside these ranges and needn't reach their ends.
Inputs may be any that keep to these rules, and one draw needn't show every extreme that they name: `expert_ids`: rows are taken in micro-spans: micro-span c of a device is its rows c * 32 to (c + 1) * 32 - 1 within each aligned block of 128 rows. Each row names 8 different experts. Every row of micro-span c names hot_ids[c] once. In each micro-span of each device every other expert is named by at least 1 and at most 2 rows, and some by exactly 2. hot_ids[c] is the popular expert of micro-span c; the micro-spans' popular experts are different, and expert 128 - 1 is the popular one of some micro-span.
All inputs are finite; a program needn't handle non-finite values.
Results may differ from the reference program's by a relative error of at most 0.015.
Values may be sent and summed in bfloat16 or wider, within the bound.
No kernel may reach another device: no remote copies, remote signals or barrier semaphores. Data moves between devices by JAX's collectives and lax.ppermute only.
A program may use at most 128 MiB of HBM per device.

```python
import math
import jax
import jax.numpy as jnp
from jax import lax

D = 2048
FF = 768
TOPK = 8
SPANS = 4
EXPERTS = 128
TOKENS = 8192
CROWS = 32
CAP = 2
N_EXPERT = 64
N_TENSOR = 4


def routing_tables(key):
    others = jax.random.permutation(jax.random.fold_in(key, 101), EXPERTS - 1)[:SPANS].astype(jnp.int32)
    top_slot = jax.random.randint(jax.random.fold_in(key, 404), (), 0, SPANS).astype(jnp.int32)
    hot_list = jnp.where(jnp.arange(SPANS, dtype=jnp.int32) == top_slot, EXPERTS - 1, others).astype(jnp.int32)
    block_count = TOKENS // CROWS
    other_count = EXPERTS - 1
    raw_scores = jax.random.randint(jax.random.fold_in(key, 202), (block_count, other_count), 0, 1 << 20)
    ordering = jnp.argsort(raw_scores * other_count + jnp.arange(other_count, dtype=jnp.int32)[None, :], axis=1).astype(jnp.int32)
    pair_slots = jnp.arange(CROWS * (TOPK - 1), dtype=jnp.int32) % other_count
    picked = ordering[:, pair_slots]
    span_of = jnp.arange(block_count, dtype=jnp.int32) % SPANS
    block_hot = hot_list[span_of]
    picked = picked + (picked >= block_hot[:, None]).astype(jnp.int32)
    picked = picked.reshape(block_count, CROWS, TOPK - 1)
    hot_column = jnp.broadcast_to(block_hot[:, None, None], (block_count, CROWS, 1))
    full_rows = jnp.concatenate([picked, hot_column], axis=2)
    shuffle_keys = jax.random.randint(jax.random.fold_in(key, 303), (block_count, CROWS, TOPK), 0, 1 << 20)
    shuffle_order = jnp.argsort(shuffle_keys * TOPK + jnp.arange(TOPK, dtype=jnp.int32)[None, None, :], axis=2)
    full_rows = jnp.take_along_axis(full_rows, shuffle_order, axis=2)
    return (hot_list, full_rows.reshape(TOKENS, TOPK).astype(jnp.int32))


def draw_expert_ids(key, part):
    return routing_tables(key)[1]


def draw_hot_ids(key, part):
    return routing_tables(key)[0]


def steps_of(own_key, dims, pieces, smallest, high):
    factor_of = 1.0
    for dim, shards_of in pieces:
        steps = jax.random.uniform(jax.random.fold_in(jax.random.fold_in(own_key, 6), dim), (shards_of,), jnp.float32, smallest / len(pieces), high / len(pieces))
        factor_of = factor_of * jnp.repeat(jnp.exp(steps), dims[dim] // shards_of).reshape((-1,) + (1,) * (len(dims) - 1 - dim))
    return factor_of


def normal_values(own_key, shape, width, reach, pieces=(), kind=jnp.bfloat16):
    factor_of = steps_of(own_key, shape, pieces, -0.22, 0.18) if pieces else 1.0
    array = jax.random.normal(own_key, shape, jnp.float32) * width * factor_of
    return jnp.minimum(jnp.maximum(array, -reach), reach).astype(kind)


def setup_inputs(seed: int = 0) -> dict:
    keys = jax.random.split(jax.random.key(seed), 8)
    return {
        "tokens": normal_values(keys[0], (TOKENS, D), 1.0, 6.0, ((0, 64),)),
        "expert_ids": draw_expert_ids(jax.random.fold_in(keys[7], 71), 0),
        "gate_values": jnp.clip(jnp.exp(math.log(1.0) - 1.3862944 * jax.random.uniform(keys[2], (TOKENS, TOPK), jnp.float32) ** steps_of(keys[2], (TOKENS, TOPK), ((0, 64),), -0.2, 0.2)), 0.25, 1.0),
        "hot_ids": draw_hot_ids(jax.random.fold_in(keys[7], 71), 0),
        "w_gate": normal_values(keys[4], (EXPERTS, FF, D), D ** -0.5, 0.125, ((0, 64), (1, 4))),
        "w_up": normal_values(keys[5], (EXPERTS, FF, D), D ** -0.5, 0.125, ((0, 64), (1, 4))),
        "w_down": normal_values(keys[6], (EXPERTS, FF, D), FF ** -0.5, 0.21875, ((0, 64), (1, 4))),
    }


def expert_rows(row_block, gate_mat, up_mat, down_mat):
    gate_proj = jnp.dot(row_block, gate_mat.T, preferred_element_type=jnp.float32)
    up_proj = jnp.dot(row_block, up_mat.T, preferred_element_type=jnp.float32)
    hidden = (jax.nn.silu(gate_proj) * up_proj).astype(jnp.bfloat16)
    shard_units = FF // N_TENSOR
    hidden_parts = hidden.reshape(row_block.shape[0], N_TENSOR, shard_units).astype(jnp.float32)
    down_parts = down_mat.reshape(N_TENSOR, shard_units, D).astype(jnp.float32)
    partial_value = jnp.einsum("rsf,sfd->srd", hidden_parts, down_parts).astype(jnp.bfloat16)
    partial_value = lax.optimization_barrier(partial_value)
    summed = jnp.sum(partial_value.astype(jnp.float32), axis=0)
    return lax.optimization_barrier(summed.astype(jnp.bfloat16))


def reference(tokens, expert_ids, gate_values, hot_ids, w_gate, w_up, w_down):
    block_count = TOKENS // CROWS
    buffer_rows = block_count * CAP
    span_of_row = (jnp.arange(TOKENS, dtype=jnp.int32) // CROWS) % SPANS
    row_hot = hot_ids[span_of_row]
    is_hot = expert_ids == row_hot[:, None]

    def per_expert(carry, expert):
        named = jnp.logical_and(expert_ids == expert, jnp.logical_not(is_hot))
        token_mask = jnp.any(named, axis=1)
        token_gate = jnp.sum(jnp.where(named, gate_values, jnp.zeros_like(gate_values)), axis=1)
        position = (jnp.cumsum(token_mask.astype(jnp.int32)) - 1).astype(jnp.int32)
        target = jnp.where(token_mask, position, buffer_rows).astype(jnp.int32)
        gathered = jnp.zeros((buffer_rows, D), tokens.dtype).at[target].set(tokens, mode="drop")
        result = expert_rows(gathered, w_gate[expert], w_up[expert], w_down[expert])
        picked = jnp.take(result, jnp.where(token_mask, position, 0).astype(jnp.int32), axis=0).astype(jnp.float32)
        return carry + token_gate[:, None] * picked, None

    total, _ = lax.scan(per_expert, jnp.zeros((TOKENS, D), jnp.float32), jnp.arange(EXPERTS, dtype=jnp.int32))
    for span_idx in range(SPANS):
        grouped = tokens.reshape(N_EXPERT, SPANS, CROWS, D)[:, span_idx].reshape(N_EXPERT * CROWS, D)
        ids_span = expert_ids.reshape(N_EXPERT, SPANS, CROWS, TOPK)[:, span_idx].reshape(N_EXPERT * CROWS, TOPK)
        gates_span = gate_values.reshape(N_EXPERT, SPANS, CROWS, TOPK)[:, span_idx].reshape(N_EXPERT * CROWS, TOPK)
        hot_expert = hot_ids[span_idx]
        hot_weight = jnp.sum(jnp.where(ids_span == hot_expert, gates_span, jnp.zeros_like(gates_span)), axis=1)
        result = expert_rows(grouped, w_gate[hot_expert], w_up[hot_expert], w_down[hot_expert]).astype(jnp.float32)
        contribution = (hot_weight[:, None] * result).reshape(N_EXPERT, CROWS, D)
        total = total.reshape(N_EXPERT, SPANS, CROWS, D).at[:, span_idx].add(contribution).reshape(TOKENS, D)
    return total.astype(jnp.bfloat16)
```

```python
import jax
import jax.numpy as jnp
from jax import lax
from jax.sharding import Mesh, PartitionSpec as P

SPANS = 4
CAPACITY = 2
SWAP = ((0, 1), (1, 0))


def dot(a, b, dims):
    return lax.dot_general(a, b, (dims, ((), ())), preferred_element_type=jnp.float32)


def hot_round(turn, held, wanted, chunks, zh, c):
    chip_of, core_of, local_of, order_of = wanted
    my_chip = (lax.axis_index("y") * 2 + zh) * 4 + lax.axis_index("x")
    mine = (chip_of == my_chip) & (order_of == turn)
    local = jnp.sum(jnp.where(mine, local_of, 0))
    core = jnp.sum(jnp.where(mine, core_of, 0))
    rows = jnp.concatenate(
        [lax.dynamic_index_in_dim(w, local, 0, keepdims=False) for w in held], axis=0
    )
    half = rows.shape[0] // 2
    keep = lax.dynamic_slice_in_dim(rows, c * half, half, 0)
    give = lax.dynamic_slice_in_dim(rows, (1 - c) * half, half, 0)
    got = lax.ppermute(give, "c", SWAP)
    part = jnp.where(core == c, keep, got)
    part = part.reshape(half, 16, -1).transpose(1, 0, 2)
    part = lax.all_to_all(part, ("y", "x"), 0, 0, tiled=True)
    new = []
    for span in range(SPANS):
        chip = chip_of[span]
        source = chip // 8 * 4 + chip % 4
        here = (chip // 4 % 2 == zh) & (order_of[span] == turn)
        found = lax.dynamic_index_in_dim(part, source, 0, keepdims=False)
        new.append(jnp.where(here, found, chunks[span]))
    return jnp.stack(new)


def fetch_hot(hot_ids, held, zh, c):
    device_of = hot_ids // 2
    chip_of, core_of, local_of = device_of // 2, device_of % 2, hot_ids % 2
    before = jnp.arange(SPANS)[None, :] < jnp.arange(SPANS)[:, None]
    order_of = jnp.sum((chip_of[:, None] == chip_of[None, :]) & before, axis=1)
    wanted = (chip_of, core_of, local_of, order_of)
    half = 3 * held[0].shape[1] // 2
    width = held[0].shape[2] // 16
    chunks = jnp.zeros((SPANS, half, width), jnp.bfloat16)
    chunks = hot_round(0, held, wanted, chunks, zh, c)
    turns = jnp.max(order_of) + 1
    chunks = lax.fori_loop(
        1, turns, lambda turn, got: hot_round(turn, held, wanted, got, zh, c), chunks
    )
    give = lax.dynamic_slice_in_dim(chunks, 2 * (1 - zh), 2, 0)
    got = lax.ppermute(give, "zh", SWAP)
    keep = lax.dynamic_slice_in_dim(chunks, 2 * zh, 2, 0)
    zh_of = lax.dynamic_slice_in_dim(chip_of // 4 % 2, 2 * zh, 2, 0)
    pair = jnp.where((zh_of == zh)[:, None, None], keep, got)
    mine = lax.dynamic_index_in_dim(pair, c, 0, keepdims=False)
    give = lax.dynamic_index_in_dim(pair, 1 - c, 0, keepdims=False)
    got = lax.ppermute(give, "c", SWAP)
    whole = jnp.where(c == 0, jnp.stack([mine, got]), jnp.stack([got, mine]))
    whole = whole.reshape(2 * half, width)
    return lax.all_gather(whole, ("y", "x"), axis=0, tiled=False)


def per_device(tokens, expert_ids, gate_values, hot_ids, w_gate, w_up, w_down):
    zh = lax.axis_index("zh")
    c = lax.axis_index("c")
    tok_dev, model_width = tokens.shape
    top_k = expert_ids.shape[1]
    span_rows = tok_dev // SPANS
    units = w_gate.shape[1]

    hot_parts = fetch_hot(hot_ids, (w_gate, w_up, w_down), zh, c)

    meta = jnp.concatenate([expert_ids.astype(jnp.float32), gate_values], axis=1).T
    tok_z = lax.ppermute(tokens, "zh", SWAP)
    meta_z = lax.ppermute(meta, "zh", SWAP)
    tok_c = lax.ppermute(tokens, "c", SWAP)
    tok_zc = lax.ppermute(tok_z, "c", SWAP)
    meta_c, meta_zc = jnp.split(
        lax.ppermute(jnp.concatenate([meta, meta_z], axis=1), "c", SWAP), 2, axis=1
    )
    tok = jnp.concatenate([tokens, tok_c, tok_z, tok_zc], axis=0)
    meta = jnp.concatenate([meta, meta_c, meta_z, meta_zc], axis=1)
    n_tok = 4 * tok_dev
    ids = meta[:top_k].astype(jnp.int32)
    gates = meta[top_k:]

    group = jnp.arange(n_tok, dtype=jnp.int32) // span_rows
    span_of = group % SPANS
    hot_of = sum(jnp.where(span_of == s, hot_ids[s], 0) for s in range(SPANS))
    is_hot = ids == hot_of[None, :]
    hot_weight = jnp.sum(jnp.where(is_hot, gates, 0.0), axis=0)

    place = jnp.arange(32, dtype=jnp.int32)
    experts = ((place // 8 * 2 + zh) * 4 + place // 2 % 4) * 4 + c * 2 + place % 2
    match = (ids[None] == experts[:, None, None]) & jnp.logical_not(is_hot)[None]
    named = jnp.any(match, axis=1)
    named_gate = jnp.sum(jnp.where(match, gates[None], 0.0), axis=1)
    row = jnp.arange(n_tok, dtype=jnp.int32)
    earlier = (group[:, None] == group[None, :]) & (row[:, None] < row[None, :])
    rank = dot(named.astype(jnp.bfloat16), earlier.astype(jnp.bfloat16), ((1,), (0,)))
    n_group = 4 * SPANS
    slot_group = jnp.arange(n_group * CAPACITY, dtype=jnp.int32) // CAPACITY
    slot_rank = (jnp.arange(n_group * CAPACITY, dtype=jnp.int32) % CAPACITY).astype(jnp.float32)
    chosen = (
        named[:, None, :]
        & (slot_group[:, None] == group[None, :])[None]
        & (rank[:, None, :] == slot_rank[None, :, None])
    )
    n_slot = 32 * n_group * CAPACITY
    pick = chosen.astype(jnp.bfloat16).reshape(n_slot, n_tok)
    mix = jnp.where(chosen, named_gate[:, None, :], 0.0).astype(jnp.bfloat16)
    mix = mix.reshape(n_slot, n_tok)

    send = dot(pick, tok, ((1,), (0,))).astype(jnp.bfloat16)
    send = send.reshape(16, n_slot // 16, model_width)
    received = lax.all_to_all(send, ("y", "x"), 0, 0, tiled=True)
    received = received.reshape(16, 2, n_slot // 32, model_width)
    gate_proj = jnp.einsum("nerd,efd->nerf", received, w_gate, preferred_element_type=jnp.float32)
    up_proj = jnp.einsum("nerd,efd->nerf", received, w_up, preferred_element_type=jnp.float32)
    hidden = (jax.nn.silu(gate_proj) * up_proj).astype(jnp.bfloat16)
    part = jnp.einsum("nerf,efd->nerd", hidden, w_down, preferred_element_type=jnp.float32)
    part = part.astype(jnp.bfloat16).reshape(16, n_slot // 16, model_width)
    returned = lax.all_to_all(part, ("y", "x"), 0, 0, tiled=True)
    returned = returned.reshape(n_slot, model_width)

    my_span = 2 * zh + c
    hot_w = hot_parts.transpose(1, 0, 2).reshape(3 * units, model_width)
    hot_tok = lax.dynamic_slice_in_dim(
        tok.reshape(4, tok_dev, model_width), my_span * span_rows, span_rows, 1
    ).reshape(4 * span_rows, model_width)
    hot_gate = dot(hot_tok, hot_w[:units], ((1,), (1,)))
    hot_up = dot(hot_tok, hot_w[units : 2 * units], ((1,), (1,)))
    hot_hidden = (jax.nn.silu(hot_gate) * hot_up).astype(jnp.bfloat16)
    hot_out = dot(hot_hidden, hot_w[2 * units :], ((1,), (0,))).astype(jnp.bfloat16)
    hot_row = jnp.arange(4 * span_rows, dtype=jnp.int32)
    hot_row = hot_row // span_rows * tok_dev + my_span * span_rows + hot_row % span_rows
    hot_mix = jnp.where(hot_row[:, None] == row[None, :], hot_weight[None, :], 0.0)
    hot_mix = hot_mix.astype(jnp.bfloat16)

    summed = dot(mix, returned, ((0,), (0,))) + dot(hot_mix, hot_out, ((0,), (0,)))
    summed = summed.reshape(2, 2, tok_dev, model_width)
    other = lax.ppermute(summed[:, 1].astype(jnp.bfloat16), "c", SWAP)
    summed = summed[:, 0] + other.astype(jnp.float32)
    summed = jnp.where(zh == 0, summed, summed[::-1]).astype(jnp.bfloat16)
    summed = summed.reshape(2, tok_dev, 4, model_width // 4).transpose(0, 2, 1, 3)
    summed = summed.reshape(8, tok_dev, model_width // 4)
    pieces = lax.all_to_all(summed, ("zh", "t"), 0, 0, tiled=True)
    return jnp.sum(pieces.astype(jnp.float32), axis=0).astype(jnp.bfloat16)


def solution(mesh):
    fine = Mesh(mesh.devices.reshape(4, 2, 4, 2, 4), ("y", "zh", "x", "c", "t"))
    owner = ("y", "zh", "x", "c")
    in_specs = (
        P(owner, None),
        P(owner, None),
        P(owner, None),
        P(),
        P(owner, "t", None),
        P(owner, "t", None),
        P(owner, "t", None),
    )
    return jax.shard_map(
        per_device, mesh=fine, in_specs=in_specs, out_specs=P(owner, "t"), check_vma=False
    )
```

```python
import jax
import jax.numpy as jnp
from jax import lax
from jax.experimental import pallas as pl
from jax.experimental.pallas import tpu as pltpu
from jax.sharding import Mesh, PartitionSpec as P

SPANS = 4
CAPACITY = 2
SWAP = ((0, 1), (1, 0))
VMEM_LIMIT = 32 * 1024 * 1024


def dot(a, b, contract_a, contract_b):
    dims = (((contract_a,), (contract_b,)), ((), ()))
    return lax.dot_general(a, b, dims, preferred_element_type=jnp.float32)


def iota(shape, dim):
    return lax.broadcasted_iota(jnp.int32, shape, dim)


def cost(flops, moved):
    return pl.CostEstimate(flops=flops, bytes_accessed=moved, transcendentals=0)


PARAMS = pltpu.CompilerParams(vmem_limit_bytes=VMEM_LIMIT)


def whole(shape):
    return pl.BlockSpec(shape, lambda *_: (0,) * len(shape))


def chunk_kernel(info, gate_ref, up_ref, down_ref, keep_ref, give_ref):
    units = gate_ref.shape[1]
    mid = units // 2

    def first(out):
        out[0, :units] = gate_ref[0]
        out[0, units:] = up_ref[0, :mid]

    def second(out):
        out[0, :mid] = up_ref[0, mid:]
        out[0, mid:] = down_ref[0]

    @pl.when(info[1] == 0)
    def _():
        first(keep_ref)
        second(give_ref)

    @pl.when(info[1] == 1)
    def _():
        second(keep_ref)
        first(give_ref)


def cut_chunks(local, c, held):
    _, units, width = held[0].shape
    lane = width // 16
    half = 3 * units // 2
    spec = pl.BlockSpec((1, units, lane), lambda n, info: (info[0], 0, n))
    out = pl.BlockSpec((1, half, lane), lambda n, info: (n, 0, 0))
    shape = jax.ShapeDtypeStruct((16, half, lane), jnp.bfloat16)
    return pl.pallas_call(
        chunk_kernel,
        out_shape=(shape, shape),
        grid_spec=pltpu.PrefetchScalarGridSpec(
            num_scalar_prefetch=1, grid=(16,), in_specs=[spec] * 3, out_specs=(out, out)
        ),
        compiler_params=PARAMS,
        cost_estimate=cost(0, 4 * 3 * units * width),
    )(jnp.stack([local, c]).astype(jnp.int32), *held)


def hot_round(turn, held, wanted, chunks, zh, c):
    chip_of, core_of, local_of, order_of = wanted
    my_chip = (lax.axis_index("y") * 2 + zh) * 4 + lax.axis_index("x")
    mine = (chip_of == my_chip) & (order_of == turn)
    local = jnp.sum(jnp.where(mine, local_of, 0))
    core = jnp.sum(jnp.where(mine, core_of, 0))
    keep, give = cut_chunks(local, c, held)
    got = lax.ppermute(give, "c", SWAP)
    part = jnp.where(core == c, keep, got)
    part = lax.all_to_all(part, ("y", "x"), 0, 0, tiled=True)
    new = []
    for span in range(SPANS):
        chip = chip_of[span]
        source = chip // 8 * 4 + chip % 4
        here = (chip // 4 % 2 == zh) & (order_of[span] == turn)
        found = lax.dynamic_index_in_dim(part, source, 0, keepdims=False)
        new.append(jnp.where(here, found, chunks[span]))
    return jnp.stack(new)


def fetch_hot(hot_ids, held, zh, c):
    device_of = hot_ids // 2
    chip_of, core_of, local_of = device_of // 2, device_of % 2, hot_ids % 2
    before = jnp.arange(SPANS)[None, :] < jnp.arange(SPANS)[:, None]
    order_of = jnp.sum((chip_of[:, None] == chip_of[None, :]) & before, axis=1)
    wanted = (chip_of, core_of, local_of, order_of)
    half = 3 * held[0].shape[1] // 2
    width = held[0].shape[2] // 16
    chunks = jnp.zeros((SPANS, half, width), jnp.bfloat16)
    chunks = hot_round(0, held, wanted, chunks, zh, c)
    turns = jnp.max(order_of) + 1
    chunks = lax.fori_loop(
        1, turns, lambda turn, got: hot_round(turn, held, wanted, got, zh, c), chunks
    )
    give = lax.dynamic_slice_in_dim(chunks, 2 * (1 - zh), 2, 0)
    got = lax.ppermute(give, "zh", SWAP)
    keep = lax.dynamic_slice_in_dim(chunks, 2 * zh, 2, 0)
    zh_of = lax.dynamic_slice_in_dim(chip_of // 4 % 2, 2 * zh, 2, 0)
    pair = jnp.where((zh_of == zh)[:, None, None], keep, got)
    mine = lax.dynamic_index_in_dim(pair, c, 0, keepdims=False)
    give = lax.dynamic_index_in_dim(pair, 1 - c, 0, keepdims=False)
    got = lax.ppermute(give, "c", SWAP)
    both = jnp.where(c == 0, jnp.stack([mine, got]), jnp.stack([got, mine]))
    both = both.reshape(2 * half, width)
    return lax.all_gather(both, ("y", "x"), axis=0, tiled=False)


def hot_kernel(info, *refs):
    *tok_refs, w_ref, near_ref, far_ref = refs
    tok = jnp.concatenate([r[...] for r in tok_refs], axis=0)
    units = w_ref.shape[1] // 3
    lane = w_ref.shape[2]
    n_chunk = w_ref.shape[0]
    proj = sum(
        dot(tok[:, n * lane : (n + 1) * lane], w_ref[n, : 2 * units], 1, 1) for n in range(n_chunk)
    )
    hidden = (jax.nn.silu(proj[:, :units]) * proj[:, units:]).astype(jnp.bfloat16)
    half = tok.shape[0] // 2
    for n in range(n_chunk):
        out = dot(hidden, w_ref[n, 2 * units :], 1, 0).astype(jnp.bfloat16)
        near_ref[:, n * lane : (n + 1) * lane] = out[:half]
        far_ref[:, n * lane : (n + 1) * lane] = out[half:]


def hot_ffn(info, blocks, hot_w):
    tok_dev, width = blocks[0].shape
    rows = tok_dev // SPANS
    spec = pl.BlockSpec((rows, width), lambda i, info: (2 * info[4] + info[5], 0))
    shape = jax.ShapeDtypeStruct((2 * rows, width), jnp.bfloat16)
    return pl.pallas_call(
        hot_kernel,
        out_shape=(shape, shape),
        grid_spec=pltpu.PrefetchScalarGridSpec(
            num_scalar_prefetch=1,
            grid=(1,),
            in_specs=[spec] * 4 + [whole(hot_w.shape)],
            out_specs=(whole(shape.shape), whole(shape.shape)),
        ),
        compiler_params=PARAMS,
        cost_estimate=cost(8 * rows * hot_w.size, 2 * hot_w.size + 16 * rows * width),
    )(info, *blocks, hot_w)


def route_kernel(info, meta_ref, a_ref, b_ref, send_ref, mix_ref, hot_mix_ref):
    zh, c = info[4], info[5]
    n_tok = meta_ref.shape[1]
    n_slot = send_ref.shape[0]
    top_k = meta_ref.shape[0] // 2
    tok_dev = n_tok // 2
    span_rows = tok_dev // SPANS

    row = iota((1, n_tok), 1)
    group = row // span_rows
    span = group % SPANS
    hot = sum(jnp.where(span == s, info[s], 0) for s in range(SPANS)).astype(jnp.float32)

    slot = pl.program_id(0) * n_slot + iota((n_slot, 1), 0)
    dest, local = slot // 32, slot // 16 % 2
    expert = ((dest // 4 * 2 + zh) * 4 + dest % 4) * 4 + c * 2 + local
    expert = expert.astype(jnp.float32)
    gate = jnp.zeros((n_slot, n_tok), jnp.float32)
    hits = jnp.zeros((n_slot, n_tok), jnp.float32)
    hot_gate = jnp.zeros((1, n_tok), jnp.float32)
    for k in range(top_k):
        ids, gates = meta_ref[k : k + 1], meta_ref[top_k + k : top_k + k + 1]
        same = expert == ids
        gate = jnp.where(same, gates, gate)
        hits = jnp.where(same, 1.0, hits)
        hot_gate += jnp.where(ids == hot, gates, 0.0)
    named = jnp.where(expert == hot, 0.0, hits)
    before, after = iota((n_tok, n_tok), 0), iota((n_tok, n_tok), 1)
    earlier = (before // span_rows == after // span_rows) & (before < after)
    earlier = jnp.where(earlier, 1.0, 0.0).astype(jnp.bfloat16)
    rank = dot(named.astype(jnp.bfloat16), earlier, 1, 0)
    at = (slot // CAPACITY % (2 * SPANS)) == group
    chosen = (named > 0.5) & at & (rank == (slot % CAPACITY).astype(jnp.float32))
    pick = jnp.where(chosen, 1.0, 0.0).astype(jnp.bfloat16)
    sent = dot(pick[:, :tok_dev], a_ref[...], 1, 0) + dot(pick[:, tok_dev:], b_ref[...], 1, 0)
    send_ref[...] = sent.astype(jnp.bfloat16)
    mix_ref[...] = jnp.where(chosen, gate, 0.0).astype(jnp.bfloat16)
    hot_row = iota((2 * span_rows, 1), 0)
    hot_row = hot_row // span_rows * tok_dev + (2 * zh + c) * span_rows + hot_row % span_rows
    hot_mix_ref[...] = jnp.where(hot_row == row, hot_gate, 0.0).astype(jnp.bfloat16)


def route(info, meta, a, b):
    tok_dev, width = a.shape
    n_slot = 32 * 2 * SPANS * CAPACITY
    steps = 4
    span_rows = tok_dev // SPANS
    shapes = (
        jax.ShapeDtypeStruct((n_slot, width), jnp.bfloat16),
        jax.ShapeDtypeStruct((n_slot, 2 * tok_dev), jnp.bfloat16),
        jax.ShapeDtypeStruct((2 * span_rows, 2 * tok_dev), jnp.bfloat16),
    )
    return pl.pallas_call(
        route_kernel,
        out_shape=shapes,
        grid_spec=pltpu.PrefetchScalarGridSpec(
            num_scalar_prefetch=1,
            grid=(steps,),
            in_specs=[whole(meta.shape), whole(a.shape), whole(b.shape)],
            out_specs=(
                pl.BlockSpec((n_slot // steps, width), lambda i, info: (i, 0)),
                pl.BlockSpec((n_slot // steps, 2 * tok_dev), lambda i, info: (i, 0)),
                whole(shapes[2].shape),
            ),
        ),
        compiler_params=PARAMS,
        cost_estimate=cost(4 * n_slot * tok_dev * width, 2 * width * (n_slot + 2 * tok_dev)),
    )(info, meta, a, b)


def ffn_kernel(x_ref, gate_ref, up_ref, down_ref, out_ref):
    n_src, rows, width = x_ref.shape
    x = x_ref[...].reshape(n_src * rows, width)
    gate = dot(x, gate_ref[0], 1, 1)
    up = dot(x, up_ref[0], 1, 1)
    hidden = (jax.nn.silu(gate) * up).astype(jnp.bfloat16)
    out = dot(hidden, down_ref[0], 1, 0).astype(jnp.bfloat16)
    out_ref[...] = out.reshape(n_src, rows, width)


def ffn(x, w_gate, w_up, w_down):
    n_src, rows, width = x.shape
    exp_dev, units, _ = w_gate.shape
    steps = 2
    block = pl.BlockSpec((n_src // steps, rows // exp_dev, width), lambda e, i: (i, e, 0))
    w_spec = pl.BlockSpec((1, units, width), lambda e, i: (e, 0, 0))
    return pl.pallas_call(
        ffn_kernel,
        out_shape=jax.ShapeDtypeStruct(x.shape, jnp.bfloat16),
        grid=(exp_dev, steps),
        in_specs=[block, w_spec, w_spec, w_spec],
        out_specs=block,
        compiler_params=PARAMS,
        cost_estimate=cost(6 * n_src * rows * units * width, 4 * x.size + 6 * w_gate.size),
    )(x, w_gate, w_up, w_down)


def mix_kernel(mix_ref, hot_mix_ref, ret_ref, hot_ref, own_ref, other_ref):
    out = dot(mix_ref[...], ret_ref[...], 0, 0) + dot(hot_mix_ref[...], hot_ref[...], 0, 0)
    out = out.astype(jnp.bfloat16)
    half = out.shape[0] // 2
    own_ref[0] = out[:half]
    other_ref[0] = out[half:]


def mix_rows(mix, hot_mix, returned, hot):
    n_slot, n_tok = mix.shape
    width = returned.shape[1]
    n_group = lax.axis_size("t")
    cols = width // n_group
    shape = jax.ShapeDtypeStruct((n_group, n_tok // 2, cols), jnp.bfloat16)
    out = pl.BlockSpec((1, n_tok // 2, cols), lambda i: (i, 0, 0))
    return pl.pallas_call(
        mix_kernel,
        out_shape=(shape, shape),
        grid=(n_group,),
        in_specs=[
            whole(mix.shape),
            whole(hot_mix.shape),
            pl.BlockSpec((n_slot, cols), lambda i: (0, i)),
            pl.BlockSpec((hot.shape[0], cols), lambda i: (0, i)),
        ],
        out_specs=(out, out),
        compiler_params=PARAMS,
        cost_estimate=cost(2 * n_slot * n_tok * width, 2 * width * (n_slot + n_tok)),
    )(mix, hot_mix, returned, hot)


def exchange(send):
    rows, width = send.shape
    out = lax.all_to_all(send.reshape(16, rows // 16, width), ("y", "x"), 0, 0, tiled=True)
    return out


def pieces_of(own, other, t, axes, perm_of, first):
    got = lax.ppermute(other, "c", SWAP)
    pieces = []
    n_group = own.shape[0]
    for shift in range(n_group):
        q = (t + shift) % n_group
        piece = lax.dynamic_index_in_dim(own, q, 0, keepdims=False).astype(jnp.float32)
        piece += lax.dynamic_index_in_dim(got, q, 0, keepdims=False).astype(jnp.float32)
        if shift >= first:
            piece = lax.ppermute(piece.astype(jnp.bfloat16), axes, perm_of(shift))
        pieces.append(piece.astype(jnp.float32))
    return pieces


def per_device(tokens, expert_ids, gate_values, hot_ids, w_gate, w_up, w_down):
    zh = lax.axis_index("zh")
    c = lax.axis_index("c")
    t = lax.axis_index("t")
    n_t = lax.axis_size("t")
    info = jnp.concatenate([hot_ids, jnp.stack([zh, c]).astype(jnp.int32)])

    meta = jnp.concatenate([expert_ids.astype(jnp.float32), gate_values], axis=1).T
    tok_z = lax.ppermute(tokens, "zh", SWAP)
    meta_z = lax.ppermute(meta, "zh", SWAP)
    tok_c = lax.ppermute(tokens, "c", SWAP)
    meta_c = lax.ppermute(meta, "c", SWAP)
    tok_zc = lax.ppermute(tok_z, "c", SWAP)
    meta_zc = lax.ppermute(meta_z, "c", SWAP)

    hot_w = fetch_hot(hot_ids, (w_gate, w_up, w_down), zh, c)

    near, near_mix, near_hot_mix = route(
        info, jnp.concatenate([meta, meta_c], axis=1), tokens, tok_c
    )
    near = exchange(near)
    far, far_mix, far_hot_mix = route(
        info, jnp.concatenate([meta_z, meta_zc], axis=1), tok_z, tok_zc
    )
    far = exchange(far)
    n_slot = near_mix.shape[0]
    width = tokens.shape[1]
    near = exchange(ffn(near, w_gate, w_up, w_down).reshape(n_slot, width)).reshape(n_slot, width)
    far = exchange(ffn(far, w_gate, w_up, w_down).reshape(n_slot, width)).reshape(n_slot, width)

    near_hot, far_hot = hot_ffn(info, (tokens, tok_c, tok_z, tok_zc), hot_w)
    own, other = mix_rows(near_mix, near_hot_mix, near, near_hot)
    pieces = pieces_of(
        own, other, t, "t", lambda k: [(i, (i + k) % n_t) for i in range(n_t)], 1
    )
    own, other = mix_rows(far_mix, far_hot_mix, far, far_hot)
    pieces += pieces_of(
        own,
        other,
        t,
        ("zh", "t"),
        lambda k: [(z * n_t + i, (1 - z) * n_t + (i + k) % n_t) for z in (0, 1) for i in range(n_t)],
        0,
    )
    return sum(pieces).astype(jnp.bfloat16)


def solution(mesh):
    fine = Mesh(mesh.devices.reshape(4, 2, 4, 2, 4), ("y", "zh", "x", "c", "t"))
    owner = ("y", "zh", "x", "c")
    in_specs = (
        P(owner, None),
        P(owner, None),
        P(owner, None),
        P(),
        P(owner, "t", None),
        P(owner, "t", None),
        P(owner, "t", None),
    )
    return jax.shard_map(
        per_device, mesh=fine, in_specs=in_specs, out_specs=P(owner, "t"), check_vma=False
    )
```

```python
import jax
import jax.numpy as jnp
from jax import lax
from jax.experimental import pallas as pl
from jax.experimental.pallas import tpu as pltpu
from jax.sharding import Mesh, PartitionSpec as P

SPANS = 4
CAPACITY = 2
TOP_K = 8
SWAP = ((0, 1), (1, 0))
VMEM_LIMIT = 32 * 1024 * 1024


def dot(a, b, contract_a, contract_b):
    dims = (((contract_a,), (contract_b,)), ((), ()))
    return lax.dot_general(a, b, dims, preferred_element_type=jnp.float32)


def iota(shape, dim):
    return lax.broadcasted_iota(jnp.int32, shape, dim)


def cost(flops, moved):
    return pl.CostEstimate(flops=flops, bytes_accessed=moved, transcendentals=0)


PARAMS = pltpu.CompilerParams(vmem_limit_bytes=VMEM_LIMIT)


def whole(shape):
    return pl.BlockSpec(shape, lambda *_: (0,) * len(shape))


CHIP, Z_HI, CORE, TENSOR, TURN = 4, 5, 6, 7, 8


def chip_of(expert):
    return expert >> 2


def order_of(info, span):
    chip = chip_of(info[span])
    return sum(((chip_of(info[s]) == chip) & (s < span)).astype(jnp.int32) for s in range(SPANS))


def my_turn(info):
    return sum(
        jnp.where((chip_of(info[s]) == info[CHIP]) & (order_of(info, s) == info[TURN]), info[s], 0)
        for s in range(SPANS)
    )


def chunk_kernel(info, gate_ref, up_ref, down_ref, keep_ref, give_ref):
    units = gate_ref.shape[1]
    mid = units // 2
    n_chunk, _, lane = keep_ref.shape

    def first(out):
        for n in range(n_chunk):
            at = slice(n * lane, (n + 1) * lane)
            out[n, :units] = gate_ref[0, :, at]
            out[n, units:] = up_ref[0, :mid, at]

    def second(out):
        for n in range(n_chunk):
            at = slice(n * lane, (n + 1) * lane)
            out[n, :mid] = up_ref[0, mid:, at]
            out[n, mid:] = down_ref[0, :, at]

    @pl.when(info[CORE] == 0)
    def _():
        first(keep_ref)
        second(give_ref)

    @pl.when(info[CORE] == 1)
    def _():
        second(keep_ref)
        first(give_ref)


def cut_chunks(info, held):
    _, units, width = held[0].shape
    steps = 4
    half, lane = 3 * units // 2, width // 16
    spec = pl.BlockSpec((1, units, width // steps), lambda n, info: (my_turn(info) & 1, 0, n))
    out = pl.BlockSpec((16 // steps, half, lane), lambda n, info: (n, 0, 0))
    shape = jax.ShapeDtypeStruct((16, half, lane), jnp.bfloat16)
    return pl.pallas_call(
        chunk_kernel,
        out_shape=(shape, shape),
        grid_spec=pltpu.PrefetchScalarGridSpec(
            num_scalar_prefetch=1, grid=(steps,), in_specs=[spec] * 3, out_specs=(out, out)
        ),
        compiler_params=PARAMS,
        cost_estimate=cost(0, 4 * 3 * units * width),
    )(info, *held)


def choose_kernel(info, keep_ref, got_ref, out_ref):
    held_here = ((my_turn(info) >> 1) & 1) == info[CORE]

    @pl.when(held_here)
    def _():
        out_ref[...] = keep_ref[...]

    @pl.when(jnp.logical_not(held_here))
    def _():
        out_ref[...] = got_ref[...]


def choose(info, keep, got):
    return pl.pallas_call(
        choose_kernel,
        out_shape=jax.ShapeDtypeStruct(keep.shape, keep.dtype),
        grid_spec=pltpu.PrefetchScalarGridSpec(
            num_scalar_prefetch=1,
            grid=(1,),
            in_specs=[whole(keep.shape)] * 2,
            out_specs=whole(keep.shape),
        ),
        compiler_params=PARAMS,
        cost_estimate=cost(0, 6 * keep.size),
    )(info, keep, got)


def span_at(info, i):
    return (2 * info[Z_HI] + info[CORE]) ^ i


def take_kernel(info, part_ref, *refs):
    *old_refs, out_ref = refs
    span = span_at(info, pl.program_id(0))
    expert = info[span]
    here = (((expert >> 4) & 1) == info[Z_HI]) & (order_of(info, span) == info[TURN])
    if old_refs:
        out_ref[...] = jnp.where(here, part_ref[...], old_refs[0][...])
    else:
        out_ref[...] = part_ref[...]


def take(info, part, *old):
    block = (1, *part.shape[1:])

    def source(i, info):
        expert = info[span_at(info, i)]
        return ((expert >> 5) * 4 + ((expert >> 2) & 3), 0, 0)

    def same(i, info):
        return (i, 0, 0)

    return pl.pallas_call(
        take_kernel,
        out_shape=jax.ShapeDtypeStruct((SPANS, *part.shape[1:]), part.dtype),
        grid_spec=pltpu.PrefetchScalarGridSpec(
            num_scalar_prefetch=1,
            grid=(SPANS,),
            in_specs=[pl.BlockSpec(block, source)] + [pl.BlockSpec(block, same)] * len(old),
            out_specs=pl.BlockSpec(block, same),
        ),
        compiler_params=PARAMS,
        cost_estimate=cost(0, 16 * block[1] * block[2]),
    )(info, part, *old)


def hot_round(info, held, *old):
    keep, give = cut_chunks(info, held)
    part = choose(info, keep, lax.ppermute(give, "c", SWAP))
    part = lax.all_to_all(part, ("y", "x"), 0, 0, tiled=True)
    return take(info, part, *old)


def pair_kernel(info, chunk_ref, got_ref, mine_ref, give_ref):
    for i, out_ref in enumerate((mine_ref, give_ref)):
        here = ((info[span_at(info, i)] >> 4) & 1) == info[Z_HI]
        out_ref[...] = jnp.where(here, chunk_ref[i], got_ref[i])


def pair(info, chunks, got):
    shape = jax.ShapeDtypeStruct(chunks.shape[1:], chunks.dtype)
    return pl.pallas_call(
        pair_kernel,
        out_shape=(shape, shape),
        grid_spec=pltpu.PrefetchScalarGridSpec(
            num_scalar_prefetch=1,
            grid=(1,),
            in_specs=[whole(got.shape)] * 2,
            out_specs=(whole(shape.shape), whole(shape.shape)),
        ),
        compiler_params=PARAMS,
        cost_estimate=cost(0, 12 * shape.size),
    )(info, chunks, got)


def fetch_hot(info, hot_ids, held, c):
    chips = chip_of(hot_ids)
    before = jnp.arange(SPANS)[None, :] < jnp.arange(SPANS)[:, None]
    turns = 1 + jnp.max(jnp.sum((chips[:, None] == chips[None, :]) & before, axis=1))
    chunks = hot_round(info, held)
    chunks = lax.fori_loop(
        1, turns, lambda turn, old: hot_round(info.at[TURN].set(turn), held, old), chunks
    )
    got = lax.ppermute(chunks[2:], "zh", SWAP)
    mine, give = pair(info, chunks, got)
    got = lax.ppermute(give, "c", SWAP)
    first, second = jnp.where(c == 0, mine, got), jnp.where(c == 0, got, mine)
    return jnp.concatenate([first, second], axis=0)


def along_y(chunk):
    n_y = lax.axis_size("y")
    column = [chunk]
    for k in range(1, n_y):
        column.append(lax.ppermute(chunk, "y", [(i, i ^ k) for i in range(n_y)]))
    return jnp.stack(column)


def shift_x(array, step):
    n_x = lax.axis_size("x")
    return lax.ppermute(array, "x", [(i, (i + step) % n_x) for i in range(n_x)])


def hot_kernel(info, *refs):
    *refs, near_ref, far_ref = refs
    tok_refs, w_refs = refs[:4], refs[4:]
    n_y, rows, lane = w_refs[0].shape
    units = rows // 3
    half = near_ref.shape[0]
    pieces = [(0, i, w_refs[0], i) for i in range(n_y)]
    pieces += [(3, i, w_refs[1], i) for i in range(n_y)]
    pieces += [(1, i, w_refs[2], i) for i in range(n_y)]
    pieces += [(2, i, w_refs[3 + i // 2], i % 2) for i in range(n_y)]

    def columns(far, i):
        start = ((info[CHIP] >> 3 ^ i) * 4 + ((info[CHIP] + far) & 3)) * lane
        return pl.ds(pl.multiple_of(start, lane), lane)

    proj = jnp.zeros((2 * half, 2 * units), jnp.float32)
    for far, i, w_ref, at in pieces:
        tok = jnp.concatenate([r[:, columns(far, i)] for r in tok_refs], axis=0)
        proj += dot(tok, w_ref[at, : 2 * units], 1, 1)
    hidden = (jax.nn.silu(proj[:, :units]) * proj[:, units:]).astype(jnp.bfloat16)
    for far, i, w_ref, at in pieces:
        out = dot(hidden, w_ref[at, 2 * units :], 1, 0).astype(jnp.bfloat16)
        near_ref[:, columns(far, i)] = out[:half]
        far_ref[:, columns(far, i)] = out[half:]


def hot_ffn(info, blocks, hot_w, rows):
    width = blocks[0].shape[1]
    w_size = sum(w.size for w in hot_w)
    spec = pl.BlockSpec((rows, width), lambda i, info: (span_at(info, 0), 0))
    shape = jax.ShapeDtypeStruct((2 * rows, width), jnp.bfloat16)
    return pl.pallas_call(
        hot_kernel,
        out_shape=(shape, shape),
        grid_spec=pltpu.PrefetchScalarGridSpec(
            num_scalar_prefetch=1,
            grid=(1,),
            in_specs=[spec] * 4 + [whole(w.shape) for w in hot_w],
            out_specs=(whole(shape.shape), whole(shape.shape)),
        ),
        compiler_params=PARAMS,
        cost_estimate=cost(8 * rows * w_size, 2 * w_size + 16 * rows * width),
    )(info, *blocks, *hot_w)


def pack(tokens, expert_ids, gate_values):
    tok_dev, width = tokens.shape
    meta = jnp.concatenate([expert_ids.astype(jnp.bfloat16), gate_values.astype(jnp.bfloat16)], axis=1)
    meta = meta.T.reshape(1, -1)
    meta = jnp.pad(meta, ((0, 7), (0, width - meta.shape[1])))
    return jnp.concatenate([tokens, meta], axis=0)


def route_kernel(info, a_ref, b_ref, send_ref, mix_ref, hot_mix_ref):
    zh, c = info[Z_HI], info[CORE]
    n_tok = mix_ref.shape[1]
    n_slot = send_ref.shape[0]
    tok_dev = n_tok // 2
    span_rows = tok_dev // SPANS

    def entry(k):
        at = slice(k * tok_dev, (k + 1) * tok_dev)
        row = jnp.concatenate(
            [a_ref[tok_dev : tok_dev + 8, at], b_ref[tok_dev : tok_dev + 8, at]], axis=1
        )
        return row.astype(jnp.float32)[:1]

    row = iota((1, n_tok), 1)
    group = row // span_rows
    span = group % SPANS
    hot = sum(jnp.where(span == s, info[s], 0) for s in range(SPANS)).astype(jnp.float32)

    slot = pl.program_id(0) * n_slot + iota((n_slot, 1), 0)
    dest, local = slot // 32, slot // 16 % 2
    expert = ((dest // 4 * 2 + zh) * 4 + dest % 4) * 4 + c * 2 + local
    expert = expert.astype(jnp.float32)
    gate = jnp.zeros((n_slot, n_tok), jnp.float32)
    hits = jnp.zeros((n_slot, n_tok), jnp.float32)
    hot_gate = jnp.zeros((1, n_tok), jnp.float32)
    for k in range(TOP_K):
        ids, gates = entry(k), entry(TOP_K + k)
        same = expert == ids
        gate = jnp.where(same, gates, gate)
        hits = jnp.where(same, 1.0, hits)
        hot_gate += jnp.where(ids == hot, gates, 0.0)
    named = jnp.where(expert == hot, 0.0, hits)
    before, after = iota((n_tok, n_tok), 0), iota((n_tok, n_tok), 1)
    earlier = (before // span_rows == after // span_rows) & (before < after)
    earlier = jnp.where(earlier, 1.0, 0.0).astype(jnp.bfloat16)
    rank = dot(named.astype(jnp.bfloat16), earlier, 1, 0)
    at = (slot // CAPACITY % (2 * SPANS)) == group
    chosen = (named > 0.5) & at & (rank == (slot % CAPACITY).astype(jnp.float32))
    pick = jnp.where(chosen, 1.0, 0.0).astype(jnp.bfloat16)
    sent = dot(pick[:, :tok_dev], a_ref[:tok_dev], 1, 0)
    sent += dot(pick[:, tok_dev:], b_ref[:tok_dev], 1, 0)
    send_ref[...] = sent.astype(jnp.bfloat16)
    mix_ref[...] = jnp.where(chosen, gate, 0.0).astype(jnp.bfloat16)
    hot_row = iota((2 * span_rows, 1), 0)
    hot_row = hot_row // span_rows * tok_dev + (2 * zh + c) * span_rows + hot_row % span_rows
    hot_mix_ref[...] = jnp.where(hot_row == row, hot_gate, 0.0).astype(jnp.bfloat16)


def route(info, a, b, tok_dev):
    width = a.shape[1]
    n_slot = 32 * 2 * SPANS * CAPACITY
    steps = 4
    span_rows = tok_dev // SPANS
    shapes = (
        jax.ShapeDtypeStruct((n_slot, width), jnp.bfloat16),
        jax.ShapeDtypeStruct((n_slot, 2 * tok_dev), jnp.bfloat16),
        jax.ShapeDtypeStruct((2 * span_rows, 2 * tok_dev), jnp.bfloat16),
    )
    return pl.pallas_call(
        route_kernel,
        out_shape=shapes,
        grid_spec=pltpu.PrefetchScalarGridSpec(
            num_scalar_prefetch=1,
            grid=(steps,),
            in_specs=[whole(a.shape), whole(b.shape)],
            out_specs=(
                pl.BlockSpec((n_slot // steps, width), lambda i, info: (i, 0)),
                pl.BlockSpec((n_slot // steps, 2 * tok_dev), lambda i, info: (i, 0)),
                whole(shapes[2].shape),
            ),
        ),
        compiler_params=PARAMS,
        cost_estimate=cost(4 * n_slot * tok_dev * width, 2 * width * (n_slot + 2 * tok_dev)),
    )(info, a, b)


def ffn_kernel(x_ref, gate_ref, up_ref, down_ref, out_ref):
    n_src, rows, width = x_ref.shape
    x = x_ref[...].reshape(n_src * rows, width)
    gate = dot(x, gate_ref[0], 1, 1)
    up = dot(x, up_ref[0], 1, 1)
    hidden = (jax.nn.silu(gate) * up).astype(jnp.bfloat16)
    out = dot(hidden, down_ref[0], 1, 0).astype(jnp.bfloat16)
    out_ref[...] = out.reshape(n_src, rows, width)


def ffn(x, w_gate, w_up, w_down):
    n_src, rows, width = x.shape
    exp_dev, units, _ = w_gate.shape
    steps = 2
    block = pl.BlockSpec((n_src // steps, rows // exp_dev, width), lambda e, i: (i, e, 0))
    w_spec = pl.BlockSpec((1, units, width), lambda e, i: (e, 0, 0))
    return pl.pallas_call(
        ffn_kernel,
        out_shape=jax.ShapeDtypeStruct(x.shape, jnp.bfloat16),
        grid=(exp_dev, steps),
        in_specs=[block, w_spec, w_spec, w_spec],
        out_specs=block,
        compiler_params=PARAMS,
        cost_estimate=cost(6 * n_src * rows * units * width, 4 * x.size + 6 * w_gate.size),
    )(x, w_gate, w_up, w_down)


def mix_kernel(info, mix_ref, hot_mix_ref, ret_ref, hot_ref, own_ref, other_ref):
    out = dot(mix_ref[...], ret_ref[...], 0, 0) + dot(hot_mix_ref[...], hot_ref[...], 0, 0)
    out = out.astype(jnp.bfloat16)
    half = out.shape[0] // 2
    own_ref[0] = out[:half]
    other_ref[0] = out[half:]


def mix_rows(info, mix, hot_mix, returned, hot):
    n_slot, n_tok = mix.shape
    width = returned.shape[1]
    n_group = lax.axis_size("t")
    cols = width // n_group
    shape = jax.ShapeDtypeStruct((n_group, n_tok // 2, cols), jnp.bfloat16)
    out = pl.BlockSpec((1, n_tok // 2, cols), lambda i, info: (i, 0, 0))
    return pl.pallas_call(
        mix_kernel,
        out_shape=(shape, shape),
        grid_spec=pltpu.PrefetchScalarGridSpec(
            num_scalar_prefetch=1,
            grid=(n_group,),
            in_specs=[
                whole(mix.shape),
                whole(hot_mix.shape),
                pl.BlockSpec((n_slot, cols), lambda i, info: (0, i ^ info[TENSOR])),
                pl.BlockSpec((hot.shape[0], cols), lambda i, info: (0, i ^ info[TENSOR])),
            ],
            out_specs=(out, out),
        ),
        compiler_params=PARAMS,
        cost_estimate=cost(2 * n_slot * n_tok * width, 2 * width * (n_slot + n_tok)),
    )(info, mix, hot_mix, returned, hot)


def exchange(send):
    rows, width = send.shape
    return lax.all_to_all(send.reshape(16, rows // 16, width), ("y", "x"), 0, 0, tiled=True)


def pieces_of(own, other, axes, perm_of, first):
    got = lax.ppermute(other, "c", SWAP)
    pieces = []
    for shift in range(own.shape[0]):
        piece = own[shift].astype(jnp.float32) + got[shift].astype(jnp.float32)
        if shift >= first:
            piece = lax.ppermute(piece.astype(jnp.bfloat16), axes, perm_of(shift))
        pieces.append(piece.astype(jnp.float32))
    return pieces


def per_device(tokens, expert_ids, gate_values, hot_ids, w_gate, w_up, w_down):
    y, zh, x, c, t = (lax.axis_index(name) for name in ("y", "zh", "x", "c", "t"))
    n_t = lax.axis_size("t")
    tok_dev, width = tokens.shape
    place = jnp.stack([(y * 2 + zh) * 4 + x, zh, c, t, 0]).astype(jnp.int32)
    info = jnp.concatenate([hot_ids, place])
    experts = (w_gate, w_up, w_down)

    own = pack(tokens, expert_ids, gate_values)
    own_z = lax.ppermute(own, "zh", SWAP)
    own_c = lax.ppermute(own, "c", SWAP)
    near, near_mix, near_hot_mix = route(info, own, own_c, tok_dev)
    n_slot = near.shape[0]

    hot_w = fetch_hot(info, hot_ids, experts, c)
    near, own_z = lax.optimization_barrier((near, own_z))
    near = exchange(near)
    hot_w = along_y(hot_w)
    own_zc = lax.ppermute(own_z, "c", SWAP)
    own_zc, hot_w = lax.optimization_barrier((own_zc, hot_w))
    far, far_mix, far_hot_mix = route(info, own_z, own_zc, tok_dev)
    far = exchange(far)
    hot_w = (hot_w, shift_x(hot_w, 1), shift_x(hot_w, -1))
    near, hot_w = lax.optimization_barrier((near, hot_w))
    near = exchange(ffn(near, *experts).reshape(n_slot, width)).reshape(n_slot, width)
    half = hot_w[0].shape[0] // 2
    hot_w += (shift_x(hot_w[1][:half], 1), shift_x(hot_w[2][half:], -1))
    far, hot_w = lax.optimization_barrier((far, hot_w))
    far = exchange(ffn(far, *experts).reshape(n_slot, width)).reshape(n_slot, width)

    near_hot, far_hot = hot_ffn(info, (own, own_c, own_z, own_zc), hot_w, tok_dev // SPANS)
    mine, other = mix_rows(info, near_mix, near_hot_mix, near, near_hot)
    pieces = pieces_of(mine, other, "t", lambda k: [(i, i ^ k) for i in range(n_t)], 1)
    far, pieces = lax.optimization_barrier((far, pieces))
    mine, other = mix_rows(info, far_mix, far_hot_mix, far, far_hot)
    pieces += pieces_of(
        mine,
        other,
        ("zh", "t"),
        lambda k: [(z * n_t + i, (1 - z) * n_t + (i ^ k)) for z in (0, 1) for i in range(n_t)],
        0,
    )
    return sum(pieces).astype(jnp.bfloat16)


def solution(mesh):
    fine = Mesh(mesh.devices.reshape(4, 2, 4, 2, 4), ("y", "zh", "x", "c", "t"))
    owner = ("y", "zh", "x", "c")
    in_specs = (
        P(owner, None),
        P(owner, None),
        P(owner, None),
        P(),
        P(owner, "t", None),
        P(owner, "t", None),
        P(owner, "t", None),
    )
    return jax.shard_map(
        per_device, mesh=fine, in_specs=in_specs, out_specs=P(owner, "t"), check_vma=False
    )
```

```python
import jax
import jax.numpy as jnp
from jax import lax
from jax.experimental import pallas as pl
from jax.experimental.pallas import tpu as pltpu
from jax.sharding import Mesh, PartitionSpec as P

SPANS = 4
CAPACITY = 2
TOP_K = 8
SWAP = ((0, 1), (1, 0))
VMEM_LIMIT = 32 * 1024 * 1024


def dot(a, b, contract_a, contract_b):
    dims = (((contract_a,), (contract_b,)), ((), ()))
    return lax.dot_general(a, b, dims, preferred_element_type=jnp.float32)


def iota(shape, dim):
    return lax.broadcasted_iota(jnp.int32, shape, dim)


def cost(flops, moved):
    return pl.CostEstimate(flops=flops, bytes_accessed=moved, transcendentals=0)


PARAMS = pltpu.CompilerParams(vmem_limit_bytes=VMEM_LIMIT)


def whole(shape):
    return pl.BlockSpec(shape, lambda *_: (0,) * len(shape))


CHIP, Z_HI, CORE, TENSOR, TURN = 4, 5, 6, 7, 8


def chip_of(expert):
    return expert >> 2


def order_of(info, span):
    chip = chip_of(info[span])
    return sum(((chip_of(info[s]) == chip) & (s < span)).astype(jnp.int32) for s in range(SPANS))


def my_turn(info):
    return sum(
        jnp.where((chip_of(info[s]) == info[CHIP]) & (order_of(info, s) == info[TURN]), info[s], 0)
        for s in range(SPANS)
    )


def chunk_kernel(info, gate_ref, up_ref, down_ref, keep_ref, give_ref):
    units = gate_ref.shape[1]
    mid = units // 2
    n_chunk, _, lane = keep_ref.shape

    def first(out):
        for n in range(n_chunk):
            at = slice(n * lane, (n + 1) * lane)
            out[n, :units] = gate_ref[0, :, at]
            out[n, units:] = up_ref[0, :mid, at]

    def second(out):
        for n in range(n_chunk):
            at = slice(n * lane, (n + 1) * lane)
            out[n, :mid] = up_ref[0, mid:, at]
            out[n, mid:] = down_ref[0, :, at]

    @pl.when(info[CORE] == 0)
    def _():
        first(keep_ref)
        second(give_ref)

    @pl.when(info[CORE] == 1)
    def _():
        second(keep_ref)
        first(give_ref)


def cut_chunks(info, held):
    _, units, width = held[0].shape
    steps = 4
    half, lane = 3 * units // 2, width // 16
    spec = pl.BlockSpec((1, units, width // steps), lambda n, info: (my_turn(info) & 1, 0, n))
    out = pl.BlockSpec((16 // steps, half, lane), lambda n, info: (n, 0, 0))
    shape = jax.ShapeDtypeStruct((16, half, lane), jnp.bfloat16)
    return pl.pallas_call(
        chunk_kernel,
        out_shape=(shape, shape),
        grid_spec=pltpu.PrefetchScalarGridSpec(
            num_scalar_prefetch=1, grid=(steps,), in_specs=[spec] * 3, out_specs=(out, out)
        ),
        compiler_params=PARAMS,
        cost_estimate=cost(0, 4 * 3 * units * width),
    )(info, *held)


def choose_kernel(info, keep_ref, got_ref, out_ref):
    held_here = ((my_turn(info) >> 1) & 1) == info[CORE]

    @pl.when(held_here)
    def _():
        out_ref[...] = keep_ref[...]

    @pl.when(jnp.logical_not(held_here))
    def _():
        out_ref[...] = got_ref[...]


def choose(info, keep, got):
    return pl.pallas_call(
        choose_kernel,
        out_shape=jax.ShapeDtypeStruct(keep.shape, keep.dtype),
        grid_spec=pltpu.PrefetchScalarGridSpec(
            num_scalar_prefetch=1,
            grid=(1,),
            in_specs=[whole(keep.shape)] * 2,
            out_specs=whole(keep.shape),
        ),
        compiler_params=PARAMS,
        cost_estimate=cost(0, 6 * keep.size),
    )(info, keep, got)


def span_at(info, i):
    return (2 * info[Z_HI] + info[CORE]) ^ i


def take_kernel(info, part_ref, *refs):
    *old_refs, out_ref = refs
    span = span_at(info, pl.program_id(0))
    expert = info[span]
    here = (((expert >> 4) & 1) == info[Z_HI]) & (order_of(info, span) == info[TURN])
    if old_refs:
        out_ref[...] = jnp.where(here, part_ref[...], old_refs[0][...])
    else:
        out_ref[...] = part_ref[...]


def take(info, part, *old):
    block = (1, *part.shape[1:])

    def source(i, info):
        expert = info[span_at(info, i)]
        return ((expert >> 5) * 4 + ((expert >> 2) & 3), 0, 0)

    def same(i, info):
        return (i, 0, 0)

    return pl.pallas_call(
        take_kernel,
        out_shape=jax.ShapeDtypeStruct((SPANS, *part.shape[1:]), part.dtype),
        grid_spec=pltpu.PrefetchScalarGridSpec(
            num_scalar_prefetch=1,
            grid=(SPANS,),
            in_specs=[pl.BlockSpec(block, source)] + [pl.BlockSpec(block, same)] * len(old),
            out_specs=pl.BlockSpec(block, same),
        ),
        compiler_params=PARAMS,
        cost_estimate=cost(0, 16 * block[1] * block[2]),
    )(info, part, *old)


def hot_round(info, held, *old):
    keep, give = cut_chunks(info, held)
    part = choose(info, keep, lax.ppermute(give, "c", SWAP))
    part = lax.all_to_all(part, ("y", "x"), 0, 0, tiled=True)
    return take(info, part, *old)


def pair_kernel(info, chunk_ref, got_ref, mine_ref, give_ref):
    for i, out_ref in enumerate((mine_ref, give_ref)):
        here = ((info[span_at(info, i)] >> 4) & 1) == info[Z_HI]
        out_ref[...] = jnp.where(here, chunk_ref[i], got_ref[i])


def pair(info, chunks, got):
    shape = jax.ShapeDtypeStruct(chunks.shape[1:], chunks.dtype)
    return pl.pallas_call(
        pair_kernel,
        out_shape=(shape, shape),
        grid_spec=pltpu.PrefetchScalarGridSpec(
            num_scalar_prefetch=1,
            grid=(1,),
            in_specs=[whole(got.shape)] * 2,
            out_specs=(whole(shape.shape), whole(shape.shape)),
        ),
        compiler_params=PARAMS,
        cost_estimate=cost(0, 12 * shape.size),
    )(info, chunks, got)


def fetch_hot(info, hot_ids, held, c):
    chips = chip_of(hot_ids)
    before = jnp.arange(SPANS)[None, :] < jnp.arange(SPANS)[:, None]
    turns = 1 + jnp.max(jnp.sum((chips[:, None] == chips[None, :]) & before, axis=1))
    chunks = hot_round(info, held)
    chunks = lax.fori_loop(
        1, turns, lambda turn, old: hot_round(info.at[TURN].set(turn), held, old), chunks
    )
    got = lax.ppermute(chunks[2:], "zh", SWAP)
    mine, give = pair(info, chunks, got)
    got = lax.ppermute(give, "c", SWAP)
    first, second = jnp.where(c == 0, mine, got), jnp.where(c == 0, got, mine)
    return jnp.concatenate([first, second], axis=0)


def along_y(chunk):
    n_y = lax.axis_size("y")
    column = [chunk]
    for k in range(1, n_y):
        column.append(lax.ppermute(chunk, "y", [(i, i ^ k) for i in range(n_y)]))
    return jnp.stack(column)


def shift_x(array, step):
    n_x = lax.axis_size("x")
    return lax.ppermute(array, "x", [(i, (i + step) % n_x) for i in range(n_x)])


def hot_kernel(info, *refs):
    *refs, far_ref, near_rows = refs
    tok_refs, w_refs, near_refs = refs[:4], refs[4:9], refs[9:]
    n_y, rows, lane = w_refs[0].shape
    units = rows // 3
    half = far_ref.shape[0]
    cols = near_refs[0].shape[1]
    pieces = [(0, i, w_refs[0], i) for i in range(n_y)]
    pieces += [(3, i, w_refs[1], i) for i in range(n_y)]
    pieces += [(1, i, w_refs[2], i) for i in range(n_y)]
    pieces += [(2, i, w_refs[3 + i // 2], i % 2) for i in range(n_y)]

    def columns(far, i):
        start = ((info[CHIP] >> 3 ^ i) * 4 + ((info[CHIP] + far) & 3)) * lane
        return pl.ds(pl.multiple_of(start, lane), lane)

    proj = jnp.zeros((2 * half, 2 * units), jnp.float32)
    for far, i, w_ref, at in pieces:
        tok = jnp.concatenate([r[:, columns(far, i)] for r in tok_refs], axis=0)
        proj += dot(tok, w_ref[at, : 2 * units], 1, 1)
    hidden = (jax.nn.silu(proj[:, :units]) * proj[:, units:]).astype(jnp.bfloat16)
    for far, i, w_ref, at in pieces:
        out = dot(hidden, w_ref[at, 2 * units :], 1, 0).astype(jnp.bfloat16)
        near_rows[:, columns(far, i)] = out[:half]
        far_ref[:, columns(far, i)] = out[half:]
    for i, near_ref in enumerate(near_refs):
        start = pl.multiple_of((info[TENSOR] ^ i) * cols, cols)
        near_ref[...] = near_rows[:, pl.ds(start, cols)]


def hot_ffn(info, blocks, hot_w, rows):
    width = blocks[0].shape[1]
    w_size = sum(w.size for w in hot_w)
    spec = pl.BlockSpec((rows, width), lambda i, info: (span_at(info, 0), 0))
    n_t = lax.axis_size("t")
    shapes = [jax.ShapeDtypeStruct((2 * rows, width // n_t), jnp.bfloat16)] * n_t
    shapes.append(jax.ShapeDtypeStruct((2 * rows, width), jnp.bfloat16))
    *near, far = pl.pallas_call(
        hot_kernel,
        out_shape=shapes,
        grid_spec=pltpu.PrefetchScalarGridSpec(
            num_scalar_prefetch=1,
            grid=(1,),
            in_specs=[spec] * 4 + [whole(w.shape) for w in hot_w],
            out_specs=[whole(shape.shape) for shape in shapes],
            scratch_shapes=[pltpu.VMEM((2 * rows, width), jnp.bfloat16)],
        ),
        compiler_params=PARAMS,
        cost_estimate=cost(8 * rows * w_size, 2 * w_size + 16 * rows * width),
    )(info, *blocks, *hot_w)
    return near, far


def pack(tokens, expert_ids, gate_values):
    tok_dev, width = tokens.shape
    meta = jnp.concatenate([expert_ids.astype(jnp.bfloat16), gate_values.astype(jnp.bfloat16)], axis=1)
    meta = meta.T.reshape(1, -1)
    meta = jnp.pad(meta, ((0, 7), (0, width - meta.shape[1])))
    return jnp.concatenate([tokens, meta], axis=0)


def route_kernel(info, a_ref, b_ref, send_ref, mix_ref, hot_mix_ref):
    zh, c = info[Z_HI], info[CORE]
    n_tok = mix_ref.shape[1]
    n_slot = send_ref.shape[0]
    tok_dev = n_tok // 2
    span_rows = tok_dev // SPANS

    def entry(k):
        at = slice(k * tok_dev, (k + 1) * tok_dev)
        row = jnp.concatenate(
            [a_ref[tok_dev : tok_dev + 8, at], b_ref[tok_dev : tok_dev + 8, at]], axis=1
        )
        return row.astype(jnp.float32)[:1]

    row = iota((1, n_tok), 1)
    group = row // span_rows
    span = group % SPANS
    hot = sum(jnp.where(span == s, info[s], 0) for s in range(SPANS)).astype(jnp.float32)

    slot = pl.program_id(0) * n_slot + iota((n_slot, 1), 0)
    dest, local = slot // 32, slot // 16 % 2
    expert = ((dest // 4 * 2 + zh) * 4 + dest % 4) * 4 + c * 2 + local
    expert = expert.astype(jnp.float32)
    gate = jnp.zeros((n_slot, n_tok), jnp.float32)
    hits = jnp.zeros((n_slot, n_tok), jnp.float32)
    hot_gate = jnp.zeros((1, n_tok), jnp.float32)
    for k in range(TOP_K):
        ids, gates = entry(k), entry(TOP_K + k)
        same = expert == ids
        gate = jnp.where(same, gates, gate)
        hits = jnp.where(same, 1.0, hits)
        hot_gate += jnp.where(ids == hot, gates, 0.0)
    named = jnp.where(expert == hot, 0.0, hits)
    before, after = iota((n_tok, n_tok), 0), iota((n_tok, n_tok), 1)
    earlier = (before // span_rows == after // span_rows) & (before < after)
    earlier = jnp.where(earlier, 1.0, 0.0).astype(jnp.bfloat16)
    rank = dot(named.astype(jnp.bfloat16), earlier, 1, 0)
    at = (slot // CAPACITY % (2 * SPANS)) == group
    chosen = (named > 0.5) & at & (rank == (slot % CAPACITY).astype(jnp.float32))
    pick = jnp.where(chosen, 1.0, 0.0).astype(jnp.bfloat16)
    sent = dot(pick[:, :tok_dev], a_ref[:tok_dev], 1, 0)
    sent += dot(pick[:, tok_dev:], b_ref[:tok_dev], 1, 0)
    send_ref[...] = sent.astype(jnp.bfloat16)
    mix_ref[...] = jnp.where(chosen, gate, 0.0).astype(jnp.bfloat16)
    hot_row = iota((2 * span_rows, 1), 0)
    hot_row = hot_row // span_rows * tok_dev + (2 * zh + c) * span_rows + hot_row % span_rows
    hot_mix_ref[...] = jnp.where(hot_row == row, hot_gate, 0.0).astype(jnp.bfloat16)


def route(info, a, b, tok_dev):
    width = a.shape[1]
    n_slot = 32 * 2 * SPANS * CAPACITY
    steps = 4
    span_rows = tok_dev // SPANS
    shapes = (
        jax.ShapeDtypeStruct((n_slot, width), jnp.bfloat16),
        jax.ShapeDtypeStruct((n_slot, 2 * tok_dev), jnp.bfloat16),
        jax.ShapeDtypeStruct((2 * span_rows, 2 * tok_dev), jnp.bfloat16),
    )
    return pl.pallas_call(
        route_kernel,
        out_shape=shapes,
        grid_spec=pltpu.PrefetchScalarGridSpec(
            num_scalar_prefetch=1,
            grid=(steps,),
            in_specs=[whole(a.shape), whole(b.shape)],
            out_specs=(
                pl.BlockSpec((n_slot // steps, width), lambda i, info: (i, 0)),
                pl.BlockSpec((n_slot // steps, 2 * tok_dev), lambda i, info: (i, 0)),
                whole(shapes[2].shape),
            ),
        ),
        compiler_params=PARAMS,
        cost_estimate=cost(4 * n_slot * tok_dev * width, 2 * width * (n_slot + 2 * tok_dev)),
    )(info, a, b)


def ffn_kernel(info, x_ref, gate_ref, up_ref, down_ref, *out_refs):
    n_src, rows, width = x_ref.shape
    x = x_ref[...].reshape(n_src * rows, width)
    gate = dot(x, gate_ref[0], 1, 1)
    up = dot(x, up_ref[0], 1, 1)
    hidden = (jax.nn.silu(gate) * up).astype(jnp.bfloat16)
    if len(out_refs) == 1:
        out = dot(hidden, down_ref[0], 1, 0).astype(jnp.bfloat16)
        out_refs[0][...] = out.reshape(n_src, rows, width)
        return
    cols = width // len(out_refs)
    for i, out_ref in enumerate(out_refs):
        start = pl.multiple_of((info[TENSOR] ^ i) * cols, cols)
        out = dot(hidden, down_ref[0, :, pl.ds(start, cols)], 1, 0).astype(jnp.bfloat16)
        out_ref[...] = out.reshape(n_src, rows, cols)


def ffn(info, x, w_gate, w_up, w_down, groups):
    n_src, rows, width = x.shape
    exp_dev, units, _ = w_gate.shape
    steps = 2

    def block(cols):
        return pl.BlockSpec((n_src // steps, rows // exp_dev, cols), lambda e, i, info: (i, e, 0))

    w_spec = pl.BlockSpec((1, units, width), lambda e, i, info: (e, 0, 0))
    cols = width // groups
    return pl.pallas_call(
        ffn_kernel,
        out_shape=[jax.ShapeDtypeStruct((n_src, rows, cols), jnp.bfloat16)] * groups,
        grid_spec=pltpu.PrefetchScalarGridSpec(
            num_scalar_prefetch=1,
            grid=(exp_dev, steps),
            in_specs=[block(width), w_spec, w_spec, w_spec],
            out_specs=[block(cols)] * groups,
        ),
        compiler_params=PARAMS,
        cost_estimate=cost(6 * n_src * rows * units * width, 4 * x.size + 6 * w_gate.size),
    )(info, x, w_gate, w_up, w_down)


def mix_kernel(info, mix_ref, hot_mix_ref, ret_ref, hot_ref, own_ref, other_ref):
    out = dot(mix_ref[...], ret_ref[...], 0, 0) + dot(hot_mix_ref[...], hot_ref[...], 0, 0)
    out = out.astype(jnp.bfloat16)
    half = out.shape[0] // 2
    own_ref[0] = out[:half]
    other_ref[0] = out[half:]


def mix_rows(info, mix, hot_mix, returned, hot):
    n_slot, n_tok = mix.shape
    width = returned.shape[1]
    n_group = lax.axis_size("t")
    cols = width // n_group
    shape = jax.ShapeDtypeStruct((n_group, n_tok // 2, cols), jnp.bfloat16)
    out = pl.BlockSpec((1, n_tok // 2, cols), lambda i, info: (i, 0, 0))
    return pl.pallas_call(
        mix_kernel,
        out_shape=(shape, shape),
        grid_spec=pltpu.PrefetchScalarGridSpec(
            num_scalar_prefetch=1,
            grid=(n_group,),
            in_specs=[
                whole(mix.shape),
                whole(hot_mix.shape),
                pl.BlockSpec((n_slot, cols), lambda i, info: (0, i ^ info[TENSOR])),
                pl.BlockSpec((hot.shape[0], cols), lambda i, info: (0, i ^ info[TENSOR])),
            ],
            out_specs=(out, out),
        ),
        compiler_params=PARAMS,
        cost_estimate=cost(2 * n_slot * n_tok * width, 2 * width * (n_slot + n_tok)),
    )(info, mix, hot_mix, returned, hot)


def mix_quarter_kernel(mix_ref, hot_mix_ref, ret_ref, hot_ref, own_ref, other_ref):
    out = dot(mix_ref[...], ret_ref[...], 0, 0) + dot(hot_mix_ref[...], hot_ref[...], 0, 0)
    half = out.shape[0] // 2
    own_ref[...] = out[:half]
    other_ref[...] = out[half:].astype(jnp.bfloat16)


def mix_quarter(mix, hot_mix, returned, hot):
    rows, cols = mix.shape[1] // 2, returned.shape[1]
    return pl.pallas_call(
        mix_quarter_kernel,
        out_shape=(
            jax.ShapeDtypeStruct((rows, cols), jnp.float32),
            jax.ShapeDtypeStruct((rows, cols), jnp.bfloat16),
        ),
        compiler_params=PARAMS,
        cost_estimate=cost(2 * mix.size * cols, 2 * (mix.size + returned.size)),
    )(mix, hot_mix, returned, hot)


def exchange(send):
    return lax.all_to_all(send, ("y", "x"), 0, 0, tiled=True)


def to_t(groups, *shifts):
    pairs = range(len(groups))
    return tuple(lax.ppermute(groups[k], "t", [(i, i ^ k) for i in pairs]) for k in shifts)


def total_of(parts):
    return sum(part.astype(jnp.float32) for part in parts).astype(jnp.bfloat16)


def per_device(tokens, expert_ids, gate_values, hot_ids, w_gate, w_up, w_down):
    y, zh, x, c, t = (lax.axis_index(name) for name in ("y", "zh", "x", "c", "t"))
    n_t = lax.axis_size("t")
    tok_dev, width = tokens.shape
    place = jnp.stack([(y * 2 + zh) * 4 + x, zh, c, t, 0]).astype(jnp.int32)
    info = jnp.concatenate([hot_ids, place])
    experts = (w_gate, w_up, w_down)

    own = pack(tokens, expert_ids, gate_values)
    own_z = lax.ppermute(own, "zh", SWAP)
    own_c = lax.ppermute(own, "c", SWAP)
    near, near_mix, near_hot_mix = route(info, own, own_c, tok_dev)
    n_slot = near.shape[0]
    slots = (16, n_slot // 16, width)

    hot_w = fetch_hot(info, hot_ids, experts, c)
    near, own_z = lax.optimization_barrier((near, own_z))
    near = exchange(near.reshape(slots))
    hot_w = along_y(hot_w)
    own_zc = lax.ppermute(own_z, "c", SWAP)
    own_zc, hot_w = lax.optimization_barrier((own_zc, hot_w))
    far, far_mix, far_hot_mix = route(info, own_z, own_zc, tok_dev)
    far = exchange(far.reshape(slots))
    hot_w = (hot_w, shift_x(hot_w, 1), shift_x(hot_w, -1))
    near = ffn(info, near, *experts, n_t)
    summands = (near[0], *to_t(near, 1, 2))
    far, hot_w, summands = lax.optimization_barrier((far, hot_w, summands))
    near = total_of(summands + to_t(near, 3))
    (far,) = ffn(info, far, *experts, 1)
    far = exchange(far)
    half = hot_w[0].shape[0] // 2
    hot_w += (shift_x(hot_w[1][:half], 1), shift_x(hot_w[2][half:], -1))
    near_hot, far_hot = hot_ffn(info, (own, own_c, own_z, own_zc), hot_w, tok_dev // SPANS)
    near_hot = total_of((near_hot[0], *to_t(near_hot, 1, 2, 3)))
    far, near, near_hot, far_hot = lax.optimization_barrier((far, near, near_hot, far_hot))

    near = exchange(near).reshape(n_slot, width // n_t)
    mine, other = mix_rows(info, far_mix, far_hot_mix, far.reshape(n_slot, width), far_hot)
    got = lax.ppermute(other, "c", SWAP)
    total = jnp.zeros((tok_dev, width // n_t), jnp.float32)
    for k in range(n_t):
        piece = (mine[k].astype(jnp.float32) + got[k].astype(jnp.float32)).astype(jnp.bfloat16)
        there = [(z * n_t + i, (1 - z) * n_t + (i ^ k)) for z in (0, 1) for i in range(n_t)]
        total += lax.ppermute(piece, ("zh", "t"), there).astype(jnp.float32)
    near, total = lax.optimization_barrier((near, total))
    mine, other = mix_quarter(near_mix, near_hot_mix, near, near_hot)
    got = lax.ppermute(other, "c", SWAP)
    return (total + mine + got.astype(jnp.float32)).astype(jnp.bfloat16)


def solution(mesh):
    fine = Mesh(mesh.devices.reshape(4, 2, 4, 2, 4), ("y", "zh", "x", "c", "t"))
    owner = ("y", "zh", "x", "c")
    in_specs = (
        P(owner, None),
        P(owner, None),
        P(owner, None),
        P(),
        P(owner, "t", None),
        P(owner, "t", None),
        P(owner, "t", None),
    )
    return jax.shard_map(
        per_device, mesh=fine, in_specs=in_specs, out_specs=P(owner, "t"), check_vma=False
    )
```

```python
import jax
import jax.numpy as jnp
from jax import lax
from jax.experimental import pallas as pl
from jax.experimental.pallas import tpu as pltpu
from jax.sharding import Mesh, PartitionSpec as P

SPANS = 4
CAPACITY = 2
TOP_K = 8
SWAP = ((0, 1), (1, 0))
VMEM_LIMIT = 32 * 1024 * 1024


def dot(a, b, contract_a, contract_b):
    dims = (((contract_a,), (contract_b,)), ((), ()))
    return lax.dot_general(a, b, dims, preferred_element_type=jnp.float32)


def iota(shape, dim):
    return lax.broadcasted_iota(jnp.int32, shape, dim)


def cost(flops, moved):
    return pl.CostEstimate(flops=flops, bytes_accessed=moved, transcendentals=0)


PARAMS = pltpu.CompilerParams(vmem_limit_bytes=VMEM_LIMIT)


def whole(shape):
    return pl.BlockSpec(shape, lambda *_: (0,) * len(shape))


CHIP, Z_HI, CORE, TENSOR, TURN = 4, 5, 6, 7, 8


def chip_of(expert):
    return expert >> 2


def order_of(info, span):
    chip = chip_of(info[span])
    return sum(((chip_of(info[s]) == chip) & (s < span)).astype(jnp.int32) for s in range(SPANS))


def my_turn(info):
    return sum(
        jnp.where((chip_of(info[s]) == info[CHIP]) & (order_of(info, s) == info[TURN]), info[s], 0)
        for s in range(SPANS)
    )


def chunk_kernel(info, gate_ref, up_ref, down_ref, keep_ref, give_ref):
    units = gate_ref.shape[1]
    mid = units // 2
    n_chunk, _, lane = keep_ref.shape

    def first(out):
        for n in range(n_chunk):
            at = slice(n * lane, (n + 1) * lane)
            out[n, :units] = gate_ref[0, :, at]
            out[n, units:] = up_ref[0, :mid, at]

    def second(out):
        for n in range(n_chunk):
            at = slice(n * lane, (n + 1) * lane)
            out[n, :mid] = up_ref[0, mid:, at]
            out[n, mid:] = down_ref[0, :, at]

    @pl.when(info[CORE] == 0)
    def _():
        first(keep_ref)
        second(give_ref)

    @pl.when(info[CORE] == 1)
    def _():
        second(keep_ref)
        first(give_ref)


def cut_chunks(info, held):
    _, units, width = held[0].shape
    steps = 4
    half, lane = 3 * units // 2, width // 16
    spec = pl.BlockSpec((1, units, width // steps), lambda n, info: (my_turn(info) & 1, 0, n))
    out = pl.BlockSpec((16 // steps, half, lane), lambda n, info: (n, 0, 0))
    shape = jax.ShapeDtypeStruct((16, half, lane), jnp.bfloat16)
    return pl.pallas_call(
        chunk_kernel,
        out_shape=(shape, shape),
        grid_spec=pltpu.PrefetchScalarGridSpec(
            num_scalar_prefetch=1, grid=(steps,), in_specs=[spec] * 3, out_specs=(out, out)
        ),
        compiler_params=PARAMS,
        cost_estimate=cost(0, 4 * 3 * units * width),
    )(info, *held)


def choose_kernel(info, keep_ref, got_ref, out_ref):
    held_here = ((my_turn(info) >> 1) & 1) == info[CORE]

    @pl.when(held_here)
    def _():
        out_ref[...] = keep_ref[...]

    @pl.when(jnp.logical_not(held_here))
    def _():
        out_ref[...] = got_ref[...]


def choose(info, keep, got):
    return pl.pallas_call(
        choose_kernel,
        out_shape=jax.ShapeDtypeStruct(keep.shape, keep.dtype),
        grid_spec=pltpu.PrefetchScalarGridSpec(
            num_scalar_prefetch=1,
            grid=(1,),
            in_specs=[whole(keep.shape)] * 2,
            out_specs=whole(keep.shape),
        ),
        compiler_params=PARAMS,
        cost_estimate=cost(0, 6 * keep.size),
    )(info, keep, got)


def span_at(info, i):
    return (2 * info[Z_HI] + info[CORE]) ^ i


def take_kernel(info, *refs):
    *part_refs, out_ref = refs
    rows = 0
    for part_ref in part_refs:
        out_ref[:, rows : rows + part_ref.shape[1]] = part_ref[...]
        rows += part_ref.shape[1]


def source_of(expert):
    return (expert >> 5) * 4 + ((expert >> 2) & 3)


def take(info, received, first, rows):
    lane = received.shape[2]
    sizes = (256, rows - 256)

    def spec(size, start):
        return pl.BlockSpec(
            (1, size, lane), lambda i, info: (source_of(info[span_at(info, i)]), start // size, 0)
        )

    return pl.pallas_call(
        take_kernel,
        out_shape=jax.ShapeDtypeStruct((SPANS, rows, lane), received.dtype),
        grid_spec=pltpu.PrefetchScalarGridSpec(
            num_scalar_prefetch=1,
            grid=(SPANS,),
            in_specs=[spec(sizes[0], first), spec(sizes[1], first + sizes[0])],
            out_specs=pl.BlockSpec((1, rows, lane), lambda i, info: (i, 0, 0)),
        ),
        compiler_params=PARAMS,
        cost_estimate=cost(0, 16 * rows * lane),
    )(info, received, received)


def take_more_kernel(info, part_ref, old_ref, out_ref):
    span = span_at(info, pl.program_id(0))
    here = (((info[span] >> 4) & 1) == info[Z_HI]) & (order_of(info, span) == info[TURN])
    out_ref[...] = jnp.where(here, part_ref[...], old_ref[...])


def take_more(info, part, old):
    block = (1, *part.shape[1:])
    same = pl.BlockSpec(block, lambda i, info: (i, 0, 0))
    return pl.pallas_call(
        take_more_kernel,
        out_shape=jax.ShapeDtypeStruct(old.shape, old.dtype),
        grid_spec=pltpu.PrefetchScalarGridSpec(
            num_scalar_prefetch=1,
            grid=(SPANS,),
            in_specs=[
                pl.BlockSpec(block, lambda i, info: (source_of(info[span_at(info, i)]), 0, 0)),
                same,
            ],
            out_specs=same,
        ),
        compiler_params=PARAMS,
        cost_estimate=cost(0, 24 * block[1] * block[2]),
    )(info, part, old)


def later_turn(info, held, old):
    keep, give = cut_chunks(info, held)
    part = choose(info, keep, lax.ppermute(give, "c", SWAP))
    part = lax.all_to_all(part, ("y", "x"), 0, 0, tiled=True)
    return take_more(info, part, old)


def pair_kernel(info, chunk_ref, got_ref, mine_ref, give_ref):
    for i, out_ref in enumerate((mine_ref, give_ref)):
        here = ((info[span_at(info, i)] >> 4) & 1) == info[Z_HI]
        out_ref[...] = jnp.where(here, chunk_ref[i], got_ref[i])


def pair(info, chunks, got):
    shape = jax.ShapeDtypeStruct(chunks.shape[1:], chunks.dtype)
    return pl.pallas_call(
        pair_kernel,
        out_shape=(shape, shape),
        grid_spec=pltpu.PrefetchScalarGridSpec(
            num_scalar_prefetch=1,
            grid=(1,),
            in_specs=[whole(got.shape)] * 2,
            out_specs=(whole(shape.shape), whole(shape.shape)),
        ),
        compiler_params=PARAMS,
        cost_estimate=cost(0, 12 * shape.size),
    )(info, chunks, got)


def later_turns(info, hot_ids, held, chunks):
    chips = chip_of(hot_ids)
    before = jnp.arange(SPANS)[None, :] < jnp.arange(SPANS)[:, None]
    turns = 1 + jnp.max(jnp.sum((chips[:, None] == chips[None, :]) & before, axis=1))
    return lax.fori_loop(
        1, turns, lambda turn, old: later_turn(info.at[TURN].set(turn), held, old), chunks
    )


def own_span(info, chunks, c):
    got = lax.ppermute(chunks[2:], "zh", SWAP)
    mine, give = pair(info, chunks, got)
    got = lax.ppermute(give, "c", SWAP)
    first, second = jnp.where(c == 0, mine, got), jnp.where(c == 0, got, mine)
    return jnp.concatenate([first, second], axis=0)


def along_y(chunk):
    n_y = lax.axis_size("y")
    column = [chunk]
    for k in range(1, n_y):
        column.append(lax.ppermute(chunk, "y", [(i, i ^ k) for i in range(n_y)]))
    return jnp.stack(column)


def shift_x(array, step):
    n_x = lax.axis_size("x")
    return lax.ppermute(array, "x", [(i, (i + step) % n_x) for i in range(n_x)])


def hot_kernel(info, *refs):
    *refs, far_ref, near_rows = refs
    tok_refs, w_refs, near_refs = refs[:4], refs[4:9], refs[9:]
    n_y, rows, lane = w_refs[0].shape
    units = rows // 3
    half = far_ref.shape[0]
    cols = near_refs[0].shape[1]
    pieces = [(0, i, w_refs[0], i) for i in range(n_y)]
    pieces += [(3, i, w_refs[1], i) for i in range(n_y)]
    pieces += [(1, i, w_refs[2], i) for i in range(n_y)]
    pieces += [(2, i, w_refs[3 + i // 2], i % 2) for i in range(n_y)]

    def columns(far, i):
        start = ((info[CHIP] >> 3 ^ i) * 4 + ((info[CHIP] + far) & 3)) * lane
        return pl.ds(pl.multiple_of(start, lane), lane)

    proj = jnp.zeros((2 * half, 2 * units), jnp.float32)
    for far, i, w_ref, at in pieces:
        tok = jnp.concatenate([r[:, columns(far, i)] for r in tok_refs], axis=0)
        proj += dot(tok, w_ref[at, : 2 * units], 1, 1)
    hidden = (jax.nn.silu(proj[:, :units]) * proj[:, units:]).astype(jnp.bfloat16)
    for far, i, w_ref, at in pieces:
        out = dot(hidden, w_ref[at, 2 * units :], 1, 0).astype(jnp.bfloat16)
        near_rows[:, columns(far, i)] = out[:half]
        far_ref[:, columns(far, i)] = out[half:]
    for i, near_ref in enumerate(near_refs):
        start = pl.multiple_of((info[TENSOR] ^ i) * cols, cols)
        near_ref[...] = near_rows[:, pl.ds(start, cols)]


def hot_ffn(info, blocks, hot_w, rows):
    width = blocks[0].shape[1]
    w_size = sum(w.size for w in hot_w)
    spec = pl.BlockSpec((rows, width), lambda i, info: (span_at(info, 0), 0))
    n_t = lax.axis_size("t")
    shapes = [jax.ShapeDtypeStruct((2 * rows, width // n_t), jnp.bfloat16)] * n_t
    shapes.append(jax.ShapeDtypeStruct((2 * rows, width), jnp.bfloat16))
    *near, far = pl.pallas_call(
        hot_kernel,
        out_shape=shapes,
        grid_spec=pltpu.PrefetchScalarGridSpec(
            num_scalar_prefetch=1,
            grid=(1,),
            in_specs=[spec] * 4 + [whole(w.shape) for w in hot_w],
            out_specs=[whole(shape.shape) for shape in shapes],
            scratch_shapes=[pltpu.VMEM((2 * rows, width), jnp.bfloat16)],
        ),
        compiler_params=PARAMS,
        cost_estimate=cost(8 * rows * w_size, 2 * w_size + 16 * rows * width),
    )(info, *blocks, *hot_w)
    return near, far


def pack(tokens, expert_ids, gate_values):
    tok_dev, width = tokens.shape
    meta = jnp.concatenate([expert_ids.astype(jnp.bfloat16), gate_values.astype(jnp.bfloat16)], axis=1)
    meta = meta.T.reshape(1, -1)
    meta = jnp.pad(meta, ((0, 7), (0, width - meta.shape[1])))
    return jnp.concatenate([tokens, meta], axis=0)


def route_kernel(info, a_ref, b_ref, *refs):
    *chunk_refs, send_ref, mix_ref, hot_mix_ref = refs
    zh, c = info[Z_HI], info[CORE]
    n_slot, n_tok = mix_ref.shape
    tok_dev = n_tok // 2
    span_rows = tok_dev // SPANS

    def entry(k):
        at = slice(k * tok_dev, (k + 1) * tok_dev)
        row = jnp.concatenate(
            [a_ref[tok_dev : tok_dev + 8, at], b_ref[tok_dev : tok_dev + 8, at]], axis=1
        )
        return row.astype(jnp.float32)[:1]

    row = iota((1, n_tok), 1)
    group = row // span_rows
    span = group % SPANS
    hot = sum(jnp.where(span == s, info[s], 0) for s in range(SPANS)).astype(jnp.float32)

    slot = pl.program_id(0) * n_slot + iota((n_slot, 1), 0)
    dest, local = slot // 32, slot // 16 % 2
    expert = ((dest // 4 * 2 + zh) * 4 + dest % 4) * 4 + c * 2 + local
    expert = expert.astype(jnp.float32)
    gate = jnp.zeros((n_slot, n_tok), jnp.float32)
    hits = jnp.zeros((n_slot, n_tok), jnp.float32)
    hot_gate = jnp.zeros((1, n_tok), jnp.float32)
    for k in range(TOP_K):
        ids, gates = entry(k), entry(TOP_K + k)
        same = expert == ids
        gate = jnp.where(same, gates, gate)
        hits = jnp.where(same, 1.0, hits)
        hot_gate += jnp.where(ids == hot, gates, 0.0)
    named = jnp.where(expert == hot, 0.0, hits)
    before, after = iota((n_tok, n_tok), 0), iota((n_tok, n_tok), 1)
    earlier = (before // span_rows == after // span_rows) & (before < after)
    earlier = jnp.where(earlier, 1.0, 0.0).astype(jnp.bfloat16)
    rank = dot(named.astype(jnp.bfloat16), earlier, 1, 0)
    at = (slot // CAPACITY % (2 * SPANS)) == group
    chosen = (named > 0.5) & at & (rank == (slot % CAPACITY).astype(jnp.float32))
    pick = jnp.where(chosen, 1.0, 0.0).astype(jnp.bfloat16)
    sent = dot(pick[:, :tok_dev], a_ref[:tok_dev], 1, 0)
    sent += dot(pick[:, tok_dev:], b_ref[:tok_dev], 1, 0)
    sent = sent.astype(jnp.bfloat16)
    lane = send_ref.shape[2]
    n_col = sent.shape[1] // lane
    for d in range(n_slot // 32):
        for e in range(2):
            for n in range(n_col):
                at = (e * n_col + n) * 16
                send_ref[d, at : at + 16] = sent[d * 32 + e * 16 : d * 32 + e * 16 + 16, n * lane : (n + 1) * lane]
    if chunk_refs:
        keep_ref, got_ref = chunk_refs
        held_here = ((my_turn(info) >> 1) & 1) == c
        send_ref[:, 32 * n_col :] = jnp.where(held_here, keep_ref[...], got_ref[...])
    mix_ref[...] = jnp.where(chosen, gate, 0.0).astype(jnp.bfloat16)
    hot_row = iota((2 * span_rows, 1), 0)
    hot_row = hot_row // span_rows * tok_dev + (2 * zh + c) * span_rows + hot_row % span_rows
    hot_mix_ref[...] = jnp.where(hot_row == row, hot_gate, 0.0).astype(jnp.bfloat16)


def route(info, a, b, tok_dev, chunks=()):
    width = a.shape[1]
    n_slot = 32 * 2 * SPANS * CAPACITY
    n_dest = 16
    steps = 4
    lane = width // 16
    span_rows = tok_dev // SPANS
    rows = n_slot // n_dest * 16
    chunk_rows = chunks[0].shape[1] if chunks else 0
    shapes = (
        jax.ShapeDtypeStruct((n_dest, rows + chunk_rows, lane), jnp.bfloat16),
        jax.ShapeDtypeStruct((n_slot, 2 * tok_dev), jnp.bfloat16),
        jax.ShapeDtypeStruct((2 * span_rows, 2 * tok_dev), jnp.bfloat16),
    )

    def some(rows):
        return pl.BlockSpec((n_dest // steps, rows, lane), lambda i, info: (i, 0, 0))

    return pl.pallas_call(
        route_kernel,
        out_shape=shapes,
        grid_spec=pltpu.PrefetchScalarGridSpec(
            num_scalar_prefetch=1,
            grid=(steps,),
            in_specs=[whole(a.shape), whole(b.shape)] + [some(chunk_rows)] * len(chunks),
            out_specs=(
                some(rows + chunk_rows),
                pl.BlockSpec((n_slot // steps, 2 * tok_dev), lambda i, info: (i, 0)),
                whole(shapes[2].shape),
            ),
        ),
        compiler_params=PARAMS,
        cost_estimate=cost(4 * n_slot * tok_dev * width, 2 * width * (n_slot + 2 * tok_dev)),
    )(info, a, b, *chunks)


def ffn_kernel(info, x_ref, gate_ref, up_ref, down_ref, *out_refs):
    n_src, _, lane = x_ref.shape
    rows = out_refs[0].shape[1]
    width = gate_ref.shape[2]
    x = jnp.concatenate(
        [
            x_ref[:, n * rows : (n + 1) * rows].reshape(n_src * rows, lane)
            for n in range(width // lane)
        ],
        axis=1,
    )
    gate = dot(x, gate_ref[0], 1, 1)
    up = dot(x, up_ref[0], 1, 1)
    hidden = (jax.nn.silu(gate) * up).astype(jnp.bfloat16)
    if len(out_refs) == 1:
        out = dot(hidden, down_ref[0], 1, 0).astype(jnp.bfloat16)
        out_refs[0][...] = out.reshape(n_src, rows, width)
        return
    cols = width // len(out_refs)
    for i, out_ref in enumerate(out_refs):
        start = pl.multiple_of((info[TENSOR] ^ i) * cols, cols)
        out = dot(hidden, down_ref[0, :, pl.ds(start, cols)], 1, 0).astype(jnp.bfloat16)
        out_ref[...] = out.reshape(n_src, rows, cols)


def ffn(info, x, w_gate, w_up, w_down, groups):
    n_src, _, lane = x.shape
    exp_dev, units, width = w_gate.shape
    rows = exp_dev * 16
    steps = 2
    x_spec = pl.BlockSpec(
        (n_src // steps, 16 * width // lane, lane), lambda e, i, info: (i, e, 0)
    )

    def block(cols):
        return pl.BlockSpec((n_src // steps, rows // exp_dev, cols), lambda e, i, info: (i, e, 0))

    w_spec = pl.BlockSpec((1, units, width), lambda e, i, info: (e, 0, 0))
    cols = width // groups
    return pl.pallas_call(
        ffn_kernel,
        out_shape=[jax.ShapeDtypeStruct((n_src, rows, cols), jnp.bfloat16)] * groups,
        grid_spec=pltpu.PrefetchScalarGridSpec(
            num_scalar_prefetch=1,
            grid=(exp_dev, steps),
            in_specs=[x_spec, w_spec, w_spec, w_spec],
            out_specs=[block(cols)] * groups,
        ),
        compiler_params=PARAMS,
        cost_estimate=cost(6 * n_src * rows * units * width, 4 * x.size + 6 * w_gate.size),
    )(info, x, w_gate, w_up, w_down)


def mix_kernel(info, mix_ref, hot_mix_ref, ret_ref, hot_ref, own_ref, other_ref):
    out = dot(mix_ref[...], ret_ref[...], 0, 0) + dot(hot_mix_ref[...], hot_ref[...], 0, 0)
    out = out.astype(jnp.bfloat16)
    half = out.shape[0] // 2
    own_ref[0] = out[:half]
    other_ref[0] = out[half:]


def mix_rows(info, mix, hot_mix, returned, hot):
    n_slot, n_tok = mix.shape
    width = returned.shape[1]
    n_group = lax.axis_size("t")
    cols = width // n_group
    shape = jax.ShapeDtypeStruct((n_group, n_tok // 2, cols), jnp.bfloat16)
    out = pl.BlockSpec((1, n_tok // 2, cols), lambda i, info: (i, 0, 0))
    return pl.pallas_call(
        mix_kernel,
        out_shape=(shape, shape),
        grid_spec=pltpu.PrefetchScalarGridSpec(
            num_scalar_prefetch=1,
            grid=(n_group,),
            in_specs=[
                whole(mix.shape),
                whole(hot_mix.shape),
                pl.BlockSpec((n_slot, cols), lambda i, info: (0, i ^ info[TENSOR])),
                pl.BlockSpec((hot.shape[0], cols), lambda i, info: (0, i ^ info[TENSOR])),
            ],
            out_specs=(out, out),
        ),
        compiler_params=PARAMS,
        cost_estimate=cost(2 * n_slot * n_tok * width, 2 * width * (n_slot + n_tok)),
    )(info, mix, hot_mix, returned, hot)


def mix_quarter_kernel(mix_ref, hot_mix_ref, ret_ref, hot_ref, own_ref, other_ref):
    out = dot(mix_ref[...], ret_ref[...], 0, 0) + dot(hot_mix_ref[...], hot_ref[...], 0, 0)
    half = out.shape[0] // 2
    own_ref[...] = out[:half]
    other_ref[...] = out[half:].astype(jnp.bfloat16)


def mix_quarter(mix, hot_mix, returned, hot):
    rows, cols = mix.shape[1] // 2, returned.shape[1]
    return pl.pallas_call(
        mix_quarter_kernel,
        out_shape=(
            jax.ShapeDtypeStruct((rows, cols), jnp.float32),
            jax.ShapeDtypeStruct((rows, cols), jnp.bfloat16),
        ),
        compiler_params=PARAMS,
        cost_estimate=cost(2 * mix.size * cols, 2 * (mix.size + returned.size)),
    )(mix, hot_mix, returned, hot)


def exchange(send):
    return lax.all_to_all(send, ("y", "x"), 0, 0, tiled=True)


def to_t(groups, *shifts):
    pairs = range(len(groups))
    return tuple(lax.ppermute(groups[k], "t", [(i, i ^ k) for i in pairs]) for k in shifts)


def total_of(parts):
    return sum(part.astype(jnp.float32) for part in parts).astype(jnp.bfloat16)


def per_device(tokens, expert_ids, gate_values, hot_ids, w_gate, w_up, w_down):
    y, zh, x, c, t = (lax.axis_index(name) for name in ("y", "zh", "x", "c", "t"))
    n_t = lax.axis_size("t")
    tok_dev, width = tokens.shape
    place = jnp.stack([(y * 2 + zh) * 4 + x, zh, c, t, 0]).astype(jnp.int32)
    info = jnp.concatenate([hot_ids, place])
    experts = (w_gate, w_up, w_down)

    own = pack(tokens, expert_ids, gate_values)
    own_z = lax.ppermute(own, "zh", SWAP)
    own_c = lax.ppermute(own, "c", SWAP)
    keep, give = cut_chunks(info, experts)
    got = lax.ppermute(give, "c", SWAP)
    near, near_mix, near_hot_mix = route(info, own, own_c, tok_dev, (keep, got))
    near = exchange(near)
    own_zc = lax.ppermute(own_z, "c", SWAP)
    far, far_mix, far_hot_mix = route(info, own_z, own_zc, tok_dev)
    n_slot = near_mix.shape[0]
    chunks = take(info, near, far.shape[1], keep.shape[1])
    chunks = later_turns(info, hot_ids, experts, chunks)
    chunks, far = lax.optimization_barrier((chunks, far))
    far = exchange(far)
    hot_w = along_y(own_span(info, chunks, c))
    near = ffn(info, near, *experts, n_t)
    summands = (near[0], *to_t(near, 1, 2))
    far, hot_w, summands = lax.optimization_barrier((far, hot_w, summands))
    hot_w = (hot_w, shift_x(hot_w, 1), shift_x(hot_w, -1))
    (far,) = ffn(info, far, *experts, 1)
    far, hot_w = lax.optimization_barrier((far, hot_w))
    near = total_of(summands + to_t(near, 3))
    far = exchange(far)
    half = hot_w[0].shape[0] // 2
    hot_w += (shift_x(hot_w[1][:half], 1), shift_x(hot_w[2][half:], -1))
    near_hot, far_hot = hot_ffn(info, (own, own_c, own_z, own_zc), hot_w, tok_dev // SPANS)
    near_hot = total_of((near_hot[0], *to_t(near_hot, 1, 2, 3)))
    far, near, near_hot, far_hot = lax.optimization_barrier((far, near, near_hot, far_hot))

    near = exchange(near).reshape(n_slot, width // n_t)
    mine, other = mix_rows(info, far_mix, far_hot_mix, far.reshape(n_slot, width), far_hot)
    got = lax.ppermute(other, "c", SWAP)
    total = jnp.zeros((tok_dev, width // n_t), jnp.float32)
    for k in range(n_t):
        piece = (mine[k].astype(jnp.float32) + got[k].astype(jnp.float32)).astype(jnp.bfloat16)
        there = [(z * n_t + i, (1 - z) * n_t + (i ^ k)) for z in (0, 1) for i in range(n_t)]
        total += lax.ppermute(piece, ("zh", "t"), there).astype(jnp.float32)
    near, total = lax.optimization_barrier((near, total))
    mine, other = mix_quarter(near_mix, near_hot_mix, near, near_hot)
    got = lax.ppermute(other, "c", SWAP)
    return (total + mine + got.astype(jnp.float32)).astype(jnp.bfloat16)


def solution(mesh):
    fine = Mesh(mesh.devices.reshape(4, 2, 4, 2, 4), ("y", "zh", "x", "c", "t"))
    owner = ("y", "zh", "x", "c")
    in_specs = (
        P(owner, None),
        P(owner, None),
        P(owner, None),
        P(),
        P(owner, "t", None),
        P(owner, "t", None),
        P(owner, "t", None),
    )
    return jax.shard_map(
        per_device, mesh=fine, in_specs=in_specs, out_specs=P(owner, "t"), check_vma=False
    )
```

```python
import jax
import jax.numpy as jnp
from jax import lax
from jax.experimental import pallas as pl
from jax.experimental.pallas import tpu as pltpu
from jax.sharding import Mesh, PartitionSpec as P

SPANS = 4
CAPACITY = 2
TOP_K = 8
SWAP = ((0, 1), (1, 0))
VMEM_LIMIT = 32 * 1024 * 1024


def dot(a, b, contract_a, contract_b):
    dims = (((contract_a,), (contract_b,)), ((), ()))
    return lax.dot_general(a, b, dims, preferred_element_type=jnp.float32)


def iota(shape, dim):
    return lax.broadcasted_iota(jnp.int32, shape, dim)


def cost(flops, moved):
    return pl.CostEstimate(flops=flops, bytes_accessed=moved, transcendentals=0)


PARAMS = pltpu.CompilerParams(vmem_limit_bytes=VMEM_LIMIT)


def whole(shape):
    return pl.BlockSpec(shape, lambda *_: (0,) * len(shape))


CHIP, Z_HI, CORE, TENSOR, TURN = 4, 5, 6, 7, 8


def chip_of(expert):
    return expert >> 2


def order_of(info, span):
    chip = chip_of(info[span])
    return sum(((chip_of(info[s]) == chip) & (s < span)).astype(jnp.int32) for s in range(SPANS))


def my_turn(info):
    return sum(
        jnp.where((chip_of(info[s]) == info[CHIP]) & (order_of(info, s) == info[TURN]), info[s], 0)
        for s in range(SPANS)
    )


def chunk_kernel(info, gate_ref, up_ref, down_ref, keep_ref, give_ref):
    units = gate_ref.shape[1]
    mid = units // 2
    n_chunk, _, lane = keep_ref.shape

    def first(out):
        for n in range(n_chunk):
            at = slice(n * lane, (n + 1) * lane)
            out[n, :units] = gate_ref[0, :, at]
            out[n, units:] = up_ref[0, :mid, at]

    def second(out):
        for n in range(n_chunk):
            at = slice(n * lane, (n + 1) * lane)
            out[n, :mid] = up_ref[0, mid:, at]
            out[n, mid:] = down_ref[0, :, at]

    @pl.when(info[CORE] == 0)
    def _():
        first(keep_ref)
        second(give_ref)

    @pl.when(info[CORE] == 1)
    def _():
        second(keep_ref)
        first(give_ref)


def cut_chunks(info, held):
    _, units, width = held[0].shape
    steps = 4
    half, lane = 3 * units // 2, width // 16
    spec = pl.BlockSpec((1, units, width // steps), lambda n, info: (my_turn(info) & 1, 0, n))
    out = pl.BlockSpec((16 // steps, half, lane), lambda n, info: (n, 0, 0))
    shape = jax.ShapeDtypeStruct((16, half, lane), jnp.bfloat16)
    return pl.pallas_call(
        chunk_kernel,
        out_shape=(shape, shape),
        grid_spec=pltpu.PrefetchScalarGridSpec(
            num_scalar_prefetch=1, grid=(steps,), in_specs=[spec] * 3, out_specs=(out, out)
        ),
        compiler_params=PARAMS,
        cost_estimate=cost(0, 4 * 3 * units * width),
    )(info, *held)


def choose_kernel(info, keep_ref, got_ref, out_ref):
    held_here = ((my_turn(info) >> 1) & 1) == info[CORE]

    @pl.when(held_here)
    def _():
        out_ref[...] = keep_ref[...]

    @pl.when(jnp.logical_not(held_here))
    def _():
        out_ref[...] = got_ref[...]


def choose(info, keep, got):
    return pl.pallas_call(
        choose_kernel,
        out_shape=jax.ShapeDtypeStruct(keep.shape, keep.dtype),
        grid_spec=pltpu.PrefetchScalarGridSpec(
            num_scalar_prefetch=1,
            grid=(1,),
            in_specs=[whole(keep.shape)] * 2,
            out_specs=whole(keep.shape),
        ),
        compiler_params=PARAMS,
        cost_estimate=cost(0, 6 * keep.size),
    )(info, keep, got)


def span_at(info, i):
    return (2 * info[Z_HI] + info[CORE]) ^ i


def take_kernel(info, part_ref, *refs):
    *old_refs, out_ref = refs
    span = span_at(info, pl.program_id(0))
    expert = info[span]
    here = (((expert >> 4) & 1) == info[Z_HI]) & (order_of(info, span) == info[TURN])
    if old_refs:
        out_ref[...] = jnp.where(here, part_ref[...], old_refs[0][...])
    else:
        out_ref[...] = part_ref[...]


def take(info, part, *old):
    block = (1, *part.shape[1:])

    def source(i, info):
        expert = info[span_at(info, i)]
        return ((expert >> 5) * 4 + ((expert >> 2) & 3), 0, 0)

    def same(i, info):
        return (i, 0, 0)

    return pl.pallas_call(
        take_kernel,
        out_shape=jax.ShapeDtypeStruct((SPANS, *part.shape[1:]), part.dtype),
        grid_spec=pltpu.PrefetchScalarGridSpec(
            num_scalar_prefetch=1,
            grid=(SPANS,),
            in_specs=[pl.BlockSpec(block, source)] + [pl.BlockSpec(block, same)] * len(old),
            out_specs=pl.BlockSpec(block, same),
        ),
        compiler_params=PARAMS,
        cost_estimate=cost(0, 16 * block[1] * block[2]),
    )(info, part, *old)


def hot_round(info, held, *old):
    keep, give = cut_chunks(info, held)
    part = choose(info, keep, lax.ppermute(give, "c", SWAP))
    part = lax.all_to_all(part, ("y", "x"), 0, 0, tiled=True)
    return take(info, part, *old)


def pair_kernel(info, chunk_ref, got_ref, mine_ref, give_ref):
    for i, out_ref in enumerate((mine_ref, give_ref)):
        here = ((info[span_at(info, i)] >> 4) & 1) == info[Z_HI]
        out_ref[...] = jnp.where(here, chunk_ref[i], got_ref[i])


def pair(info, chunks, got):
    shape = jax.ShapeDtypeStruct(chunks.shape[1:], chunks.dtype)
    return pl.pallas_call(
        pair_kernel,
        out_shape=(shape, shape),
        grid_spec=pltpu.PrefetchScalarGridSpec(
            num_scalar_prefetch=1,
            grid=(1,),
            in_specs=[whole(got.shape)] * 2,
            out_specs=(whole(shape.shape), whole(shape.shape)),
        ),
        compiler_params=PARAMS,
        cost_estimate=cost(0, 12 * shape.size),
    )(info, chunks, got)


def first_chunks(info, hot_ids, held):
    chips = chip_of(hot_ids)
    before = jnp.arange(SPANS)[None, :] < jnp.arange(SPANS)[:, None]
    turns = 1 + jnp.max(jnp.sum((chips[:, None] == chips[None, :]) & before, axis=1))
    chunks = hot_round(info, held)
    return lax.fori_loop(
        1, turns, lambda turn, old: hot_round(info.at[TURN].set(turn), held, old), chunks
    )


def own_span(info, chunks, c):
    got = lax.ppermute(chunks[2:], "zh", SWAP)
    mine, give = pair(info, chunks, got)
    got = lax.ppermute(give, "c", SWAP)
    first, second = jnp.where(c == 0, mine, got), jnp.where(c == 0, got, mine)
    return jnp.concatenate([first, second], axis=0)


def along_y(chunk):
    n_y = lax.axis_size("y")
    column = [chunk]
    for k in range(1, n_y):
        column.append(lax.ppermute(chunk, "y", [(i, i ^ k) for i in range(n_y)]))
    return jnp.stack(column)


def shift_x(array, step):
    n_x = lax.axis_size("x")
    return lax.ppermute(array, "x", [(i, (i + step) % n_x) for i in range(n_x)])


def hot_kernel(info, *refs):
    *refs, near_ref, far_rows = refs
    tok_refs, w_refs, far_refs = refs[:4], refs[4:9], refs[9:]
    n_y, rows, lane = w_refs[0].shape
    units = rows // 3
    half = near_ref.shape[0]
    cols = far_refs[0].shape[1]
    pieces = [(0, i, w_refs[0], i) for i in range(n_y)]
    pieces += [(3, i, w_refs[1], i) for i in range(n_y)]
    pieces += [(1, i, w_refs[2], i) for i in range(n_y)]
    pieces += [(2, i, w_refs[3 + i // 2], i % 2) for i in range(n_y)]

    def columns(far, i):
        start = ((info[CHIP] >> 3 ^ i) * 4 + ((info[CHIP] + far) & 3)) * lane
        return pl.ds(pl.multiple_of(start, lane), lane)

    proj = jnp.zeros((2 * half, 2 * units), jnp.float32)
    for far, i, w_ref, at in pieces:
        tok = jnp.concatenate([r[:, columns(far, i)] for r in tok_refs], axis=0)
        proj += dot(tok, w_ref[at, : 2 * units], 1, 1)
    hidden = (jax.nn.silu(proj[:, :units]) * proj[:, units:]).astype(jnp.bfloat16)
    for far, i, w_ref, at in pieces:
        out = dot(hidden, w_ref[at, 2 * units :], 1, 0).astype(jnp.bfloat16)
        far_rows[:, columns(far, i)] = out[:half]
        near_ref[:, columns(far, i)] = out[half:]
    for i, far_ref in enumerate(far_refs):
        start = pl.multiple_of((info[TENSOR] ^ i) * cols, cols)
        far_ref[...] = far_rows[:, pl.ds(start, cols)]


def hot_ffn(info, blocks, hot_w, rows):
    width = blocks[0].shape[1]
    w_size = sum(w.size for w in hot_w)
    spec = pl.BlockSpec((rows, width), lambda i, info: (span_at(info, 0), 0))
    n_t = lax.axis_size("t")
    shapes = [jax.ShapeDtypeStruct((2 * rows, width // n_t), jnp.bfloat16)] * n_t
    shapes.append(jax.ShapeDtypeStruct((2 * rows, width), jnp.bfloat16))
    *far, near = pl.pallas_call(
        hot_kernel,
        out_shape=shapes,
        grid_spec=pltpu.PrefetchScalarGridSpec(
            num_scalar_prefetch=1,
            grid=(1,),
            in_specs=[spec] * 4 + [whole(w.shape) for w in hot_w],
            out_specs=[whole(shape.shape) for shape in shapes],
            scratch_shapes=[pltpu.VMEM((2 * rows, width), jnp.bfloat16)],
        ),
        compiler_params=PARAMS,
        cost_estimate=cost(8 * rows * w_size, 2 * w_size + 16 * rows * width),
    )(info, *blocks, *hot_w)
    return near, far


def pack(tokens, expert_ids, gate_values):
    tok_dev, width = tokens.shape
    meta = jnp.concatenate([expert_ids.astype(jnp.bfloat16), gate_values.astype(jnp.bfloat16)], axis=1)
    meta = meta.T.reshape(1, -1)
    meta = jnp.pad(meta, ((0, 7), (0, width - meta.shape[1])))
    return jnp.concatenate([tokens, meta], axis=0)


def route_kernel(info, a_ref, b_ref, send_ref, mix_ref, hot_mix_ref):
    zh, c = info[Z_HI], info[CORE]
    n_tok = mix_ref.shape[1]
    n_slot = send_ref.shape[0]
    tok_dev = n_tok // 2
    span_rows = tok_dev // SPANS

    def entry(k):
        at = slice(k * tok_dev, (k + 1) * tok_dev)
        row = jnp.concatenate(
            [a_ref[tok_dev : tok_dev + 8, at], b_ref[tok_dev : tok_dev + 8, at]], axis=1
        )
        return row.astype(jnp.float32)[:1]

    row = iota((1, n_tok), 1)
    group = row // span_rows
    span = group % SPANS
    hot = sum(jnp.where(span == s, info[s], 0) for s in range(SPANS)).astype(jnp.float32)

    slot = pl.program_id(0) * n_slot + iota((n_slot, 1), 0)
    dest, local = slot // 32, slot // 16 % 2
    expert = ((dest // 4 * 2 + zh) * 4 + dest % 4) * 4 + c * 2 + local
    expert = expert.astype(jnp.float32)
    gate = jnp.zeros((n_slot, n_tok), jnp.float32)
    hits = jnp.zeros((n_slot, n_tok), jnp.float32)
    hot_gate = jnp.zeros((1, n_tok), jnp.float32)
    for k in range(TOP_K):
        ids, gates = entry(k), entry(TOP_K + k)
        same = expert == ids
        gate = jnp.where(same, gates, gate)
        hits = jnp.where(same, 1.0, hits)
        hot_gate += jnp.where(ids == hot, gates, 0.0)
    named = jnp.where(expert == hot, 0.0, hits)
    before, after = iota((n_tok, n_tok), 0), iota((n_tok, n_tok), 1)
    earlier = (before // span_rows == after // span_rows) & (before < after)
    earlier = jnp.where(earlier, 1.0, 0.0).astype(jnp.bfloat16)
    rank = dot(named.astype(jnp.bfloat16), earlier, 1, 0)
    at = (slot // CAPACITY % (2 * SPANS)) == group
    chosen = (named > 0.5) & at & (rank == (slot % CAPACITY).astype(jnp.float32))
    pick = jnp.where(chosen, 1.0, 0.0).astype(jnp.bfloat16)
    sent = dot(pick[:, :tok_dev], a_ref[:tok_dev], 1, 0)
    sent += dot(pick[:, tok_dev:], b_ref[:tok_dev], 1, 0)
    send_ref[...] = sent.astype(jnp.bfloat16)
    mix_ref[...] = jnp.where(chosen, gate, 0.0).astype(jnp.bfloat16)
    hot_row = iota((2 * span_rows, 1), 0)
    hot_row = hot_row // span_rows * tok_dev + (2 * zh + c) * span_rows + hot_row % span_rows
    hot_mix_ref[...] = jnp.where(hot_row == row, hot_gate, 0.0).astype(jnp.bfloat16)


def route(info, a, b, tok_dev):
    width = a.shape[1]
    n_slot = 32 * 2 * SPANS * CAPACITY
    steps = 4
    span_rows = tok_dev // SPANS
    shapes = (
        jax.ShapeDtypeStruct((n_slot, width), jnp.bfloat16),
        jax.ShapeDtypeStruct((n_slot, 2 * tok_dev), jnp.bfloat16),
        jax.ShapeDtypeStruct((2 * span_rows, 2 * tok_dev), jnp.bfloat16),
    )
    return pl.pallas_call(
        route_kernel,
        out_shape=shapes,
        grid_spec=pltpu.PrefetchScalarGridSpec(
            num_scalar_prefetch=1,
            grid=(steps,),
            in_specs=[whole(a.shape), whole(b.shape)],
            out_specs=(
                pl.BlockSpec((n_slot // steps, width), lambda i, info: (i, 0)),
                pl.BlockSpec((n_slot // steps, 2 * tok_dev), lambda i, info: (i, 0)),
                whole(shapes[2].shape),
            ),
        ),
        compiler_params=PARAMS,
        cost_estimate=cost(4 * n_slot * tok_dev * width, 2 * width * (n_slot + 2 * tok_dev)),
    )(info, a, b)


def ffn_kernel(info, x_ref, gate_ref, up_ref, down_ref, *out_refs):
    n_src, rows, width = x_ref.shape
    x = x_ref[...].reshape(n_src * rows, width)
    gate = dot(x, gate_ref[0], 1, 1)
    up = dot(x, up_ref[0], 1, 1)
    hidden = (jax.nn.silu(gate) * up).astype(jnp.bfloat16)
    if len(out_refs) == 1:
        out = dot(hidden, down_ref[0], 1, 0).astype(jnp.bfloat16)
        out_refs[0][...] = out.reshape(n_src, rows, width)
        return
    cols = width // len(out_refs)
    for i, out_ref in enumerate(out_refs):
        start = pl.multiple_of((info[TENSOR] ^ i) * cols, cols)
        out = dot(hidden, down_ref[0, :, pl.ds(start, cols)], 1, 0).astype(jnp.bfloat16)
        out_ref[...] = out.reshape(n_src, rows, cols)


def ffn(info, x, w_gate, w_up, w_down, groups):
    n_src, rows, width = x.shape
    exp_dev, units, _ = w_gate.shape
    steps = 1

    def block(cols):
        return pl.BlockSpec((n_src // steps, rows // exp_dev, cols), lambda e, i, info: (i, e, 0))

    w_spec = pl.BlockSpec((1, units, width), lambda e, i, info: (e, 0, 0))
    cols = width // groups
    return pl.pallas_call(
        ffn_kernel,
        out_shape=[jax.ShapeDtypeStruct((n_src, rows, cols), jnp.bfloat16)] * groups,
        grid_spec=pltpu.PrefetchScalarGridSpec(
            num_scalar_prefetch=1,
            grid=(exp_dev, steps),
            in_specs=[block(width), w_spec, w_spec, w_spec],
            out_specs=[block(cols)] * groups,
        ),
        compiler_params=PARAMS,
        cost_estimate=cost(6 * n_src * rows * units * width, 4 * x.size + 6 * w_gate.size),
    )(info, x, w_gate, w_up, w_down)


def mix_kernel(info, mix_ref, hot_mix_ref, ret_ref, hot_ref, own_ref, other_ref):
    out = dot(mix_ref[...], ret_ref[...], 0, 0) + dot(hot_mix_ref[...], hot_ref[...], 0, 0)
    out = out.astype(jnp.bfloat16)
    half = out.shape[0] // 2
    own_ref[0] = out[:half]
    other_ref[0] = out[half:]


def mix_rows(info, mix, hot_mix, returned, hot):
    n_slot, n_tok = mix.shape
    width = returned.shape[1]
    n_group = lax.axis_size("t")
    cols = width // n_group
    shape = jax.ShapeDtypeStruct((n_group, n_tok // 2, cols), jnp.bfloat16)
    out = pl.BlockSpec((1, n_tok // 2, cols), lambda i, info: (i, 0, 0))
    return pl.pallas_call(
        mix_kernel,
        out_shape=(shape, shape),
        grid_spec=pltpu.PrefetchScalarGridSpec(
            num_scalar_prefetch=1,
            grid=(n_group,),
            in_specs=[
                whole(mix.shape),
                whole(hot_mix.shape),
                pl.BlockSpec((n_slot, cols), lambda i, info: (0, i ^ info[TENSOR])),
                pl.BlockSpec((hot.shape[0], cols), lambda i, info: (0, i ^ info[TENSOR])),
            ],
            out_specs=(out, out),
        ),
        compiler_params=PARAMS,
        cost_estimate=cost(2 * n_slot * n_tok * width, 2 * width * (n_slot + n_tok)),
    )(info, mix, hot_mix, returned, hot)


def mix_quarter_kernel(mix_ref, hot_mix_ref, ret_ref, hot_ref, own_ref, other_ref):
    out = dot(mix_ref[...], ret_ref[...], 0, 0) + dot(hot_mix_ref[...], hot_ref[...], 0, 0)
    half = out.shape[0] // 2
    own_ref[...] = out[:half]
    other_ref[...] = out[half:].astype(jnp.bfloat16)


def mix_quarter(mix, hot_mix, returned, hot):
    rows, cols = mix.shape[1] // 2, returned.shape[1]
    return pl.pallas_call(
        mix_quarter_kernel,
        out_shape=(
            jax.ShapeDtypeStruct((rows, cols), jnp.float32),
            jax.ShapeDtypeStruct((rows, cols), jnp.bfloat16),
        ),
        compiler_params=PARAMS,
        cost_estimate=cost(2 * mix.size * cols, 2 * (mix.size + returned.size)),
    )(mix, hot_mix, returned, hot)


def exchange(send):
    return lax.all_to_all(send, ("y", "x"), 0, 0, tiled=True)


def to_t(groups, *shifts):
    pairs = range(len(groups))
    return tuple(lax.ppermute(groups[k], "t", [(i, i ^ k) for i in pairs]) for k in shifts)


def total_of(parts):
    return sum(part.astype(jnp.float32) for part in parts).astype(jnp.bfloat16)


def per_device(tokens, expert_ids, gate_values, hot_ids, w_gate, w_up, w_down):
    y, zh, x, c, t = (lax.axis_index(name) for name in ("y", "zh", "x", "c", "t"))
    n_t = lax.axis_size("t")
    tok_dev, width = tokens.shape
    place = jnp.stack([(y * 2 + zh) * 4 + x, zh, c, t, 0]).astype(jnp.int32)
    info = jnp.concatenate([hot_ids, place])
    experts = (w_gate, w_up, w_down)

    own = pack(tokens, expert_ids, gate_values)
    own_z = lax.ppermute(own, "zh", SWAP)
    own_c = lax.ppermute(own, "c", SWAP)
    near, near_mix, near_hot_mix = route(info, own, own_c, tok_dev)
    n_slot = near.shape[0]
    slots = (16, n_slot // 16, width)

    chunks = first_chunks(info, hot_ids, experts)
    near, chunks, own_z = lax.optimization_barrier((near.reshape(slots), chunks, own_z))
    near = exchange(near)
    own_zc = lax.ppermute(own_z, "c", SWAP)
    far, far_mix, far_hot_mix = route(info, own_z, own_zc, tok_dev)
    hot_w = own_span(info, chunks, c)
    far, hot_w = lax.optimization_barrier((far.reshape(slots), hot_w))
    far = exchange(far)
    hot_w = along_y(hot_w)
    (near,) = ffn(info, near, *experts, 1)
    hot_w = (hot_w, shift_x(hot_w, 1), shift_x(hot_w, -1))
    near, hot_w = lax.optimization_barrier((near, hot_w))
    near = exchange(near)
    far = ffn(info, far, *experts, n_t)
    far = total_of((far[0], *to_t(far, 1, 2, 3)))
    half = hot_w[0].shape[0] // 2
    hot_w += (shift_x(hot_w[1][:half], 1), shift_x(hot_w[2][half:], -1))
    near_hot, far_hot = hot_ffn(info, (own_z, own_zc, own, own_c), hot_w, tok_dev // SPANS)
    far_hot = total_of((far_hot[0], *to_t(far_hot, 1, 2, 3)))
    near, far, near_hot, far_hot = lax.optimization_barrier((near, far, near_hot, far_hot))

    far = exchange(far).reshape(n_slot, width // n_t)
    mine, other = mix_rows(info, near_mix, near_hot_mix, near.reshape(n_slot, width), near_hot)
    got = lax.ppermute(other, "c", SWAP)
    pieces = [mine[k].astype(jnp.float32) + got[k].astype(jnp.float32) for k in range(n_t)]
    total = pieces[0]
    for part in to_t([piece.astype(jnp.bfloat16) for piece in pieces], 1, 2, 3):
        total += part.astype(jnp.float32)
    far, total = lax.optimization_barrier((far, total))
    mine, other = mix_quarter(far_mix, far_hot_mix, far, far_hot)
    mine += lax.ppermute(other, "c", SWAP).astype(jnp.float32)
    got = lax.ppermute(mine.astype(jnp.bfloat16), "zh", SWAP)
    return (total + got.astype(jnp.float32)).astype(jnp.bfloat16)


def solution(mesh):
    fine = Mesh(mesh.devices.reshape(4, 2, 4, 2, 4), ("y", "zh", "x", "c", "t"))
    owner = ("y", "zh", "x", "c")
    in_specs = (
        P(owner, None),
        P(owner, None),
        P(owner, None),
        P(),
        P(owner, "t", None),
        P(owner, "t", None),
        P(owner, "t", None),
    )
    return jax.shard_map(
        per_device, mesh=fine, in_specs=in_specs, out_specs=P(owner, "t"), check_vma=False
    )
```

```python
import jax
import jax.numpy as jnp
from jax import lax
from jax.experimental import pallas as pl
from jax.experimental.pallas import tpu as pltpu
from jax.sharding import Mesh, PartitionSpec as P

SPANS = 4
CAPACITY = 2
TOP_K = 8
SWAP = ((0, 1), (1, 0))
VMEM_LIMIT = 32 * 1024 * 1024


def dot(a, b, contract_a, contract_b):
    dims = (((contract_a,), (contract_b,)), ((), ()))
    return lax.dot_general(a, b, dims, preferred_element_type=jnp.float32)


def iota(shape, dim):
    return lax.broadcasted_iota(jnp.int32, shape, dim)


def cost(flops, moved):
    return pl.CostEstimate(flops=flops, bytes_accessed=moved, transcendentals=0)


PARAMS = pltpu.CompilerParams(vmem_limit_bytes=VMEM_LIMIT)


def whole(shape):
    return pl.BlockSpec(shape, lambda *_: (0,) * len(shape))


CHIP, Z_HI, CORE, TENSOR, TURN = 4, 5, 6, 7, 8


def chip_of(expert):
    return expert >> 2


def order_of(info, span):
    chip = chip_of(info[span])
    return sum(((chip_of(info[s]) == chip) & (s < span)).astype(jnp.int32) for s in range(SPANS))


def my_turn(info):
    return sum(
        jnp.where((chip_of(info[s]) == info[CHIP]) & (order_of(info, s) == info[TURN]), info[s], 0)
        for s in range(SPANS)
    )


def chunk_kernel(info, gate_ref, up_ref, down_ref, keep_ref, give_ref):
    units = gate_ref.shape[1]
    mid = units // 2
    n_chunk, _, lane = keep_ref.shape

    def first(out):
        for n in range(n_chunk):
            at = slice(n * lane, (n + 1) * lane)
            out[n, :units] = gate_ref[0, :, at]
            out[n, units:] = up_ref[0, :mid, at]

    def second(out):
        for n in range(n_chunk):
            at = slice(n * lane, (n + 1) * lane)
            out[n, :mid] = up_ref[0, mid:, at]
            out[n, mid:] = down_ref[0, :, at]

    @pl.when(info[CORE] == 0)
    def _():
        first(keep_ref)
        second(give_ref)

    @pl.when(info[CORE] == 1)
    def _():
        second(keep_ref)
        first(give_ref)


def cut_chunks(info, held):
    _, units, width = held[0].shape
    steps = 4
    half, lane = 3 * units // 2, width // 16
    spec = pl.BlockSpec((1, units, width // steps), lambda n, info: (my_turn(info) & 1, 0, n))
    out = pl.BlockSpec((16 // steps, half, lane), lambda n, info: (n, 0, 0))
    shape = jax.ShapeDtypeStruct((16, half, lane), jnp.bfloat16)
    return pl.pallas_call(
        chunk_kernel,
        out_shape=(shape, shape),
        grid_spec=pltpu.PrefetchScalarGridSpec(
            num_scalar_prefetch=1, grid=(steps,), in_specs=[spec] * 3, out_specs=(out, out)
        ),
        compiler_params=PARAMS,
        cost_estimate=cost(0, 4 * 3 * units * width),
    )(info, *held)


def choose_kernel(info, keep_ref, got_ref, out_ref):
    held_here = ((my_turn(info) >> 1) & 1) == info[CORE]

    @pl.when(held_here)
    def _():
        out_ref[...] = keep_ref[...]

    @pl.when(jnp.logical_not(held_here))
    def _():
        out_ref[...] = got_ref[...]


def choose(info, keep, got):
    return pl.pallas_call(
        choose_kernel,
        out_shape=jax.ShapeDtypeStruct(keep.shape, keep.dtype),
        grid_spec=pltpu.PrefetchScalarGridSpec(
            num_scalar_prefetch=1,
            grid=(1,),
            in_specs=[whole(keep.shape)] * 2,
            out_specs=whole(keep.shape),
        ),
        compiler_params=PARAMS,
        cost_estimate=cost(0, 6 * keep.size),
    )(info, keep, got)


def span_at(info, i):
    return (2 * info[Z_HI] + info[CORE]) ^ i


def take_kernel(info, part_ref, *refs):
    *old_refs, out_ref = refs
    span = span_at(info, pl.program_id(0))
    expert = info[span]
    here = (((expert >> 4) & 1) == info[Z_HI]) & (order_of(info, span) == info[TURN])
    if old_refs:
        out_ref[...] = jnp.where(here, part_ref[...], old_refs[0][...])
    else:
        out_ref[...] = part_ref[...]


def take(info, part, *old):
    block = (1, *part.shape[1:])

    def source(i, info):
        expert = info[span_at(info, i)]
        return ((expert >> 5) * 4 + ((expert >> 2) & 3), 0, 0)

    def same(i, info):
        return (i, 0, 0)

    return pl.pallas_call(
        take_kernel,
        out_shape=jax.ShapeDtypeStruct((SPANS, *part.shape[1:]), part.dtype),
        grid_spec=pltpu.PrefetchScalarGridSpec(
            num_scalar_prefetch=1,
            grid=(SPANS,),
            in_specs=[pl.BlockSpec(block, source)] + [pl.BlockSpec(block, same)] * len(old),
            out_specs=pl.BlockSpec(block, same),
        ),
        compiler_params=PARAMS,
        cost_estimate=cost(0, 16 * block[1] * block[2]),
    )(info, part, *old)


def hot_round(info, held, *old):
    keep, give = cut_chunks(info, held)
    part = choose(info, keep, lax.ppermute(give, "c", SWAP))
    part = lax.all_to_all(part, ("y", "x"), 0, 0, tiled=True)
    return take(info, part, *old)


def pair_kernel(info, chunk_ref, got_ref, mine_ref, give_ref):
    for i, out_ref in enumerate((mine_ref, give_ref)):
        here = ((info[span_at(info, i)] >> 4) & 1) == info[Z_HI]
        out_ref[...] = jnp.where(here, chunk_ref[i], got_ref[i])


def pair(info, chunks, got):
    shape = jax.ShapeDtypeStruct(chunks.shape[1:], chunks.dtype)
    return pl.pallas_call(
        pair_kernel,
        out_shape=(shape, shape),
        grid_spec=pltpu.PrefetchScalarGridSpec(
            num_scalar_prefetch=1,
            grid=(1,),
            in_specs=[whole(got.shape)] * 2,
            out_specs=(whole(shape.shape), whole(shape.shape)),
        ),
        compiler_params=PARAMS,
        cost_estimate=cost(0, 12 * shape.size),
    )(info, chunks, got)


def first_chunks(info, hot_ids, held):
    chips = chip_of(hot_ids)
    before = jnp.arange(SPANS)[None, :] < jnp.arange(SPANS)[:, None]
    turns = 1 + jnp.max(jnp.sum((chips[:, None] == chips[None, :]) & before, axis=1))
    chunks = hot_round(info, held)
    return lax.fori_loop(
        1, turns, lambda turn, old: hot_round(info.at[TURN].set(turn), held, old), chunks
    )


def own_span(info, chunks, c):
    got = lax.ppermute(chunks[2:], "zh", SWAP)
    mine, give = pair(info, chunks, got)
    got = lax.ppermute(give, "c", SWAP)
    first, second = jnp.where(c == 0, mine, got), jnp.where(c == 0, got, mine)
    return jnp.concatenate([first, second], axis=0)


def hot_kernel(info, *refs):
    *refs, near_ref, far_rows = refs
    tok_refs, w_ref, far_refs = refs[:4], refs[4], refs[5:]
    n_chunk, rows, lane = w_ref.shape
    units = rows // 3
    half = near_ref.shape[0]
    cols = far_refs[0].shape[1]
    tok = jnp.concatenate([r[...] for r in tok_refs], axis=0)
    proj = jnp.zeros((2 * half, 2 * units), jnp.float32)
    for n in range(n_chunk):
        proj += dot(tok[:, n * lane : (n + 1) * lane], w_ref[n, : 2 * units], 1, 1)
    hidden = (jax.nn.silu(proj[:, :units]) * proj[:, units:]).astype(jnp.bfloat16)
    for n in range(n_chunk):
        out = dot(hidden, w_ref[n, 2 * units :], 1, 0).astype(jnp.bfloat16)
        far_rows[:, n * lane : (n + 1) * lane] = out[:half]
        near_ref[:, n * lane : (n + 1) * lane] = out[half:]
    for i, far_ref in enumerate(far_refs):
        start = pl.multiple_of((info[TENSOR] ^ i) * cols, cols)
        far_ref[...] = far_rows[:, pl.ds(start, cols)]


def hot_ffn(info, blocks, hot_w, rows):
    width = blocks[0].shape[1]
    w_size = hot_w.size
    spec = pl.BlockSpec((rows, width), lambda i, info: (span_at(info, 0), 0))
    n_t = lax.axis_size("t")
    shapes = [jax.ShapeDtypeStruct((2 * rows, width // n_t), jnp.bfloat16)] * n_t
    shapes.append(jax.ShapeDtypeStruct((2 * rows, width), jnp.bfloat16))
    *far, near = pl.pallas_call(
        hot_kernel,
        out_shape=shapes,
        grid_spec=pltpu.PrefetchScalarGridSpec(
            num_scalar_prefetch=1,
            grid=(1,),
            in_specs=[spec] * 4 + [whole(hot_w.shape)],
            out_specs=[whole(shape.shape) for shape in shapes],
            scratch_shapes=[pltpu.VMEM((2 * rows, width), jnp.bfloat16)],
        ),
        compiler_params=PARAMS,
        cost_estimate=cost(8 * rows * w_size, 2 * w_size + 16 * rows * width),
    )(info, *blocks, hot_w)
    return near, far


def pack(tokens, expert_ids, gate_values):
    tok_dev, width = tokens.shape
    meta = jnp.concatenate([expert_ids.astype(jnp.bfloat16), gate_values.astype(jnp.bfloat16)], axis=1)
    meta = meta.T.reshape(1, -1)
    meta = jnp.pad(meta, ((0, 7), (0, width - meta.shape[1])))
    return jnp.concatenate([tokens, meta], axis=0)


def route_kernel(info, a_ref, b_ref, send_ref, mix_ref, hot_mix_ref):
    zh, c = info[Z_HI], info[CORE]
    n_tok = mix_ref.shape[1]
    n_slot = send_ref.shape[0]
    tok_dev = n_tok // 2
    span_rows = tok_dev // SPANS

    def entry(k):
        at = slice(k * tok_dev, (k + 1) * tok_dev)
        row = jnp.concatenate(
            [a_ref[tok_dev : tok_dev + 8, at], b_ref[tok_dev : tok_dev + 8, at]], axis=1
        )
        return row.astype(jnp.float32)[:1]

    row = iota((1, n_tok), 1)
    group = row // span_rows
    span = group % SPANS
    hot = sum(jnp.where(span == s, info[s], 0) for s in range(SPANS)).astype(jnp.float32)

    slot = pl.program_id(0) * n_slot + iota((n_slot, 1), 0)
    dest, local = slot // 32, slot // 16 % 2
    expert = ((dest // 4 * 2 + zh) * 4 + dest % 4) * 4 + c * 2 + local
    expert = expert.astype(jnp.float32)
    gate = jnp.zeros((n_slot, n_tok), jnp.float32)
    hits = jnp.zeros((n_slot, n_tok), jnp.float32)
    hot_gate = jnp.zeros((1, n_tok), jnp.float32)
    for k in range(TOP_K):
        ids, gates = entry(k), entry(TOP_K + k)
        same = expert == ids
        gate = jnp.where(same, gates, gate)
        hits = jnp.where(same, 1.0, hits)
        hot_gate += jnp.where(ids == hot, gates, 0.0)
    named = jnp.where(expert == hot, 0.0, hits)
    before, after = iota((n_tok, n_tok), 0), iota((n_tok, n_tok), 1)
    earlier = (before // span_rows == after // span_rows) & (before < after)
    earlier = jnp.where(earlier, 1.0, 0.0).astype(jnp.bfloat16)
    rank = dot(named.astype(jnp.bfloat16), earlier, 1, 0)
    at = (slot // CAPACITY % (2 * SPANS)) == group
    chosen = (named > 0.5) & at & (rank == (slot % CAPACITY).astype(jnp.float32))
    pick = jnp.where(chosen, 1.0, 0.0).astype(jnp.bfloat16)
    sent = dot(pick[:, :tok_dev], a_ref[:tok_dev], 1, 0)
    sent += dot(pick[:, tok_dev:], b_ref[:tok_dev], 1, 0)
    send_ref[...] = sent.astype(jnp.bfloat16)
    mix_ref[...] = jnp.where(chosen, gate, 0.0).astype(jnp.bfloat16)
    hot_row = iota((2 * span_rows, 1), 0)
    hot_row = hot_row // span_rows * tok_dev + (2 * zh + c) * span_rows + hot_row % span_rows
    hot_mix_ref[...] = jnp.where(hot_row == row, hot_gate, 0.0).astype(jnp.bfloat16)


def route(info, a, b, tok_dev):
    width = a.shape[1]
    n_slot = 32 * 2 * SPANS * CAPACITY
    steps = 4
    span_rows = tok_dev // SPANS
    shapes = (
        jax.ShapeDtypeStruct((n_slot, width), jnp.bfloat16),
        jax.ShapeDtypeStruct((n_slot, 2 * tok_dev), jnp.bfloat16),
        jax.ShapeDtypeStruct((2 * span_rows, 2 * tok_dev), jnp.bfloat16),
    )
    return pl.pallas_call(
        route_kernel,
        out_shape=shapes,
        grid_spec=pltpu.PrefetchScalarGridSpec(
            num_scalar_prefetch=1,
            grid=(steps,),
            in_specs=[whole(a.shape), whole(b.shape)],
            out_specs=(
                pl.BlockSpec((n_slot // steps, width), lambda i, info: (i, 0)),
                pl.BlockSpec((n_slot // steps, 2 * tok_dev), lambda i, info: (i, 0)),
                whole(shapes[2].shape),
            ),
        ),
        compiler_params=PARAMS,
        cost_estimate=cost(4 * n_slot * tok_dev * width, 2 * width * (n_slot + 2 * tok_dev)),
    )(info, a, b)


def ffn_kernel(info, x_ref, gate_ref, up_ref, down_ref, *out_refs):
    n_src, rows, width = x_ref.shape
    x = x_ref[...].reshape(n_src * rows, width)
    gate = dot(x, gate_ref[0], 1, 1)
    up = dot(x, up_ref[0], 1, 1)
    hidden = (jax.nn.silu(gate) * up).astype(jnp.bfloat16)
    if len(out_refs) == 1:
        out = dot(hidden, down_ref[0], 1, 0).astype(jnp.bfloat16)
        out_refs[0][...] = out.reshape(n_src, rows, width)
        return
    cols = width // len(out_refs)
    for i, out_ref in enumerate(out_refs):
        start = pl.multiple_of((info[TENSOR] ^ i) * cols, cols)
        out = dot(hidden, down_ref[0, :, pl.ds(start, cols)], 1, 0).astype(jnp.bfloat16)
        out_ref[...] = out.reshape(n_src, rows, cols)


def ffn(info, x, w_gate, w_up, w_down, groups):
    n_src, rows, width = x.shape
    exp_dev, units, _ = w_gate.shape
    steps = 1

    def block(cols):
        return pl.BlockSpec((n_src // steps, rows // exp_dev, cols), lambda e, i, info: (i, e, 0))

    w_spec = pl.BlockSpec((1, units, width), lambda e, i, info: (e, 0, 0))
    cols = width // groups
    return pl.pallas_call(
        ffn_kernel,
        out_shape=[jax.ShapeDtypeStruct((n_src, rows, cols), jnp.bfloat16)] * groups,
        grid_spec=pltpu.PrefetchScalarGridSpec(
            num_scalar_prefetch=1,
            grid=(exp_dev, steps),
            in_specs=[block(width), w_spec, w_spec, w_spec],
            out_specs=[block(cols)] * groups,
        ),
        compiler_params=PARAMS,
        cost_estimate=cost(6 * n_src * rows * units * width, 4 * x.size + 6 * w_gate.size),
    )(info, x, w_gate, w_up, w_down)


def mix_kernel(info, mix_ref, hot_mix_ref, ret_ref, hot_ref, own_ref, other_ref):
    out = dot(mix_ref[...], ret_ref[...], 0, 0) + dot(hot_mix_ref[...], hot_ref[...], 0, 0)
    out = out.astype(jnp.bfloat16)
    half = out.shape[0] // 2
    own_ref[0] = out[:half]
    other_ref[0] = out[half:]


def mix_rows(info, mix, hot_mix, returned, hot):
    n_slot, n_tok = mix.shape
    width = returned.shape[1]
    n_group = lax.axis_size("t")
    cols = width // n_group
    shape = jax.ShapeDtypeStruct((n_group, n_tok // 2, cols), jnp.bfloat16)
    out = pl.BlockSpec((1, n_tok // 2, cols), lambda i, info: (i, 0, 0))
    return pl.pallas_call(
        mix_kernel,
        out_shape=(shape, shape),
        grid_spec=pltpu.PrefetchScalarGridSpec(
            num_scalar_prefetch=1,
            grid=(n_group,),
            in_specs=[
                whole(mix.shape),
                whole(hot_mix.shape),
                pl.BlockSpec((n_slot, cols), lambda i, info: (0, i ^ info[TENSOR])),
                pl.BlockSpec((hot.shape[0], cols), lambda i, info: (0, i ^ info[TENSOR])),
            ],
            out_specs=(out, out),
        ),
        compiler_params=PARAMS,
        cost_estimate=cost(2 * n_slot * n_tok * width, 2 * width * (n_slot + n_tok)),
    )(info, mix, hot_mix, returned, hot)


def mix_quarter_kernel(mix_ref, hot_mix_ref, ret_ref, hot_ref, own_ref, other_ref):
    out = dot(mix_ref[...], ret_ref[...], 0, 0) + dot(hot_mix_ref[...], hot_ref[...], 0, 0)
    half = out.shape[0] // 2
    own_ref[...] = out[:half]
    other_ref[...] = out[half:].astype(jnp.bfloat16)


def mix_quarter(mix, hot_mix, returned, hot):
    rows, cols = mix.shape[1] // 2, returned.shape[1]
    return pl.pallas_call(
        mix_quarter_kernel,
        out_shape=(
            jax.ShapeDtypeStruct((rows, cols), jnp.float32),
            jax.ShapeDtypeStruct((rows, cols), jnp.bfloat16),
        ),
        compiler_params=PARAMS,
        cost_estimate=cost(2 * mix.size * cols, 2 * (mix.size + returned.size)),
    )(mix, hot_mix, returned, hot)


def exchange(send):
    return lax.all_to_all(send, ("y", "x"), 0, 0, tiled=True)


def to_t(groups, *shifts):
    pairs = range(len(groups))
    return tuple(lax.ppermute(groups[k], "t", [(i, i ^ k) for i in pairs]) for k in shifts)


def total_of(parts):
    return sum(part.astype(jnp.float32) for part in parts).astype(jnp.bfloat16)


def per_device(tokens, expert_ids, gate_values, hot_ids, w_gate, w_up, w_down):
    y, zh, x, c, t = (lax.axis_index(name) for name in ("y", "zh", "x", "c", "t"))
    n_t = lax.axis_size("t")
    tok_dev, width = tokens.shape
    place = jnp.stack([(y * 2 + zh) * 4 + x, zh, c, t, 0]).astype(jnp.int32)
    info = jnp.concatenate([hot_ids, place])
    experts = (w_gate, w_up, w_down)

    own = pack(tokens, expert_ids, gate_values)
    own_z = lax.ppermute(own, "zh", SWAP)
    own_c = lax.ppermute(own, "c", SWAP)
    near, near_mix, near_hot_mix = route(info, own, own_c, tok_dev)
    n_slot = near.shape[0]
    slots = (16, n_slot // 16, width)

    chunks = first_chunks(info, hot_ids, experts)
    near, chunks, own_z = lax.optimization_barrier((near.reshape(slots), chunks, own_z))
    near = exchange(near)
    own_zc = lax.ppermute(own_z, "c", SWAP)
    far, far_mix, far_hot_mix = route(info, own_z, own_zc, tok_dev)
    hot_w = own_span(info, chunks, c)
    far, hot_w = lax.optimization_barrier((far.reshape(slots), hot_w))
    hot_w = lax.all_gather(hot_w, ("y", "x"), axis=0, tiled=False)
    far = exchange(far)
    (near,) = ffn(info, near, *experts, 1)
    near = exchange(near)
    far = ffn(info, far, *experts, n_t)
    far = total_of((far[0], *to_t(far, 1, 2, 3)))
    near_hot, far_hot = hot_ffn(info, (own_z, own_zc, own, own_c), hot_w, tok_dev // SPANS)
    far_hot = total_of((far_hot[0], *to_t(far_hot, 1, 2, 3)))
    near, far = lax.optimization_barrier((near, far))

    far = exchange(far).reshape(n_slot, width // n_t)
    mine, other = mix_rows(info, near_mix, near_hot_mix, near.reshape(n_slot, width), near_hot)
    got = lax.ppermute(other, "c", SWAP)
    pieces = [mine[k].astype(jnp.float32) + got[k].astype(jnp.float32) for k in range(n_t)]
    total = pieces[0]
    for part in to_t([piece.astype(jnp.bfloat16) for piece in pieces], 1, 2, 3):
        total += part.astype(jnp.float32)
    far, total = lax.optimization_barrier((far, total))
    mine, other = mix_quarter(far_mix, far_hot_mix, far, far_hot)
    mine += lax.ppermute(other, "c", SWAP).astype(jnp.float32)
    got = lax.ppermute(mine.astype(jnp.bfloat16), "zh", SWAP)
    return (total + got.astype(jnp.float32)).astype(jnp.bfloat16)


def solution(mesh):
    fine = Mesh(mesh.devices.reshape(4, 2, 4, 2, 4), ("y", "zh", "x", "c", "t"))
    owner = ("y", "zh", "x", "c")
    in_specs = (
        P(owner, None),
        P(owner, None),
        P(owner, None),
        P(),
        P(owner, "t", None),
        P(owner, "t", None),
        P(owner, "t", None),
    )
    return jax.shard_map(
        per_device, mesh=fine, in_specs=in_specs, out_specs=P(owner, "t"), check_vma=False
    )
```

```python
import jax
import jax.numpy as jnp
from jax import lax
from jax.experimental import pallas as pl
from jax.experimental.pallas import tpu as pltpu
from jax.sharding import Mesh, PartitionSpec as P

SPANS = 4
CAPACITY = 2
TOP_K = 8
SWAP = ((0, 1), (1, 0))
VMEM_LIMIT = 32 * 1024 * 1024


def dot(a, b, contract_a, contract_b):
    dims = (((contract_a,), (contract_b,)), ((), ()))
    return lax.dot_general(a, b, dims, preferred_element_type=jnp.float32)


def iota(shape, dim):
    return lax.broadcasted_iota(jnp.int32, shape, dim)


def cost(flops, moved):
    return pl.CostEstimate(flops=flops, bytes_accessed=moved, transcendentals=0)


PARAMS = pltpu.CompilerParams(vmem_limit_bytes=VMEM_LIMIT)


def whole(shape):
    return pl.BlockSpec(shape, lambda *_: (0,) * len(shape))


CHIP, Z_HI, CORE, TENSOR, TURN = 4, 5, 6, 7, 8


def chip_of(expert):
    return expert >> 2


def order_of(info, span):
    chip = chip_of(info[span])
    return sum(((chip_of(info[s]) == chip) & (s < span)).astype(jnp.int32) for s in range(SPANS))


def my_turn(info):
    return sum(
        jnp.where((chip_of(info[s]) == info[CHIP]) & (order_of(info, s) == info[TURN]), info[s], 0)
        for s in range(SPANS)
    )


def chunk_kernel(info, gate_ref, up_ref, down_ref, keep_ref, give_ref):
    units = gate_ref.shape[1]
    mid = units // 2
    n_chunk, _, lane = keep_ref.shape

    def first(out):
        for n in range(n_chunk):
            at = slice(n * lane, (n + 1) * lane)
            out[n, :units] = gate_ref[0, :, at]
            out[n, units:] = up_ref[0, :mid, at]

    def second(out):
        for n in range(n_chunk):
            at = slice(n * lane, (n + 1) * lane)
            out[n, :mid] = up_ref[0, mid:, at]
            out[n, mid:] = down_ref[0, :, at]

    @pl.when(info[CORE] == 0)
    def _():
        first(keep_ref)
        second(give_ref)

    @pl.when(info[CORE] == 1)
    def _():
        second(keep_ref)
        first(give_ref)


def cut_chunks(info, held):
    _, units, width = held[0].shape
    steps = 4
    half, lane = 3 * units // 2, width // 16
    spec = pl.BlockSpec((1, units, width // steps), lambda n, info: (my_turn(info) & 1, 0, n))
    out = pl.BlockSpec((16 // steps, half, lane), lambda n, info: (n, 0, 0))
    shape = jax.ShapeDtypeStruct((16, half, lane), jnp.bfloat16)
    return pl.pallas_call(
        chunk_kernel,
        out_shape=(shape, shape),
        grid_spec=pltpu.PrefetchScalarGridSpec(
            num_scalar_prefetch=1, grid=(steps,), in_specs=[spec] * 3, out_specs=(out, out)
        ),
        compiler_params=PARAMS,
        cost_estimate=cost(0, 4 * 3 * units * width),
    )(info, *held)


def choose_kernel(info, keep_ref, got_ref, out_ref):
    held_here = ((my_turn(info) >> 1) & 1) == info[CORE]

    @pl.when(held_here)
    def _():
        out_ref[...] = keep_ref[...]

    @pl.when(jnp.logical_not(held_here))
    def _():
        out_ref[...] = got_ref[...]


def choose(info, keep, got):
    return pl.pallas_call(
        choose_kernel,
        out_shape=jax.ShapeDtypeStruct(keep.shape, keep.dtype),
        grid_spec=pltpu.PrefetchScalarGridSpec(
            num_scalar_prefetch=1,
            grid=(1,),
            in_specs=[whole(keep.shape)] * 2,
            out_specs=whole(keep.shape),
        ),
        compiler_params=PARAMS,
        cost_estimate=cost(0, 6 * keep.size),
    )(info, keep, got)


def span_at(info, i):
    return (2 * info[Z_HI] + info[CORE]) ^ i


def take_kernel(info, part_ref, *refs):
    *old_refs, out_ref = refs
    span = span_at(info, pl.program_id(0))
    expert = info[span]
    here = (((expert >> 4) & 1) == info[Z_HI]) & (order_of(info, span) == info[TURN])
    if old_refs:
        out_ref[...] = jnp.where(here, part_ref[...], old_refs[0][...])
    else:
        out_ref[...] = part_ref[...]


def take(info, part, *old):
    block = (1, *part.shape[1:])

    def source(i, info):
        expert = info[span_at(info, i)]
        return ((expert >> 5) * 4 + ((expert >> 2) & 3), 0, 0)

    def same(i, info):
        return (i, 0, 0)

    return pl.pallas_call(
        take_kernel,
        out_shape=jax.ShapeDtypeStruct((SPANS, *part.shape[1:]), part.dtype),
        grid_spec=pltpu.PrefetchScalarGridSpec(
            num_scalar_prefetch=1,
            grid=(SPANS,),
            in_specs=[pl.BlockSpec(block, source)] + [pl.BlockSpec(block, same)] * len(old),
            out_specs=pl.BlockSpec(block, same),
        ),
        compiler_params=PARAMS,
        cost_estimate=cost(0, 16 * block[1] * block[2]),
    )(info, part, *old)


def hot_round(info, held, *old):
    keep, give = cut_chunks(info, held)
    part = choose(info, keep, lax.ppermute(give, "c", SWAP))
    part = lax.all_to_all(part, ("y", "x"), 0, 0, tiled=True)
    return take(info, part, *old)


def pair_kernel(info, chunk_ref, got_ref, mine_ref, give_ref):
    for i, out_ref in enumerate((mine_ref, give_ref)):
        here = ((info[span_at(info, i)] >> 4) & 1) == info[Z_HI]
        out_ref[...] = jnp.where(here, chunk_ref[i], got_ref[i])


def pair(info, chunks, got):
    shape = jax.ShapeDtypeStruct(chunks.shape[1:], chunks.dtype)
    return pl.pallas_call(
        pair_kernel,
        out_shape=(shape, shape),
        grid_spec=pltpu.PrefetchScalarGridSpec(
            num_scalar_prefetch=1,
            grid=(1,),
            in_specs=[whole(got.shape)] * 2,
            out_specs=(whole(shape.shape), whole(shape.shape)),
        ),
        compiler_params=PARAMS,
        cost_estimate=cost(0, 12 * shape.size),
    )(info, chunks, got)


def first_chunks(info, hot_ids, held):
    chips = chip_of(hot_ids)
    before = jnp.arange(SPANS)[None, :] < jnp.arange(SPANS)[:, None]
    turns = 1 + jnp.max(jnp.sum((chips[:, None] == chips[None, :]) & before, axis=1))
    chunks = hot_round(info, held)
    return lax.fori_loop(
        1, turns, lambda turn, old: hot_round(info.at[TURN].set(turn), held, old), chunks
    )


def own_span(info, chunks, c):
    got = lax.ppermute(chunks[2:], "zh", SWAP)
    mine, give = pair(info, chunks, got)
    got = lax.ppermute(give, "c", SWAP)
    first, second = jnp.where(c == 0, mine, got), jnp.where(c == 0, got, mine)
    return jnp.concatenate([first, second], axis=0)


def along_y(chunk):
    n_y = lax.axis_size("y")
    column = [chunk]
    for k in range(1, n_y):
        column.append(lax.ppermute(chunk, "y", [(i, i ^ k) for i in range(n_y)]))
    return jnp.stack(column)


def shift_x(array, step):
    n_x = lax.axis_size("x")
    return lax.ppermute(array, "x", [(i, (i + step) % n_x) for i in range(n_x)])


def hot_kernel(info, *refs):
    *refs, near_ref, far_rows = refs
    tok_refs, w_refs, far_refs = refs[:4], refs[4:9], refs[9:]
    n_y, rows, lane = w_refs[0].shape
    units = rows // 3
    half = near_ref.shape[0]
    cols = far_refs[0].shape[1]
    pieces = [(0, i, w_refs[0], i) for i in range(n_y)]
    pieces += [(3, i, w_refs[1], i) for i in range(n_y)]
    pieces += [(1, i, w_refs[2], i) for i in range(n_y)]
    pieces += [(2, i, w_refs[3 + i // 2], i % 2) for i in range(n_y)]

    def columns(far, i):
        start = ((info[CHIP] >> 3 ^ i) * 4 + ((info[CHIP] + far) & 3)) * lane
        return pl.ds(pl.multiple_of(start, lane), lane)

    proj = jnp.zeros((2 * half, 2 * units), jnp.float32)
    for far, i, w_ref, at in pieces:
        tok = jnp.concatenate([r[:, columns(far, i)] for r in tok_refs], axis=0)
        proj += dot(tok, w_ref[at, : 2 * units], 1, 1)
    hidden = (jax.nn.silu(proj[:, :units]) * proj[:, units:]).astype(jnp.bfloat16)
    for far, i, w_ref, at in pieces:
        out = dot(hidden, w_ref[at, 2 * units :], 1, 0).astype(jnp.bfloat16)
        far_rows[:, columns(far, i)] = out[:half]
        near_ref[:, columns(far, i)] = out[half:]
    for i, far_ref in enumerate(far_refs):
        start = pl.multiple_of((info[TENSOR] ^ i) * cols, cols)
        far_ref[...] = far_rows[:, pl.ds(start, cols)]


def hot_ffn(info, blocks, hot_w, rows):
    width = blocks[0].shape[1]
    w_size = sum(w.size for w in hot_w)
    spec = pl.BlockSpec((rows, width), lambda i, info: (span_at(info, 0), 0))
    n_t = lax.axis_size("t")
    shapes = [jax.ShapeDtypeStruct((2 * rows, width // n_t), jnp.bfloat16)] * n_t
    shapes.append(jax.ShapeDtypeStruct((2 * rows, width), jnp.bfloat16))
    *far, near = pl.pallas_call(
        hot_kernel,
        out_shape=shapes,
        grid_spec=pltpu.PrefetchScalarGridSpec(
            num_scalar_prefetch=1,
            grid=(1,),
            in_specs=[spec] * 4 + [whole(w.shape) for w in hot_w],
            out_specs=[whole(shape.shape) for shape in shapes],
            scratch_shapes=[pltpu.VMEM((2 * rows, width), jnp.bfloat16)],
        ),
        compiler_params=PARAMS,
        cost_estimate=cost(8 * rows * w_size, 2 * w_size + 16 * rows * width),
    )(info, *blocks, *hot_w)
    return near, far


def pack(tokens, expert_ids, gate_values):
    tok_dev, width = tokens.shape
    meta = jnp.concatenate([expert_ids.astype(jnp.bfloat16), gate_values.astype(jnp.bfloat16)], axis=1)
    meta = meta.T.reshape(1, -1)
    meta = jnp.pad(meta, ((0, 7), (0, width - meta.shape[1])))
    return jnp.concatenate([tokens, meta], axis=0)


def route_kernel(info, a_ref, b_ref, send_ref, mix_ref, hot_mix_ref):
    zh, c = info[Z_HI], info[CORE]
    n_tok = mix_ref.shape[1]
    n_slot = send_ref.shape[0]
    tok_dev = n_tok // 2
    span_rows = tok_dev // SPANS

    def entry(k):
        at = slice(k * tok_dev, (k + 1) * tok_dev)
        row = jnp.concatenate(
            [a_ref[tok_dev : tok_dev + 8, at], b_ref[tok_dev : tok_dev + 8, at]], axis=1
        )
        return row.astype(jnp.float32)[:1]

    row = iota((1, n_tok), 1)
    group = row // span_rows
    span = group % SPANS
    hot = sum(jnp.where(span == s, info[s], 0) for s in range(SPANS)).astype(jnp.float32)

    slot = pl.program_id(0) * n_slot + iota((n_slot, 1), 0)
    dest, local = slot // 32, slot // 16 % 2
    expert = ((dest // 4 * 2 + zh) * 4 + dest % 4) * 4 + c * 2 + local
    expert = expert.astype(jnp.float32)
    gate = jnp.zeros((n_slot, n_tok), jnp.float32)
    hits = jnp.zeros((n_slot, n_tok), jnp.float32)
    hot_gate = jnp.zeros((1, n_tok), jnp.float32)
    for k in range(TOP_K):
        ids, gates = entry(k), entry(TOP_K + k)
        same = expert == ids
        gate = jnp.where(same, gates, gate)
        hits = jnp.where(same, 1.0, hits)
        hot_gate += jnp.where(ids == hot, gates, 0.0)
    named = jnp.where(expert == hot, 0.0, hits)
    before, after = iota((n_tok, n_tok), 0), iota((n_tok, n_tok), 1)
    earlier = (before // span_rows == after // span_rows) & (before < after)
    earlier = jnp.where(earlier, 1.0, 0.0).astype(jnp.bfloat16)
    rank = dot(named.astype(jnp.bfloat16), earlier, 1, 0)
    at = (slot // CAPACITY % (2 * SPANS)) == group
    chosen = (named > 0.5) & at & (rank == (slot % CAPACITY).astype(jnp.float32))
    pick = jnp.where(chosen, 1.0, 0.0).astype(jnp.bfloat16)
    sent = dot(pick[:, :tok_dev], a_ref[:tok_dev], 1, 0)
    sent += dot(pick[:, tok_dev:], b_ref[:tok_dev], 1, 0)
    send_ref[...] = sent.astype(jnp.bfloat16)
    mix_ref[...] = jnp.where(chosen, gate, 0.0).astype(jnp.bfloat16)
    hot_row = iota((2 * span_rows, 1), 0)
    hot_row = hot_row // span_rows * tok_dev + (2 * zh + c) * span_rows + hot_row % span_rows
    hot_mix_ref[...] = jnp.where(hot_row == row, hot_gate, 0.0).astype(jnp.bfloat16)


def route(info, a, b, tok_dev):
    width = a.shape[1]
    n_slot = 32 * 2 * SPANS * CAPACITY
    steps = 4
    span_rows = tok_dev // SPANS
    shapes = (
        jax.ShapeDtypeStruct((n_slot, width), jnp.bfloat16),
        jax.ShapeDtypeStruct((n_slot, 2 * tok_dev), jnp.bfloat16),
        jax.ShapeDtypeStruct((2 * span_rows, 2 * tok_dev), jnp.bfloat16),
    )
    return pl.pallas_call(
        route_kernel,
        out_shape=shapes,
        grid_spec=pltpu.PrefetchScalarGridSpec(
            num_scalar_prefetch=1,
            grid=(steps,),
            in_specs=[whole(a.shape), whole(b.shape)],
            out_specs=(
                pl.BlockSpec((n_slot // steps, width), lambda i, info: (i, 0)),
                pl.BlockSpec((n_slot // steps, 2 * tok_dev), lambda i, info: (i, 0)),
                whole(shapes[2].shape),
            ),
        ),
        compiler_params=PARAMS,
        cost_estimate=cost(4 * n_slot * tok_dev * width, 2 * width * (n_slot + 2 * tok_dev)),
    )(info, a, b)


def ffn_kernel(info, x_ref, gate_ref, up_ref, down_ref, *out_refs):
    n_src, rows, width = x_ref.shape
    x = x_ref[...].reshape(n_src * rows, width)
    gate = dot(x, gate_ref[0], 1, 1)
    up = dot(x, up_ref[0], 1, 1)
    hidden = (jax.nn.silu(gate) * up).astype(jnp.bfloat16)
    if len(out_refs) == 1:
        out = dot(hidden, down_ref[0], 1, 0).astype(jnp.bfloat16)
        out_refs[0][...] = out.reshape(n_src, rows, width)
        return
    cols = width // len(out_refs)
    for i, out_ref in enumerate(out_refs):
        start = pl.multiple_of((info[TENSOR] ^ i) * cols, cols)
        out = dot(hidden, down_ref[0, :, pl.ds(start, cols)], 1, 0).astype(jnp.bfloat16)
        out_ref[...] = out.reshape(n_src, rows, cols)


def ffn(info, x, w_gate, w_up, w_down, groups):
    n_src, rows, width = x.shape
    exp_dev, units, _ = w_gate.shape
    steps = 1

    def block(cols):
        return pl.BlockSpec((n_src // steps, rows // exp_dev, cols), lambda e, i, info: (i, e, 0))

    w_spec = pl.BlockSpec((1, units, width), lambda e, i, info: (e, 0, 0))
    cols = width // groups
    return pl.pallas_call(
        ffn_kernel,
        out_shape=[jax.ShapeDtypeStruct((n_src, rows, cols), jnp.bfloat16)] * groups,
        grid_spec=pltpu.PrefetchScalarGridSpec(
            num_scalar_prefetch=1,
            grid=(exp_dev, steps),
            in_specs=[block(width), w_spec, w_spec, w_spec],
            out_specs=[block(cols)] * groups,
        ),
        compiler_params=PARAMS,
        cost_estimate=cost(6 * n_src * rows * units * width, 4 * x.size + 6 * w_gate.size),
    )(info, x, w_gate, w_up, w_down)


def mix_kernel(info, mix_ref, hot_mix_ref, ret_ref, hot_ref, own_ref, other_ref):
    out = dot(mix_ref[...], ret_ref[...], 0, 0) + dot(hot_mix_ref[...], hot_ref[...], 0, 0)
    out = out.astype(jnp.bfloat16)
    half = out.shape[0] // 2
    own_ref[0] = out[:half]
    other_ref[0] = out[half:]


def mix_rows(info, mix, hot_mix, returned, hot):
    n_slot, n_tok = mix.shape
    width = returned.shape[1]
    n_group = lax.axis_size("t")
    cols = width // n_group
    shape = jax.ShapeDtypeStruct((n_group, n_tok // 2, cols), jnp.bfloat16)
    out = pl.BlockSpec((1, n_tok // 2, cols), lambda i, info: (i, 0, 0))
    return pl.pallas_call(
        mix_kernel,
        out_shape=(shape, shape),
        grid_spec=pltpu.PrefetchScalarGridSpec(
            num_scalar_prefetch=1,
            grid=(n_group,),
            in_specs=[
                whole(mix.shape),
                whole(hot_mix.shape),
                pl.BlockSpec((n_slot, cols), lambda i, info: (0, i ^ info[TENSOR])),
                pl.BlockSpec((hot.shape[0], cols), lambda i, info: (0, i ^ info[TENSOR])),
            ],
            out_specs=(out, out),
        ),
        compiler_params=PARAMS,
        cost_estimate=cost(2 * n_slot * n_tok * width, 2 * width * (n_slot + n_tok)),
    )(info, mix, hot_mix, returned, hot)


def mix_quarter_kernel(mix_ref, hot_mix_ref, ret_ref, hot_ref, own_ref, other_ref):
    out = dot(mix_ref[...], ret_ref[...], 0, 0) + dot(hot_mix_ref[...], hot_ref[...], 0, 0)
    half = out.shape[0] // 2
    own_ref[...] = out[:half]
    other_ref[...] = out[half:].astype(jnp.bfloat16)


def mix_quarter(mix, hot_mix, returned, hot):
    rows, cols = mix.shape[1] // 2, returned.shape[1]
    return pl.pallas_call(
        mix_quarter_kernel,
        out_shape=(
            jax.ShapeDtypeStruct((rows, cols), jnp.float32),
            jax.ShapeDtypeStruct((rows, cols), jnp.bfloat16),
        ),
        compiler_params=PARAMS,
        cost_estimate=cost(2 * mix.size * cols, 2 * (mix.size + returned.size)),
    )(mix, hot_mix, returned, hot)


def exchange(send):
    return lax.all_to_all(send, ("y", "x"), 0, 0, tiled=True)


def to_t(groups, *shifts):
    pairs = range(len(groups))
    return tuple(lax.ppermute(groups[k], "t", [(i, i ^ k) for i in pairs]) for k in shifts)


def total_of(parts):
    return sum(part.astype(jnp.float32) for part in parts).astype(jnp.bfloat16)


def per_device(tokens, expert_ids, gate_values, hot_ids, w_gate, w_up, w_down):
    y, zh, x, c, t = (lax.axis_index(name) for name in ("y", "zh", "x", "c", "t"))
    n_t = lax.axis_size("t")
    tok_dev, width = tokens.shape
    place = jnp.stack([(y * 2 + zh) * 4 + x, zh, c, t, 0]).astype(jnp.int32)
    info = jnp.concatenate([hot_ids, place])
    experts = (w_gate, w_up, w_down)

    own = pack(tokens, expert_ids, gate_values)
    own_z = lax.ppermute(own, "zh", SWAP)
    own_c = lax.ppermute(own, "c", SWAP)
    near, near_mix, near_hot_mix = route(info, own, own_c, tok_dev)
    n_slot = near.shape[0]
    slots = (16, n_slot // 16, width)

    chunks = first_chunks(info, hot_ids, experts)
    near, chunks, own_z = lax.optimization_barrier((near.reshape(slots), chunks, own_z))
    near = exchange(near)
    own_zc = lax.ppermute(own_z, "c", SWAP)
    far, far_mix, far_hot_mix = route(info, own_z, own_zc, tok_dev)
    hot_w = along_y(own_span(info, chunks, c))
    far, hot_w = lax.optimization_barrier((far.reshape(slots), hot_w))
    far = exchange(far)
    hot_w = (hot_w, shift_x(hot_w, 1), shift_x(hot_w, -1))
    (near,) = ffn(info, near, *experts, 1)
    near, hot_w = lax.optimization_barrier((near, hot_w))
    near = exchange(near)
    far = ffn(info, far, *experts, n_t)
    far, hot_w = lax.optimization_barrier((tuple(far), hot_w))
    half = hot_w[0].shape[0] // 2
    hot_w += (shift_x(hot_w[1][:half], 1), shift_x(hot_w[2][half:], -1))
    far = total_of((far[0], *to_t(far, 1, 2, 3)))
    near_hot, far_hot = hot_ffn(info, (own_z, own_zc, own, own_c), hot_w, tok_dev // SPANS)
    mine, other = mix_rows(info, near_mix, near_hot_mix, near.reshape(n_slot, width), near_hot)
    got = lax.ppermute(other, "c", SWAP)
    mine, got, far, far_hot = lax.optimization_barrier((mine, got, far, far_hot))

    far_hot = total_of((far_hot[0], *to_t(far_hot, 1, 2, 3)))
    far = exchange(far).reshape(n_slot, width // n_t)
    pieces = [mine[k].astype(jnp.float32) + got[k].astype(jnp.float32) for k in range(n_t)]
    total = pieces[0]
    for part in to_t([piece.astype(jnp.bfloat16) for piece in pieces], 1, 2, 3):
        total += part.astype(jnp.float32)
    far, total = lax.optimization_barrier((far, total))
    mine, other = mix_quarter(far_mix, far_hot_mix, far, far_hot)
    mine += lax.ppermute(other, "c", SWAP).astype(jnp.float32)
    got = lax.ppermute(mine.astype(jnp.bfloat16), "zh", SWAP)
    return (total + got.astype(jnp.float32)).astype(jnp.bfloat16)


def solution(mesh):
    fine = Mesh(mesh.devices.reshape(4, 2, 4, 2, 4), ("y", "zh", "x", "c", "t"))
    owner = ("y", "zh", "x", "c")
    in_specs = (
        P(owner, None),
        P(owner, None),
        P(owner, None),
        P(),
        P(owner, "t", None),
        P(owner, "t", None),
        P(owner, "t", None),
    )
    return jax.shard_map(
        per_device, mesh=fine, in_specs=in_specs, out_specs=P(owner, "t"), check_vma=False
    )
```

```python
import jax
import jax.numpy as jnp
from jax import lax
from jax.experimental import pallas as pl
from jax.experimental.pallas import tpu as pltpu
from jax.sharding import Mesh, PartitionSpec as P

SPANS = 4
CAPACITY = 2
TOP_K = 8
SWAP = ((0, 1), (1, 0))
VMEM_LIMIT = 32 * 1024 * 1024


def dot(a, b, contract_a, contract_b):
    dims = (((contract_a,), (contract_b,)), ((), ()))
    return lax.dot_general(a, b, dims, preferred_element_type=jnp.float32)


def iota(shape, dim):
    return lax.broadcasted_iota(jnp.int32, shape, dim)


def cost(flops, moved):
    return pl.CostEstimate(flops=flops, bytes_accessed=moved, transcendentals=0)


PARAMS = pltpu.CompilerParams(vmem_limit_bytes=VMEM_LIMIT)


def whole(shape):
    return pl.BlockSpec(shape, lambda *_: (0,) * len(shape))


CHIP, Z_HI, CORE, TENSOR, TURN = 4, 5, 6, 7, 8


def chip_of(expert):
    return expert >> 2


def order_of(info, span):
    chip = chip_of(info[span])
    return sum(((chip_of(info[s]) == chip) & (s < span)).astype(jnp.int32) for s in range(SPANS))


def my_turn(info):
    return sum(
        jnp.where((chip_of(info[s]) == info[CHIP]) & (order_of(info, s) == info[TURN]), info[s], 0)
        for s in range(SPANS)
    )


def chunk_kernel(info, gate_ref, up_ref, down_ref, keep_ref, give_ref):
    units = gate_ref.shape[1]
    mid = units // 2
    n_chunk, _, lane = keep_ref.shape

    def first(out):
        for n in range(n_chunk):
            at = slice(n * lane, (n + 1) * lane)
            out[n, :units] = gate_ref[0, :, at]
            out[n, units:] = up_ref[0, :mid, at]

    def second(out):
        for n in range(n_chunk):
            at = slice(n * lane, (n + 1) * lane)
            out[n, :mid] = up_ref[0, mid:, at]
            out[n, mid:] = down_ref[0, :, at]

    @pl.when(info[CORE] == 0)
    def _():
        first(keep_ref)
        second(give_ref)

    @pl.when(info[CORE] == 1)
    def _():
        second(keep_ref)
        first(give_ref)


def cut_chunks(info, held):
    _, units, width = held[0].shape
    steps = 4
    half, lane = 3 * units // 2, width // 16
    spec = pl.BlockSpec((1, units, width // steps), lambda n, info: (my_turn(info) & 1, 0, n))
    out = pl.BlockSpec((16 // steps, half, lane), lambda n, info: (n, 0, 0))
    shape = jax.ShapeDtypeStruct((16, half, lane), jnp.bfloat16)
    return pl.pallas_call(
        chunk_kernel,
        out_shape=(shape, shape),
        grid_spec=pltpu.PrefetchScalarGridSpec(
            num_scalar_prefetch=1, grid=(steps,), in_specs=[spec] * 3, out_specs=(out, out)
        ),
        compiler_params=PARAMS,
        cost_estimate=cost(0, 4 * 3 * units * width),
    )(info, *held)


def choose_kernel(info, keep_ref, got_ref, out_ref):
    held_here = ((my_turn(info) >> 1) & 1) == info[CORE]

    @pl.when(held_here)
    def _():
        out_ref[...] = keep_ref[...]

    @pl.when(jnp.logical_not(held_here))
    def _():
        out_ref[...] = got_ref[...]


def choose(info, keep, got):
    return pl.pallas_call(
        choose_kernel,
        out_shape=jax.ShapeDtypeStruct(keep.shape, keep.dtype),
        grid_spec=pltpu.PrefetchScalarGridSpec(
            num_scalar_prefetch=1,
            grid=(1,),
            in_specs=[whole(keep.shape)] * 2,
            out_specs=whole(keep.shape),
        ),
        compiler_params=PARAMS,
        cost_estimate=cost(0, 6 * keep.size),
    )(info, keep, got)


def span_at(info, i):
    return (2 * info[Z_HI] + info[CORE]) ^ i


def take_kernel(info, part_ref, *refs):
    *old_refs, out_ref = refs
    span = span_at(info, pl.program_id(0))
    expert = info[span]
    here = (((expert >> 4) & 1) == info[Z_HI]) & (order_of(info, span) == info[TURN])
    if old_refs:
        out_ref[...] = jnp.where(here, part_ref[...], old_refs[0][...])
    else:
        out_ref[...] = part_ref[...]


def take(info, part, *old):
    block = (1, *part.shape[1:])

    def source(i, info):
        expert = info[span_at(info, i)]
        return ((expert >> 5) * 4 + ((expert >> 2) & 3), 0, 0)

    def same(i, info):
        return (i, 0, 0)

    return pl.pallas_call(
        take_kernel,
        out_shape=jax.ShapeDtypeStruct((SPANS, *part.shape[1:]), part.dtype),
        grid_spec=pltpu.PrefetchScalarGridSpec(
            num_scalar_prefetch=1,
            grid=(SPANS,),
            in_specs=[pl.BlockSpec(block, source)] + [pl.BlockSpec(block, same)] * len(old),
            out_specs=pl.BlockSpec(block, same),
        ),
        compiler_params=PARAMS,
        cost_estimate=cost(0, 16 * block[1] * block[2]),
    )(info, part, *old)


def hot_round(info, held, *old):
    keep, give = cut_chunks(info, held)
    part = choose(info, keep, lax.ppermute(give, "c", SWAP))
    part = lax.all_to_all(part, ("y", "x"), 0, 0, tiled=True)
    return take(info, part, *old)


def pair_kernel(info, chunk_ref, got_ref, mine_ref, give_ref):
    for i, out_ref in enumerate((mine_ref, give_ref)):
        here = ((info[span_at(info, i)] >> 4) & 1) == info[Z_HI]
        out_ref[...] = jnp.where(here, chunk_ref[i], got_ref[i])


def pair(info, chunks, got):
    shape = jax.ShapeDtypeStruct(chunks.shape[1:], chunks.dtype)
    return pl.pallas_call(
        pair_kernel,
        out_shape=(shape, shape),
        grid_spec=pltpu.PrefetchScalarGridSpec(
            num_scalar_prefetch=1,
            grid=(1,),
            in_specs=[whole(got.shape)] * 2,
            out_specs=(whole(shape.shape), whole(shape.shape)),
        ),
        compiler_params=PARAMS,
        cost_estimate=cost(0, 12 * shape.size),
    )(info, chunks, got)


def first_chunks(info, hot_ids, held):
    chips = chip_of(hot_ids)
    before = jnp.arange(SPANS)[None, :] < jnp.arange(SPANS)[:, None]
    turns = 1 + jnp.max(jnp.sum((chips[:, None] == chips[None, :]) & before, axis=1))
    chunks = hot_round(info, held)
    return lax.fori_loop(
        1, turns, lambda turn, old: hot_round(info.at[TURN].set(turn), held, old), chunks
    )


def own_span(info, chunks, c):
    got = lax.ppermute(chunks[2:], "zh", SWAP)
    mine, give = pair(info, chunks, got)
    got = lax.ppermute(give, "c", SWAP)
    first, second = jnp.where(c == 0, mine, got), jnp.where(c == 0, got, mine)
    return jnp.concatenate([first, second], axis=0)


def along_y(chunk):
    n_y = lax.axis_size("y")
    column = [chunk]
    for k in range(1, n_y):
        column.append(lax.ppermute(chunk, "y", [(i, i ^ k) for i in range(n_y)]))
    return jnp.stack(column)


def shift_x(array, step):
    n_x = lax.axis_size("x")
    return lax.ppermute(array, "x", [(i, (i + step) % n_x) for i in range(n_x)])


def hot_kernel(info, *refs):
    *refs, near_ref, far_rows = refs
    tok_refs, w_refs, far_refs = refs[:4], refs[4:9], refs[9:]
    n_y, rows, lane = w_refs[0].shape
    units = rows // 3
    half = near_ref.shape[0]
    cols = far_refs[0].shape[1]
    pieces = [(0, i, w_refs[0], i) for i in range(n_y)]
    pieces += [(3, i, w_refs[1], i) for i in range(n_y)]
    pieces += [(1, i, w_refs[2], i) for i in range(n_y)]
    pieces += [(2, i, w_refs[3 + i // 2], i % 2) for i in range(n_y)]

    def columns(far, i):
        start = ((info[CHIP] >> 3 ^ i) * 4 + ((info[CHIP] + far) & 3)) * lane
        return pl.ds(pl.multiple_of(start, lane), lane)

    proj = jnp.zeros((2 * half, 2 * units), jnp.float32)
    for far, i, w_ref, at in pieces:
        tok = jnp.concatenate([r[:, columns(far, i)] for r in tok_refs], axis=0)
        proj += dot(tok, w_ref[at, : 2 * units], 1, 1)
    hidden = (jax.nn.silu(proj[:, :units]) * proj[:, units:]).astype(jnp.bfloat16)
    for far, i, w_ref, at in pieces:
        out = dot(hidden, w_ref[at, 2 * units :], 1, 0).astype(jnp.bfloat16)
        far_rows[:, columns(far, i)] = out[:half]
        near_ref[:, columns(far, i)] = out[half:]
    for i, far_ref in enumerate(far_refs):
        start = pl.multiple_of((info[TENSOR] ^ i) * cols, cols)
        far_ref[...] = far_rows[:, pl.ds(start, cols)]


def hot_ffn(info, blocks, hot_w, rows):
    width = blocks[0].shape[1]
    w_size = sum(w.size for w in hot_w)
    spec = pl.BlockSpec((rows, width), lambda i, info: (span_at(info, 0), 0))
    n_t = lax.axis_size("t")
    shapes = [jax.ShapeDtypeStruct((2 * rows, width // n_t), jnp.bfloat16)] * n_t
    shapes.append(jax.ShapeDtypeStruct((2 * rows, width), jnp.bfloat16))
    *far, near = pl.pallas_call(
        hot_kernel,
        out_shape=shapes,
        grid_spec=pltpu.PrefetchScalarGridSpec(
            num_scalar_prefetch=1,
            grid=(1,),
            in_specs=[spec] * 4 + [whole(w.shape) for w in hot_w],
            out_specs=[whole(shape.shape) for shape in shapes],
            scratch_shapes=[pltpu.VMEM((2 * rows, width), jnp.bfloat16)],
        ),
        compiler_params=PARAMS,
        cost_estimate=cost(8 * rows * w_size, 2 * w_size + 16 * rows * width),
    )(info, *blocks, *hot_w)
    return near, far


def pack(tokens, expert_ids, gate_values):
    tok_dev, width = tokens.shape
    meta = jnp.concatenate([expert_ids.astype(jnp.bfloat16), gate_values.astype(jnp.bfloat16)], axis=1)
    meta = meta.T.reshape(1, -1)
    meta = jnp.pad(meta, ((0, 7), (0, width - meta.shape[1])))
    return jnp.concatenate([tokens, meta], axis=0)


def route_kernel(info, a_ref, b_ref, *refs):
    send_ref, mix_ref, hot_mix_ref = refs[-3:]
    zh, c = info[Z_HI], info[CORE]
    n_slot, n_tok = mix_ref.shape
    tok_dev = n_tok // 2
    span_rows = tok_dev // SPANS

    def entry(k):
        at = slice(k * tok_dev, (k + 1) * tok_dev)
        row = jnp.concatenate(
            [a_ref[tok_dev : tok_dev + 8, at], b_ref[tok_dev : tok_dev + 8, at]], axis=1
        )
        return row.astype(jnp.float32)[:1]

    row = iota((1, n_tok), 1)
    group = row // span_rows
    span = group % SPANS
    hot = sum(jnp.where(span == s, info[s], 0) for s in range(SPANS)).astype(jnp.float32)

    slot = pl.program_id(0) * n_slot + iota((n_slot, 1), 0)
    dest, local = slot // 32, slot // 16 % 2
    expert = ((dest // 4 * 2 + zh) * 4 + dest % 4) * 4 + c * 2 + local
    expert = expert.astype(jnp.float32)
    gate = jnp.zeros((n_slot, n_tok), jnp.float32)
    hits = jnp.zeros((n_slot, n_tok), jnp.float32)
    hot_gate = jnp.zeros((1, n_tok), jnp.float32)
    for k in range(TOP_K):
        ids, gates = entry(k), entry(TOP_K + k)
        same = expert == ids
        gate = jnp.where(same, gates, gate)
        hits = jnp.where(same, 1.0, hits)
        hot_gate += jnp.where(ids == hot, gates, 0.0)
    named = jnp.where(expert == hot, 0.0, hits)
    before, after = iota((n_tok, n_tok), 0), iota((n_tok, n_tok), 1)
    earlier = (before // span_rows == after // span_rows) & (before < after)
    earlier = jnp.where(earlier, 1.0, 0.0).astype(jnp.bfloat16)
    rank = dot(named.astype(jnp.bfloat16), earlier, 1, 0)
    at = (slot // CAPACITY % (2 * SPANS)) == group
    chosen = (named > 0.5) & at & (rank == (slot % CAPACITY).astype(jnp.float32))
    pick = jnp.where(chosen, 1.0, 0.0).astype(jnp.bfloat16)
    sent = dot(pick[:, :tok_dev], a_ref[:tok_dev], 1, 0)
    sent += dot(pick[:, tok_dev:], b_ref[:tok_dev], 1, 0)
    send_ref[...] = sent.astype(jnp.bfloat16).reshape(send_ref.shape)
    mix_ref[...] = jnp.where(chosen, gate, 0.0).astype(jnp.bfloat16)
    hot_row = iota((2 * span_rows, 1), 0)
    hot_row = hot_row // span_rows * tok_dev + (2 * zh + c) * span_rows + hot_row % span_rows
    hot_mix_ref[...] = jnp.where(hot_row == row, hot_gate, 0.0).astype(jnp.bfloat16)


def route(info, a, b, tok_dev, half, base=()):
    width = a.shape[1]
    n_slot = 32 * 2 * SPANS * CAPACITY
    n_dest = 16
    steps = 4
    span_rows = tok_dev // SPANS
    rows = n_slot // n_dest
    shapes = (
        jax.ShapeDtypeStruct((n_dest, 2 * rows, width), jnp.bfloat16),
        jax.ShapeDtypeStruct((n_slot, 2 * tok_dev), jnp.bfloat16),
        jax.ShapeDtypeStruct((2 * span_rows, 2 * tok_dev), jnp.bfloat16),
    )
    return pl.pallas_call(
        route_kernel,
        out_shape=shapes,
        grid_spec=pltpu.PrefetchScalarGridSpec(
            num_scalar_prefetch=1,
            grid=(steps,),
            in_specs=[whole(a.shape), whole(b.shape)]
            + [pl.BlockSpec(memory_space=pl.ANY)] * len(base),
            out_specs=(
                pl.BlockSpec((n_dest // steps, rows, width), lambda i, info: (i, half, 0)),
                pl.BlockSpec((n_slot // steps, 2 * tok_dev), lambda i, info: (i, 0)),
                whole(shapes[2].shape),
            ),
        ),
        input_output_aliases={3: 0} if base else {},
        compiler_params=PARAMS,
        cost_estimate=cost(4 * n_slot * tok_dev * width, 2 * width * (n_slot + 2 * tok_dev)),
    )(info, a, b, *base)


def ffn_kernel(info, x_ref, gate_ref, up_ref, down_ref, *out_refs):
    n_src, rows, width = x_ref.shape
    x = x_ref[...].reshape(n_src * rows, width)
    gate = dot(x, gate_ref[0], 1, 1)
    up = dot(x, up_ref[0], 1, 1)
    hidden = (jax.nn.silu(gate) * up).astype(jnp.bfloat16)
    if len(out_refs) == 1:
        out = dot(hidden, down_ref[0], 1, 0).astype(jnp.bfloat16)
        out_refs[0][...] = out.reshape(n_src, rows, width)
        return
    cols = width // len(out_refs)
    for i, out_ref in enumerate(out_refs):
        start = pl.multiple_of((info[TENSOR] ^ i) * cols, cols)
        out = dot(hidden, down_ref[0, :, pl.ds(start, cols)], 1, 0).astype(jnp.bfloat16)
        out_ref[...] = out.reshape(n_src, rows, cols)


def ffn(info, x, w_gate, w_up, w_down, half, groups):
    n_src, rows, width = x.shape
    exp_dev, units, _ = w_gate.shape
    rows //= 2
    cols = width // groups
    block = (n_src, rows // exp_dev)
    w_spec = pl.BlockSpec((1, units, width), lambda e, info: (e, 0, 0))
    return pl.pallas_call(
        ffn_kernel,
        out_shape=[jax.ShapeDtypeStruct((n_src, rows, cols), jnp.bfloat16)] * groups,
        grid_spec=pltpu.PrefetchScalarGridSpec(
            num_scalar_prefetch=1,
            grid=(exp_dev,),
            in_specs=[
                pl.BlockSpec((*block, width), lambda e, info: (0, half * exp_dev + e, 0)),
                w_spec,
                w_spec,
                w_spec,
            ],
            out_specs=[pl.BlockSpec((*block, cols), lambda e, info: (0, e, 0))] * groups,
        ),
        compiler_params=PARAMS,
        cost_estimate=cost(6 * n_src * rows * units * width, 2 * x.size + 6 * w_gate.size),
    )(info, x, w_gate, w_up, w_down)


def mix_kernel(info, mix_ref, hot_mix_ref, ret_ref, hot_ref, own_ref, other_ref):
    out = dot(mix_ref[...], ret_ref[...], 0, 0) + dot(hot_mix_ref[...], hot_ref[...], 0, 0)
    out = out.astype(jnp.bfloat16)
    half = out.shape[0] // 2
    own_ref[0] = out[:half]
    other_ref[0] = out[half:]


def mix_rows(info, mix, hot_mix, returned, hot):
    n_slot, n_tok = mix.shape
    width = returned.shape[1]
    n_group = lax.axis_size("t")
    cols = width // n_group
    shape = jax.ShapeDtypeStruct((n_group, n_tok // 2, cols), jnp.bfloat16)
    out = pl.BlockSpec((1, n_tok // 2, cols), lambda i, info: (i, 0, 0))
    return pl.pallas_call(
        mix_kernel,
        out_shape=(shape, shape),
        grid_spec=pltpu.PrefetchScalarGridSpec(
            num_scalar_prefetch=1,
            grid=(n_group,),
            in_specs=[
                whole(mix.shape),
                whole(hot_mix.shape),
                pl.BlockSpec((n_slot, cols), lambda i, info: (0, i ^ info[TENSOR])),
                pl.BlockSpec((hot.shape[0], cols), lambda i, info: (0, i ^ info[TENSOR])),
            ],
            out_specs=(out, out),
        ),
        compiler_params=PARAMS,
        cost_estimate=cost(2 * n_slot * n_tok * width, 2 * width * (n_slot + n_tok)),
    )(info, mix, hot_mix, returned, hot)


def mix_quarter_kernel(mix_ref, hot_mix_ref, ret_ref, hot_ref, own_ref, other_ref):
    out = dot(mix_ref[...], ret_ref[...], 0, 0) + dot(hot_mix_ref[...], hot_ref[...], 0, 0)
    half = out.shape[0] // 2
    own_ref[...] = out[:half]
    other_ref[...] = out[half:].astype(jnp.bfloat16)


def mix_quarter(mix, hot_mix, returned, hot):
    rows, cols = mix.shape[1] // 2, returned.shape[1]
    return pl.pallas_call(
        mix_quarter_kernel,
        out_shape=(
            jax.ShapeDtypeStruct((rows, cols), jnp.float32),
            jax.ShapeDtypeStruct((rows, cols), jnp.bfloat16),
        ),
        compiler_params=PARAMS,
        cost_estimate=cost(2 * mix.size * cols, 2 * (mix.size + returned.size)),
    )(mix, hot_mix, returned, hot)


def exchange(send):
    return lax.all_to_all(send, ("y", "x"), 0, 0, tiled=True)


def to_t(groups, *shifts):
    pairs = range(len(groups))
    return tuple(lax.ppermute(groups[k], "t", [(i, i ^ k) for i in pairs]) for k in shifts)


def total_of(parts):
    return sum(part.astype(jnp.float32) for part in parts).astype(jnp.bfloat16)


def per_device(tokens, expert_ids, gate_values, hot_ids, w_gate, w_up, w_down):
    y, zh, x, c, t = (lax.axis_index(name) for name in ("y", "zh", "x", "c", "t"))
    n_t = lax.axis_size("t")
    tok_dev, width = tokens.shape
    place = jnp.stack([(y * 2 + zh) * 4 + x, zh, c, t, 0]).astype(jnp.int32)
    info = jnp.concatenate([hot_ids, place])
    experts = (w_gate, w_up, w_down)

    own = pack(tokens, expert_ids, gate_values)
    own_z = lax.ppermute(own, "zh", SWAP)
    own_c = lax.ppermute(own, "c", SWAP)
    rows, near_mix, near_hot_mix = route(info, own, own_c, tok_dev, 0)
    n_slot = near_mix.shape[0]

    chunks = first_chunks(info, hot_ids, experts)
    own_zc = lax.ppermute(own_z, "c", SWAP)
    rows, far_mix, far_hot_mix = route(info, own_z, own_zc, tok_dev, 1, (rows,))
    rows, chunks = lax.optimization_barrier((rows, chunks))
    rows = exchange(rows)
    hot_w = along_y(own_span(info, chunks, c))
    hot_w = (hot_w, shift_x(hot_w, 1), shift_x(hot_w, -1))
    rows, hot_w = lax.optimization_barrier((rows, hot_w))
    far = ffn(info, rows, *experts, 1, n_t)
    far, rows = lax.optimization_barrier((tuple(far), rows))
    (near,) = ffn(info, rows, *experts, 0, 1)
    near = exchange(near)
    far, hot_w = lax.optimization_barrier((far, hot_w))
    half = hot_w[0].shape[0] // 2
    hot_w += (shift_x(hot_w[1][:half], 1), shift_x(hot_w[2][half:], -1))
    far = total_of((far[0], *to_t(far, 1, 2, 3)))
    near_hot, far_hot = hot_ffn(info, (own_z, own_zc, own, own_c), hot_w, tok_dev // SPANS)
    mine, other = mix_rows(info, near_mix, near_hot_mix, near.reshape(n_slot, width), near_hot)
    got = lax.ppermute(other, "c", SWAP)
    mine, got, far, far_hot = lax.optimization_barrier((mine, got, far, far_hot))

    far_hot = total_of((far_hot[0], *to_t(far_hot, 1, 2, 3)))
    far = exchange(far).reshape(n_slot, width // n_t)
    pieces = [mine[k].astype(jnp.float32) + got[k].astype(jnp.float32) for k in range(n_t)]
    total = pieces[0]
    for part in to_t([piece.astype(jnp.bfloat16) for piece in pieces], 1, 2, 3):
        total += part.astype(jnp.float32)
    far, total = lax.optimization_barrier((far, total))
    mine, other = mix_quarter(far_mix, far_hot_mix, far, far_hot)
    mine += lax.ppermute(other, "c", SWAP).astype(jnp.float32)
    got = lax.ppermute(mine.astype(jnp.bfloat16), "zh", SWAP)
    return (total + got.astype(jnp.float32)).astype(jnp.bfloat16)


def solution(mesh):
    fine = Mesh(mesh.devices.reshape(4, 2, 4, 2, 4), ("y", "zh", "x", "c", "t"))
    owner = ("y", "zh", "x", "c")
    in_specs = (
        P(owner, None),
        P(owner, None),
        P(owner, None),
        P(),
        P(owner, "t", None),
        P(owner, "t", None),
        P(owner, "t", None),
    )
    return jax.shard_map(
        per_device, mesh=fine, in_specs=in_specs, out_specs=P(owner, "t"), check_vma=False
    )
```

```python
import jax
import jax.numpy as jnp
from jax import lax
from jax.experimental import pallas as pl
from jax.experimental.pallas import tpu as pltpu
from jax.sharding import Mesh, PartitionSpec as P

SPANS = 4
CAPACITY = 2
TOP_K = 8
SWAP = ((0, 1), (1, 0))
VMEM_LIMIT = 32 * 1024 * 1024


def dot(a, b, contract_a, contract_b):
    dims = (((contract_a,), (contract_b,)), ((), ()))
    return lax.dot_general(a, b, dims, preferred_element_type=jnp.float32)


def iota(shape, dim):
    return lax.broadcasted_iota(jnp.int32, shape, dim)


def cost(flops, moved):
    return pl.CostEstimate(flops=flops, bytes_accessed=moved, transcendentals=0)


PARAMS = pltpu.CompilerParams(vmem_limit_bytes=VMEM_LIMIT)


def whole(shape):
    return pl.BlockSpec(shape, lambda *_: (0,) * len(shape))


CHIP, Z_HI, CORE, TENSOR, TURN = 4, 5, 6, 7, 8


def chip_of(expert):
    return expert >> 2


def order_of(info, span):
    chip = chip_of(info[span])
    return sum(((chip_of(info[s]) == chip) & (s < span)).astype(jnp.int32) for s in range(SPANS))


def my_turn(info):
    return sum(
        jnp.where((chip_of(info[s]) == info[CHIP]) & (order_of(info, s) == info[TURN]), info[s], 0)
        for s in range(SPANS)
    )


def chunk_kernel(info, gate_ref, up_ref, down_ref, keep_ref, give_ref):
    units = gate_ref.shape[1]
    mid = units // 2
    n_chunk, _, lane = keep_ref.shape

    def first(out):
        for n in range(n_chunk):
            at = slice(n * lane, (n + 1) * lane)
            out[n, :units] = gate_ref[0, :, at]
            out[n, units:] = up_ref[0, :mid, at]

    def second(out):
        for n in range(n_chunk):
            at = slice(n * lane, (n + 1) * lane)
            out[n, :mid] = up_ref[0, mid:, at]
            out[n, mid:] = down_ref[0, :, at]

    @pl.when(info[CORE] == 0)
    def _():
        first(keep_ref)
        second(give_ref)

    @pl.when(info[CORE] == 1)
    def _():
        second(keep_ref)
        first(give_ref)


def cut_chunks(info, held):
    _, units, width = held[0].shape
    steps = 4
    half, lane = 3 * units // 2, width // 16
    spec = pl.BlockSpec((1, units, width // steps), lambda n, info: (my_turn(info) & 1, 0, n))
    out = pl.BlockSpec((16 // steps, half, lane), lambda n, info: (n, 0, 0))
    shape = jax.ShapeDtypeStruct((16, half, lane), jnp.bfloat16)
    return pl.pallas_call(
        chunk_kernel,
        out_shape=(shape, shape),
        grid_spec=pltpu.PrefetchScalarGridSpec(
            num_scalar_prefetch=1, grid=(steps,), in_specs=[spec] * 3, out_specs=(out, out)
        ),
        compiler_params=PARAMS,
        cost_estimate=cost(0, 4 * 3 * units * width),
    )(info, *held)


def choose_kernel(info, keep_ref, got_ref, out_ref):
    held_here = ((my_turn(info) >> 1) & 1) == info[CORE]

    @pl.when(held_here)
    def _():
        out_ref[...] = keep_ref[...]

    @pl.when(jnp.logical_not(held_here))
    def _():
        out_ref[...] = got_ref[...]


def choose(info, keep, got):
    return pl.pallas_call(
        choose_kernel,
        out_shape=jax.ShapeDtypeStruct(keep.shape, keep.dtype),
        grid_spec=pltpu.PrefetchScalarGridSpec(
            num_scalar_prefetch=1,
            grid=(1,),
            in_specs=[whole(keep.shape)] * 2,
            out_specs=whole(keep.shape),
        ),
        compiler_params=PARAMS,
        cost_estimate=cost(0, 6 * keep.size),
    )(info, keep, got)


def span_at(info, i):
    return (2 * info[Z_HI] + info[CORE]) ^ i


def take_kernel(info, part_ref, *refs):
    *old_refs, out_ref = refs
    span = span_at(info, pl.program_id(0))
    expert = info[span]
    here = (((expert >> 4) & 1) == info[Z_HI]) & (order_of(info, span) == info[TURN])
    if old_refs:
        out_ref[...] = jnp.where(here, part_ref[...], old_refs[0][...])
    else:
        out_ref[...] = part_ref[...]


def take(info, part, *old):
    block = (1, *part.shape[1:])

    def source(i, info):
        expert = info[span_at(info, i)]
        return ((expert >> 5) * 4 + ((expert >> 2) & 3), 0, 0)

    def same(i, info):
        return (i, 0, 0)

    return pl.pallas_call(
        take_kernel,
        out_shape=jax.ShapeDtypeStruct((SPANS, *part.shape[1:]), part.dtype),
        grid_spec=pltpu.PrefetchScalarGridSpec(
            num_scalar_prefetch=1,
            grid=(SPANS,),
            in_specs=[pl.BlockSpec(block, source)] + [pl.BlockSpec(block, same)] * len(old),
            out_specs=pl.BlockSpec(block, same),
        ),
        compiler_params=PARAMS,
        cost_estimate=cost(0, 16 * block[1] * block[2]),
    )(info, part, *old)


def hot_round(info, held, *old):
    keep, give = cut_chunks(info, held)
    part = choose(info, keep, lax.ppermute(give, "c", SWAP))
    part = lax.all_to_all(part, ("y", "x"), 0, 0, tiled=True)
    return take(info, part, *old)


def pair_kernel(info, chunk_ref, got_ref, mine_ref, give_ref):
    for i, out_ref in enumerate((mine_ref, give_ref)):
        here = ((info[span_at(info, i)] >> 4) & 1) == info[Z_HI]
        out_ref[...] = jnp.where(here, chunk_ref[i], got_ref[i])


def pair(info, chunks, got):
    shape = jax.ShapeDtypeStruct(chunks.shape[1:], chunks.dtype)
    return pl.pallas_call(
        pair_kernel,
        out_shape=(shape, shape),
        grid_spec=pltpu.PrefetchScalarGridSpec(
            num_scalar_prefetch=1,
            grid=(1,),
            in_specs=[whole(got.shape)] * 2,
            out_specs=(whole(shape.shape), whole(shape.shape)),
        ),
        compiler_params=PARAMS,
        cost_estimate=cost(0, 12 * shape.size),
    )(info, chunks, got)


def first_chunks(info, hot_ids, held):
    chips = chip_of(hot_ids)
    before = jnp.arange(SPANS)[None, :] < jnp.arange(SPANS)[:, None]
    turns = 1 + jnp.max(jnp.sum((chips[:, None] == chips[None, :]) & before, axis=1))
    chunks = hot_round(info, held)
    return lax.fori_loop(
        1, turns, lambda turn, old: hot_round(info.at[TURN].set(turn), held, old), chunks
    )


def own_span(info, chunks, c):
    got = lax.ppermute(chunks[2:], "zh", SWAP)
    mine, give = pair(info, chunks, got)
    got = lax.ppermute(give, "c", SWAP)
    first, second = jnp.where(c == 0, mine, got), jnp.where(c == 0, got, mine)
    return jnp.concatenate([first, second], axis=0)


def along_y(chunk):
    n_y = lax.axis_size("y")
    column = [chunk]
    for k in range(1, n_y):
        column.append(lax.ppermute(chunk, "y", [(i, i ^ k) for i in range(n_y)]))
    return jnp.stack(column)


def shift_x(array, step):
    n_x = lax.axis_size("x")
    return lax.ppermute(array, "x", [(i, (i + step) % n_x) for i in range(n_x)])


def hot_kernel(info, *refs):
    *refs, near_ref, far_rows = refs
    tok_refs, w_refs, far_refs = refs[:4], refs[4:9], refs[9:]
    n_y, rows, lane = w_refs[0].shape
    units = rows // 3
    half = near_ref.shape[0]
    cols = far_refs[0].shape[1]
    pieces = [(0, i, w_refs[0], i) for i in range(n_y)]
    pieces += [(3, i, w_refs[1], i) for i in range(n_y)]
    pieces += [(1, i, w_refs[2], i) for i in range(n_y)]
    pieces += [(2, i, w_refs[3 + i // 2], i % 2) for i in range(n_y)]

    def columns(far, i):
        start = ((info[CHIP] >> 3 ^ i) * 4 + ((info[CHIP] + far) & 3)) * lane
        return pl.ds(pl.multiple_of(start, lane), lane)

    proj = jnp.zeros((2 * half, 2 * units), jnp.float32)
    for far, i, w_ref, at in pieces:
        tok = jnp.concatenate([r[:, columns(far, i)] for r in tok_refs], axis=0)
        proj += dot(tok, w_ref[at, : 2 * units], 1, 1)
    hidden = (jax.nn.silu(proj[:, :units]) * proj[:, units:]).astype(jnp.bfloat16)
    for far, i, w_ref, at in pieces:
        out = dot(hidden, w_ref[at, 2 * units :], 1, 0).astype(jnp.bfloat16)
        far_rows[:, columns(far, i)] = out[:half]
        near_ref[:, columns(far, i)] = out[half:]
    for i, far_ref in enumerate(far_refs):
        start = pl.multiple_of((info[TENSOR] ^ i) * cols, cols)
        far_ref[...] = far_rows[:, pl.ds(start, cols)]


def hot_ffn(info, blocks, hot_w, rows):
    width = blocks[0].shape[1]
    w_size = sum(w.size for w in hot_w)
    spec = pl.BlockSpec((rows, width), lambda i, info: (span_at(info, 0), 0))
    n_t = lax.axis_size("t")
    shapes = [jax.ShapeDtypeStruct((2 * rows, width // n_t), jnp.bfloat16)] * n_t
    shapes.append(jax.ShapeDtypeStruct((2 * rows, width), jnp.bfloat16))
    *far, near = pl.pallas_call(
        hot_kernel,
        out_shape=shapes,
        grid_spec=pltpu.PrefetchScalarGridSpec(
            num_scalar_prefetch=1,
            grid=(1,),
            in_specs=[spec] * 4 + [whole(w.shape) for w in hot_w],
            out_specs=[whole(shape.shape) for shape in shapes],
            scratch_shapes=[pltpu.VMEM((2 * rows, width), jnp.bfloat16)],
        ),
        compiler_params=PARAMS,
        cost_estimate=cost(8 * rows * w_size, 2 * w_size + 16 * rows * width),
    )(info, *blocks, *hot_w)
    return near, far


def pack(tokens, expert_ids, gate_values):
    tok_dev, width = tokens.shape
    meta = jnp.concatenate([expert_ids.astype(jnp.bfloat16), gate_values.astype(jnp.bfloat16)], axis=1)
    meta = meta.T.reshape(1, -1)
    meta = jnp.pad(meta, ((0, 7), (0, width - meta.shape[1])))
    return jnp.concatenate([tokens, meta], axis=0)


def route_kernel(info, a_ref, b_ref, *refs):
    send_ref, mix_ref, hot_mix_ref = refs[-3:]
    zh, c = info[Z_HI], info[CORE]
    n_slot, n_tok = mix_ref.shape
    tok_dev = n_tok // 2
    span_rows = tok_dev // SPANS

    def entry(k):
        at = slice(k * tok_dev, (k + 1) * tok_dev)
        row = jnp.concatenate(
            [a_ref[tok_dev : tok_dev + 8, at], b_ref[tok_dev : tok_dev + 8, at]], axis=1
        )
        return row.astype(jnp.float32)[:1]

    row = iota((1, n_tok), 1)
    group = row // span_rows
    span = group % SPANS
    hot = sum(jnp.where(span == s, info[s], 0) for s in range(SPANS)).astype(jnp.float32)

    slot = pl.program_id(0) * n_slot + iota((n_slot, 1), 0)
    dest, local = slot // 32, slot // 16 % 2
    expert = ((dest // 4 * 2 + zh) * 4 + dest % 4) * 4 + c * 2 + local
    expert = expert.astype(jnp.float32)
    gate = jnp.zeros((n_slot, n_tok), jnp.float32)
    hits = jnp.zeros((n_slot, n_tok), jnp.float32)
    hot_gate = jnp.zeros((1, n_tok), jnp.float32)
    for k in range(TOP_K):
        ids, gates = entry(k), entry(TOP_K + k)
        same = expert == ids
        gate = jnp.where(same, gates, gate)
        hits = jnp.where(same, 1.0, hits)
        hot_gate += jnp.where(ids == hot, gates, 0.0)
    named = jnp.where(expert == hot, 0.0, hits)
    before, after = iota((n_tok, n_tok), 0), iota((n_tok, n_tok), 1)
    earlier = (before // span_rows == after // span_rows) & (before < after)
    earlier = jnp.where(earlier, 1.0, 0.0).astype(jnp.bfloat16)
    rank = dot(named.astype(jnp.bfloat16), earlier, 1, 0)
    at = (slot // CAPACITY % (2 * SPANS)) == group
    chosen = (named > 0.5) & at & (rank == (slot % CAPACITY).astype(jnp.float32))
    pick = jnp.where(chosen, 1.0, 0.0).astype(jnp.bfloat16)
    sent = dot(pick[:, :tok_dev], a_ref[:tok_dev], 1, 0)
    sent += dot(pick[:, tok_dev:], b_ref[:tok_dev], 1, 0)
    send_ref[...] = sent.astype(jnp.bfloat16).reshape(send_ref.shape)
    mix_ref[...] = jnp.where(chosen, gate, 0.0).astype(jnp.bfloat16)
    hot_row = iota((2 * span_rows, 1), 0)
    hot_row = hot_row // span_rows * tok_dev + (2 * zh + c) * span_rows + hot_row % span_rows
    hot_mix_ref[...] = jnp.where(hot_row == row, hot_gate, 0.0).astype(jnp.bfloat16)


def route(info, a, b, tok_dev, half, base=()):
    width = a.shape[1]
    n_slot = 32 * 2 * SPANS * CAPACITY
    n_dest = 16
    steps = 4
    span_rows = tok_dev // SPANS
    rows = n_slot // n_dest
    shapes = (
        jax.ShapeDtypeStruct((n_dest, 2 * rows, width), jnp.bfloat16),
        jax.ShapeDtypeStruct((n_slot, 2 * tok_dev), jnp.bfloat16),
        jax.ShapeDtypeStruct((2 * span_rows, 2 * tok_dev), jnp.bfloat16),
    )
    return pl.pallas_call(
        route_kernel,
        out_shape=shapes,
        grid_spec=pltpu.PrefetchScalarGridSpec(
            num_scalar_prefetch=1,
            grid=(steps,),
            in_specs=[whole(a.shape), whole(b.shape)]
            + [pl.BlockSpec(memory_space=pl.ANY)] * len(base),
            out_specs=(
                pl.BlockSpec((n_dest // steps, rows, width), lambda i, info: (i, half, 0)),
                pl.BlockSpec((n_slot // steps, 2 * tok_dev), lambda i, info: (i, 0)),
                whole(shapes[2].shape),
            ),
        ),
        input_output_aliases={3: 0} if base else {},
        compiler_params=PARAMS,
        cost_estimate=cost(4 * n_slot * tok_dev * width, 2 * width * (n_slot + 2 * tok_dev)),
    )(info, a, b, *base)


def ffn_kernel(info, x_ref, gate_ref, up_ref, down_ref, *out_refs):
    n_src, rows, width = x_ref.shape
    x = x_ref[...].reshape(n_src * rows, width)
    gate = dot(x, gate_ref[0], 1, 1)
    up = dot(x, up_ref[0], 1, 1)
    hidden = (jax.nn.silu(gate) * up).astype(jnp.bfloat16)
    if len(out_refs) == 1:
        out = dot(hidden, down_ref[0], 1, 0).astype(jnp.bfloat16)
        out_refs[0][...] = out.reshape(n_src, rows, width)
        return
    cols = width // len(out_refs)
    for i, out_ref in enumerate(out_refs):
        start = pl.multiple_of((info[TENSOR] ^ i) * cols, cols)
        out = dot(hidden, down_ref[0, :, pl.ds(start, cols)], 1, 0).astype(jnp.bfloat16)
        out_ref[...] = out.reshape(n_src, rows, cols)


def ffn(info, x, w_gate, w_up, w_down, half, groups):
    n_src, rows, width = x.shape
    exp_dev, units, _ = w_gate.shape
    rows //= 2
    cols = width // groups
    block = (n_src, rows // exp_dev)
    w_spec = pl.BlockSpec((1, units, width), lambda e, info: (e, 0, 0))
    return pl.pallas_call(
        ffn_kernel,
        out_shape=[jax.ShapeDtypeStruct((n_src, rows, cols), jnp.bfloat16)] * groups,
        grid_spec=pltpu.PrefetchScalarGridSpec(
            num_scalar_prefetch=1,
            grid=(exp_dev,),
            in_specs=[
                pl.BlockSpec((*block, width), lambda e, info: (0, half * exp_dev + e, 0)),
                w_spec,
                w_spec,
                w_spec,
            ],
            out_specs=[pl.BlockSpec((*block, cols), lambda e, info: (0, e, 0))] * groups,
        ),
        compiler_params=PARAMS,
        cost_estimate=cost(6 * n_src * rows * units * width, 2 * x.size + 6 * w_gate.size),
    )(info, x, w_gate, w_up, w_down)


def mix_kernel(info, mix_ref, hot_mix_ref, ret_ref, hot_ref, own_ref, other_ref):
    out = dot(mix_ref[...], ret_ref[...], 0, 0) + dot(hot_mix_ref[...], hot_ref[...], 0, 0)
    out = out.astype(jnp.bfloat16)
    half = out.shape[0] // 2
    own_ref[0] = out[:half]
    other_ref[0] = out[half:]


def mix_rows(info, mix, hot_mix, returned, hot):
    n_slot, n_tok = mix.shape
    width = returned.shape[1]
    n_group = lax.axis_size("t")
    cols = width // n_group
    shape = jax.ShapeDtypeStruct((n_group, n_tok // 2, cols), jnp.bfloat16)
    out = pl.BlockSpec((1, n_tok // 2, cols), lambda i, info: (i, 0, 0))
    return pl.pallas_call(
        mix_kernel,
        out_shape=(shape, shape),
        grid_spec=pltpu.PrefetchScalarGridSpec(
            num_scalar_prefetch=1,
            grid=(n_group,),
            in_specs=[
                whole(mix.shape),
                whole(hot_mix.shape),
                pl.BlockSpec((n_slot, cols), lambda i, info: (0, i ^ info[TENSOR])),
                pl.BlockSpec((hot.shape[0], cols), lambda i, info: (0, i ^ info[TENSOR])),
            ],
            out_specs=(out, out),
        ),
        compiler_params=PARAMS,
        cost_estimate=cost(2 * n_slot * n_tok * width, 2 * width * (n_slot + n_tok)),
    )(info, mix, hot_mix, returned, hot)


def mix_quarter_kernel(mix_ref, hot_mix_ref, ret_ref, hot_ref, own_ref, other_ref):
    out = dot(mix_ref[...], ret_ref[...], 0, 0) + dot(hot_mix_ref[...], hot_ref[...], 0, 0)
    half = out.shape[0] // 2
    own_ref[...] = out[:half]
    other_ref[...] = out[half:].astype(jnp.bfloat16)


def mix_quarter(mix, hot_mix, returned, hot):
    rows, cols = mix.shape[1] // 2, returned.shape[1]
    return pl.pallas_call(
        mix_quarter_kernel,
        out_shape=(
            jax.ShapeDtypeStruct((rows, cols), jnp.float32),
            jax.ShapeDtypeStruct((rows, cols), jnp.bfloat16),
        ),
        compiler_params=PARAMS,
        cost_estimate=cost(2 * mix.size * cols, 2 * (mix.size + returned.size)),
    )(mix, hot_mix, returned, hot)


def exchange(send):
    return lax.all_to_all(send, ("y", "x"), 0, 0, tiled=True)


def to_t(groups, *shifts):
    pairs = range(len(groups))
    return tuple(lax.ppermute(groups[k], "t", [(i, i ^ k) for i in pairs]) for k in shifts)


def total_of(parts):
    return sum(part.astype(jnp.float32) for part in parts).astype(jnp.bfloat16)


def per_device(tokens, expert_ids, gate_values, hot_ids, w_gate, w_up, w_down):
    y, zh, x, c, t = (lax.axis_index(name) for name in ("y", "zh", "x", "c", "t"))
    n_t = lax.axis_size("t")
    tok_dev, width = tokens.shape
    place = jnp.stack([(y * 2 + zh) * 4 + x, zh, c, t, 0]).astype(jnp.int32)
    info = jnp.concatenate([hot_ids, place])
    experts = (w_gate, w_up, w_down)

    own = pack(tokens, expert_ids, gate_values)
    own_z = lax.ppermute(own, "zh", SWAP)
    own_c = lax.ppermute(own, "c", SWAP)
    rows, near_mix, near_hot_mix = route(info, own, own_c, tok_dev, 0)
    n_slot = near_mix.shape[0]

    chunks = first_chunks(info, hot_ids, experts)
    own_zc = lax.ppermute(own_z, "c", SWAP)
    rows, far_mix, far_hot_mix = route(info, own_z, own_zc, tok_dev, 1, (rows,))
    rows, chunks = lax.optimization_barrier((rows, chunks))
    rows = exchange(rows)
    hot_w = along_y(own_span(info, chunks, c))
    rows, hot_w = lax.optimization_barrier((rows, hot_w))
    hot_w = (hot_w, shift_x(hot_w, 1), shift_x(hot_w, -1))
    far = ffn(info, rows, *experts, 1, n_t)
    far, rows = lax.optimization_barrier((tuple(far), rows))
    (near,) = ffn(info, rows, *experts, 0, 1)
    summands = (far[0], *to_t(far, 1))
    near, hot_w, summands = lax.optimization_barrier((near, hot_w, summands))
    near = exchange(near)
    half = hot_w[0].shape[0] // 2
    hot_w += (shift_x(hot_w[1][:half], 1), shift_x(hot_w[2][half:], -1))
    far = total_of(summands + to_t(far, 2, 3))
    near_hot, far_hot = hot_ffn(info, (own_z, own_zc, own, own_c), hot_w, tok_dev // SPANS)
    mine, other = mix_rows(info, near_mix, near_hot_mix, near.reshape(n_slot, width), near_hot)
    got = lax.ppermute(other, "c", SWAP)
    mine, got, far, far_hot = lax.optimization_barrier((mine, got, far, far_hot))

    far = exchange(far).reshape(n_slot, width // n_t)
    pieces = [mine[k].astype(jnp.float32) + got[k].astype(jnp.float32) for k in range(n_t)]
    parts = to_t(
        [jnp.concatenate([p.astype(jnp.bfloat16), h]) for p, h in zip(pieces, far_hot)], 1, 2, 3
    )
    total = pieces[0] + sum(part[:tok_dev].astype(jnp.float32) for part in parts)
    far_hot = total_of((far_hot[0], *(part[tok_dev:] for part in parts)))
    far, total = lax.optimization_barrier((far, total))
    mine, other = mix_quarter(far_mix, far_hot_mix, far, far_hot)
    mine += lax.ppermute(other, "c", SWAP).astype(jnp.float32)
    got = lax.ppermute(mine.astype(jnp.bfloat16), "zh", SWAP)
    return (total + got.astype(jnp.float32)).astype(jnp.bfloat16)


def solution(mesh):
    fine = Mesh(mesh.devices.reshape(4, 2, 4, 2, 4), ("y", "zh", "x", "c", "t"))
    owner = ("y", "zh", "x", "c")
    in_specs = (
        P(owner, None),
        P(owner, None),
        P(owner, None),
        P(),
        P(owner, "t", None),
        P(owner, "t", None),
        P(owner, "t", None),
    )
    return jax.shard_map(
        per_device, mesh=fine, in_specs=in_specs, out_specs=P(owner, "t"), check_vma=False
    )
```

```python
import jax
import jax.numpy as jnp
from jax import lax
from jax.experimental import pallas as pl
from jax.experimental.pallas import tpu as pltpu
from jax.sharding import Mesh, PartitionSpec as P

SPANS = 4
CAPACITY = 2
TOP_K = 8
SWAP = ((0, 1), (1, 0))
VMEM_LIMIT = 32 * 1024 * 1024


def dot(a, b, contract_a, contract_b):
    dims = (((contract_a,), (contract_b,)), ((), ()))
    return lax.dot_general(a, b, dims, preferred_element_type=jnp.float32)


def iota(shape, dim):
    return lax.broadcasted_iota(jnp.int32, shape, dim)


def cost(flops, moved):
    return pl.CostEstimate(flops=flops, bytes_accessed=moved, transcendentals=0)


PARAMS = pltpu.CompilerParams(vmem_limit_bytes=VMEM_LIMIT)


def whole(shape):
    return pl.BlockSpec(shape, lambda *_: (0,) * len(shape))


CHIP, Z_HI, CORE, TENSOR, TURN = 4, 5, 6, 7, 8


def chip_of(expert):
    return expert >> 2


def order_of(info, span):
    chip = chip_of(info[span])
    return sum(((chip_of(info[s]) == chip) & (s < span)).astype(jnp.int32) for s in range(SPANS))


def my_turn(info):
    return sum(
        jnp.where((chip_of(info[s]) == info[CHIP]) & (order_of(info, s) == info[TURN]), info[s], 0)
        for s in range(SPANS)
    )


def chunk_kernel(info, gate_ref, up_ref, down_ref, keep_ref, give_ref):
    units = gate_ref.shape[1]
    mid = units // 2
    n_chunk, _, lane = keep_ref.shape

    def first(out):
        for n in range(n_chunk):
            at = slice(n * lane, (n + 1) * lane)
            out[n, :units] = gate_ref[0, :, at]
            out[n, units:] = up_ref[0, :mid, at]

    def second(out):
        for n in range(n_chunk):
            at = slice(n * lane, (n + 1) * lane)
            out[n, :mid] = up_ref[0, mid:, at]
            out[n, mid:] = down_ref[0, :, at]

    @pl.when(info[CORE] == 0)
    def _():
        first(keep_ref)
        second(give_ref)

    @pl.when(info[CORE] == 1)
    def _():
        second(keep_ref)
        first(give_ref)


def cut_chunks(info, held):
    _, units, width = held[0].shape
    steps = 4
    half, lane = 3 * units // 2, width // 16
    spec = pl.BlockSpec((1, units, width // steps), lambda n, info: (my_turn(info) & 1, 0, n))
    out = pl.BlockSpec((16 // steps, half, lane), lambda n, info: (n, 0, 0))
    shape = jax.ShapeDtypeStruct((16, half, lane), jnp.bfloat16)
    return pl.pallas_call(
        chunk_kernel,
        out_shape=(shape, shape),
        grid_spec=pltpu.PrefetchScalarGridSpec(
            num_scalar_prefetch=1, grid=(steps,), in_specs=[spec] * 3, out_specs=(out, out)
        ),
        compiler_params=PARAMS,
        cost_estimate=cost(0, 4 * 3 * units * width),
    )(info, *held)


def choose_kernel(info, keep_ref, got_ref, out_ref):
    held_here = ((my_turn(info) >> 1) & 1) == info[CORE]

    @pl.when(held_here)
    def _():
        out_ref[...] = keep_ref[...]

    @pl.when(jnp.logical_not(held_here))
    def _():
        out_ref[...] = got_ref[...]


def choose(info, keep, got):
    return pl.pallas_call(
        choose_kernel,
        out_shape=jax.ShapeDtypeStruct(keep.shape, keep.dtype),
        grid_spec=pltpu.PrefetchScalarGridSpec(
            num_scalar_prefetch=1,
            grid=(1,),
            in_specs=[whole(keep.shape)] * 2,
            out_specs=whole(keep.shape),
        ),
        compiler_params=PARAMS,
        cost_estimate=cost(0, 6 * keep.size),
    )(info, keep, got)


def span_at(info, i):
    return (2 * info[Z_HI] + info[CORE]) ^ i


def take_kernel(info, part_ref, *refs):
    *old_refs, out_ref = refs
    span = span_at(info, pl.program_id(0))
    expert = info[span]
    here = (((expert >> 4) & 1) == info[Z_HI]) & (order_of(info, span) == info[TURN])
    if old_refs:
        out_ref[...] = jnp.where(here, part_ref[...], old_refs[0][...])
    else:
        out_ref[...] = part_ref[...]


def take(info, part, *old):
    block = (1, *part.shape[1:])

    def source(i, info):
        expert = info[span_at(info, i)]
        return ((expert >> 5) * 4 + ((expert >> 2) & 3), 0, 0)

    def same(i, info):
        return (i, 0, 0)

    return pl.pallas_call(
        take_kernel,
        out_shape=jax.ShapeDtypeStruct((SPANS, *part.shape[1:]), part.dtype),
        grid_spec=pltpu.PrefetchScalarGridSpec(
            num_scalar_prefetch=1,
            grid=(SPANS,),
            in_specs=[pl.BlockSpec(block, source)] + [pl.BlockSpec(block, same)] * len(old),
            out_specs=pl.BlockSpec(block, same),
        ),
        compiler_params=PARAMS,
        cost_estimate=cost(0, 16 * block[1] * block[2]),
    )(info, part, *old)


def hot_round(info, held, *old):
    keep, give = cut_chunks(info, held)
    part = choose(info, keep, lax.ppermute(give, "c", SWAP))
    part = lax.all_to_all(part, ("y", "x"), 0, 0, tiled=True)
    return take(info, part, *old)


def pair_kernel(info, chunk_ref, got_ref, mine_ref, give_ref):
    for i, out_ref in enumerate((mine_ref, give_ref)):
        here = ((info[span_at(info, i)] >> 4) & 1) == info[Z_HI]
        out_ref[...] = jnp.where(here, chunk_ref[i], got_ref[i])


def pair(info, chunks, got):
    shape = jax.ShapeDtypeStruct(chunks.shape[1:], chunks.dtype)
    return pl.pallas_call(
        pair_kernel,
        out_shape=(shape, shape),
        grid_spec=pltpu.PrefetchScalarGridSpec(
            num_scalar_prefetch=1,
            grid=(1,),
            in_specs=[whole(got.shape)] * 2,
            out_specs=(whole(shape.shape), whole(shape.shape)),
        ),
        compiler_params=PARAMS,
        cost_estimate=cost(0, 12 * shape.size),
    )(info, chunks, got)


def first_chunks(info, hot_ids, held):
    chips = chip_of(hot_ids)
    before = jnp.arange(SPANS)[None, :] < jnp.arange(SPANS)[:, None]
    turns = 1 + jnp.max(jnp.sum((chips[:, None] == chips[None, :]) & before, axis=1))
    chunks = hot_round(info, held)
    return lax.fori_loop(
        1, turns, lambda turn, old: hot_round(info.at[TURN].set(turn), held, old), chunks
    )


def own_span(info, chunks, c):
    got = lax.ppermute(chunks[2:], "zh", SWAP)
    mine, give = pair(info, chunks, got)
    got = lax.ppermute(give, "c", SWAP)
    first, second = jnp.where(c == 0, mine, got), jnp.where(c == 0, got, mine)
    return jnp.concatenate([first, second], axis=0)


def along_y(chunk):
    n_y = lax.axis_size("y")
    column = [chunk]
    for k in range(1, n_y):
        column.append(lax.ppermute(chunk, "y", [(i, i ^ k) for i in range(n_y)]))
    return jnp.stack(column)


def shift_x(array, step):
    n_x = lax.axis_size("x")
    return lax.ppermute(array, "x", [(i, (i + step) % n_x) for i in range(n_x)])


def hot_kernel(info, *refs):
    *refs, near_ref, far_rows = refs
    tok_refs, w_refs, far_refs = refs[:4], refs[4:9], refs[9:]
    n_y, rows, lane = w_refs[0].shape
    units = rows // 3
    half = near_ref.shape[0]
    cols = far_refs[0].shape[1]
    pieces = [(0, i, w_refs[0], i) for i in range(n_y)]
    pieces += [(3, i, w_refs[1], i) for i in range(n_y)]
    pieces += [(1, i, w_refs[2], i) for i in range(n_y)]
    pieces += [(2, i, w_refs[3 + i // 2], i % 2) for i in range(n_y)]

    def columns(far, i):
        start = ((info[CHIP] >> 3 ^ i) * 4 + ((info[CHIP] + far) & 3)) * lane
        return pl.ds(pl.multiple_of(start, lane), lane)

    proj = jnp.zeros((2 * half, 2 * units), jnp.float32)
    for far, i, w_ref, at in pieces:
        tok = jnp.concatenate([r[:, columns(far, i)] for r in tok_refs], axis=0)
        proj += dot(tok, w_ref[at, : 2 * units], 1, 1)
    hidden = (jax.nn.silu(proj[:, :units]) * proj[:, units:]).astype(jnp.bfloat16)
    for far, i, w_ref, at in pieces:
        out = dot(hidden, w_ref[at, 2 * units :], 1, 0).astype(jnp.bfloat16)
        far_rows[:, columns(far, i)] = out[:half]
        near_ref[:, columns(far, i)] = out[half:]
    for i, far_ref in enumerate(far_refs):
        start = pl.multiple_of((info[TENSOR] ^ i) * cols, cols)
        far_ref[...] = far_rows[:, pl.ds(start, cols)]


def hot_ffn(info, blocks, hot_w, rows):
    width = blocks[0].shape[1]
    w_size = sum(w.size for w in hot_w)
    spec = pl.BlockSpec((rows, width), lambda i, info: (span_at(info, 0), 0))
    n_t = lax.axis_size("t")
    shapes = [jax.ShapeDtypeStruct((2 * rows, width // n_t), jnp.bfloat16)] * n_t
    shapes.append(jax.ShapeDtypeStruct((2 * rows, width), jnp.bfloat16))
    *far, near = pl.pallas_call(
        hot_kernel,
        out_shape=shapes,
        grid_spec=pltpu.PrefetchScalarGridSpec(
            num_scalar_prefetch=1,
            grid=(1,),
            in_specs=[spec] * 4 + [whole(w.shape) for w in hot_w],
            out_specs=[whole(shape.shape) for shape in shapes],
            scratch_shapes=[pltpu.VMEM((2 * rows, width), jnp.bfloat16)],
        ),
        compiler_params=PARAMS,
        cost_estimate=cost(8 * rows * w_size, 2 * w_size + 16 * rows * width),
    )(info, *blocks, *hot_w)
    return near, far


def pack(tokens, expert_ids, gate_values):
    tok_dev, width = tokens.shape
    meta = jnp.concatenate([expert_ids.astype(jnp.bfloat16), gate_values.astype(jnp.bfloat16)], axis=1)
    meta = meta.T.reshape(1, -1)
    meta = jnp.pad(meta, ((0, 7), (0, width - meta.shape[1])))
    return jnp.concatenate([tokens, meta], axis=0)


def route_kernel(info, a_ref, b_ref, *refs):
    send_ref, mix_ref, hot_mix_ref = refs[-3:]
    zh, c = info[Z_HI], info[CORE]
    n_slot, n_tok = mix_ref.shape
    tok_dev = n_tok // 2
    span_rows = tok_dev // SPANS

    def entry(k):
        at = slice(k * tok_dev, (k + 1) * tok_dev)
        row = jnp.concatenate(
            [a_ref[tok_dev : tok_dev + 8, at], b_ref[tok_dev : tok_dev + 8, at]], axis=1
        )
        return row.astype(jnp.float32)[:1]

    row = iota((1, n_tok), 1)
    group = row // span_rows
    span = group % SPANS
    hot = sum(jnp.where(span == s, info[s], 0) for s in range(SPANS)).astype(jnp.float32)

    slot = pl.program_id(0) * n_slot + iota((n_slot, 1), 0)
    dest, local = slot // 32, slot // 16 % 2
    expert = ((dest // 4 * 2 + zh) * 4 + dest % 4) * 4 + c * 2 + local
    expert = expert.astype(jnp.float32)
    gate = jnp.zeros((n_slot, n_tok), jnp.float32)
    hits = jnp.zeros((n_slot, n_tok), jnp.float32)
    hot_gate = jnp.zeros((1, n_tok), jnp.float32)
    for k in range(TOP_K):
        ids, gates = entry(k), entry(TOP_K + k)
        same = expert == ids
        gate = jnp.where(same, gates, gate)
        hits = jnp.where(same, 1.0, hits)
        hot_gate += jnp.where(ids == hot, gates, 0.0)
    named = jnp.where(expert == hot, 0.0, hits)
    before, after = iota((n_tok, n_tok), 0), iota((n_tok, n_tok), 1)
    earlier = (before // span_rows == after // span_rows) & (before < after)
    earlier = jnp.where(earlier, 1.0, 0.0).astype(jnp.bfloat16)
    rank = dot(named.astype(jnp.bfloat16), earlier, 1, 0)
    at = (slot // CAPACITY % (2 * SPANS)) == group
    chosen = (named > 0.5) & at & (rank == (slot % CAPACITY).astype(jnp.float32))
    pick = jnp.where(chosen, 1.0, 0.0).astype(jnp.bfloat16)
    sent = dot(pick[:, :tok_dev], a_ref[:tok_dev], 1, 0)
    sent += dot(pick[:, tok_dev:], b_ref[:tok_dev], 1, 0)
    send_ref[...] = sent.astype(jnp.bfloat16).reshape(send_ref.shape)
    mix_ref[...] = jnp.where(chosen, gate, 0.0).astype(jnp.bfloat16)
    hot_row = iota((2 * span_rows, 1), 0)
    hot_row = hot_row // span_rows * tok_dev + (2 * zh + c) * span_rows + hot_row % span_rows
    hot_mix_ref[...] = jnp.where(hot_row == row, hot_gate, 0.0).astype(jnp.bfloat16)


def route(info, a, b, tok_dev, half, base=()):
    width = a.shape[1]
    n_slot = 32 * 2 * SPANS * CAPACITY
    n_dest = 16
    steps = 4
    span_rows = tok_dev // SPANS
    rows = n_slot // n_dest
    shapes = (
        jax.ShapeDtypeStruct((n_dest, 2 * rows, width), jnp.bfloat16),
        jax.ShapeDtypeStruct((n_slot, 2 * tok_dev), jnp.bfloat16),
        jax.ShapeDtypeStruct((2 * span_rows, 2 * tok_dev), jnp.bfloat16),
    )
    return pl.pallas_call(
        route_kernel,
        out_shape=shapes,
        grid_spec=pltpu.PrefetchScalarGridSpec(
            num_scalar_prefetch=1,
            grid=(steps,),
            in_specs=[whole(a.shape), whole(b.shape)]
            + [pl.BlockSpec(memory_space=pl.ANY)] * len(base),
            out_specs=(
                pl.BlockSpec((n_dest // steps, rows, width), lambda i, info: (i, half, 0)),
                pl.BlockSpec((n_slot // steps, 2 * tok_dev), lambda i, info: (i, 0)),
                whole(shapes[2].shape),
            ),
        ),
        input_output_aliases={3: 0} if base else {},
        compiler_params=PARAMS,
        cost_estimate=cost(4 * n_slot * tok_dev * width, 2 * width * (n_slot + 2 * tok_dev)),
    )(info, a, b, *base)


def ffn_kernel(info, x_ref, gate_ref, up_ref, down_ref, *out_refs):
    n_src, rows, width = x_ref.shape
    x = x_ref[...].reshape(n_src * rows, width)
    gate = dot(x, gate_ref[0], 1, 1)
    up = dot(x, up_ref[0], 1, 1)
    hidden = (jax.nn.silu(gate) * up).astype(jnp.bfloat16)
    if len(out_refs) == 1:
        out = dot(hidden, down_ref[0], 1, 0).astype(jnp.bfloat16)
        out_refs[0][...] = out.reshape(n_src, rows, width)
        return
    cols = width // len(out_refs)
    for i, out_ref in enumerate(out_refs):
        start = pl.multiple_of((info[TENSOR] ^ i) * cols, cols)
        out = dot(hidden, down_ref[0, :, pl.ds(start, cols)], 1, 0).astype(jnp.bfloat16)
        out_ref[...] = out.reshape(n_src, rows, cols)


def ffn(info, x, w_gate, w_up, w_down, half, groups):
    n_src, rows, width = x.shape
    exp_dev, units, _ = w_gate.shape
    rows //= 2
    cols = width // groups
    block = (n_src, rows // exp_dev)
    w_spec = pl.BlockSpec((1, units, width), lambda e, info: (e, 0, 0))
    return pl.pallas_call(
        ffn_kernel,
        out_shape=[jax.ShapeDtypeStruct((n_src, rows, cols), jnp.bfloat16)] * groups,
        grid_spec=pltpu.PrefetchScalarGridSpec(
            num_scalar_prefetch=1,
            grid=(exp_dev,),
            in_specs=[
                pl.BlockSpec((*block, width), lambda e, info: (0, half * exp_dev + e, 0)),
                w_spec,
                w_spec,
                w_spec,
            ],
            out_specs=[pl.BlockSpec((*block, cols), lambda e, info: (0, e, 0))] * groups,
        ),
        compiler_params=PARAMS,
        cost_estimate=cost(6 * n_src * rows * units * width, 2 * x.size + 6 * w_gate.size),
    )(info, x, w_gate, w_up, w_down)


def mix_kernel(info, mix_ref, hot_mix_ref, ret_ref, hot_ref, own_ref, other_ref):
    out = dot(mix_ref[...], ret_ref[...], 0, 0) + dot(hot_mix_ref[...], hot_ref[...], 0, 0)
    out = out.astype(jnp.bfloat16)
    half = out.shape[0] // 2
    own_ref[0] = out[:half]
    other_ref[0] = out[half:]


def mix_rows(info, mix, hot_mix, returned, hot):
    n_slot, n_tok = mix.shape
    width = returned.shape[1]
    n_group = lax.axis_size("t")
    cols = width // n_group
    shape = jax.ShapeDtypeStruct((n_group, n_tok // 2, cols), jnp.bfloat16)
    out = pl.BlockSpec((1, n_tok // 2, cols), lambda i, info: (i, 0, 0))
    return pl.pallas_call(
        mix_kernel,
        out_shape=(shape, shape),
        grid_spec=pltpu.PrefetchScalarGridSpec(
            num_scalar_prefetch=1,
            grid=(n_group,),
            in_specs=[
                whole(mix.shape),
                whole(hot_mix.shape),
                pl.BlockSpec((n_slot, cols), lambda i, info: (0, i ^ info[TENSOR])),
                pl.BlockSpec((hot.shape[0], cols), lambda i, info: (0, i ^ info[TENSOR])),
            ],
            out_specs=(out, out),
        ),
        compiler_params=PARAMS,
        cost_estimate=cost(2 * n_slot * n_tok * width, 2 * width * (n_slot + n_tok)),
    )(info, mix, hot_mix, returned, hot)


def mix_quarter_kernel(mix_ref, hot_mix_ref, ret_ref, hot_ref, own_ref, other_ref):
    out = dot(mix_ref[...], ret_ref[...], 0, 0) + dot(hot_mix_ref[...], hot_ref[...], 0, 0)
    half = out.shape[0] // 2
    own_ref[...] = out[:half]
    other_ref[...] = out[half:].astype(jnp.bfloat16)


def mix_quarter(mix, hot_mix, returned, hot):
    rows, cols = mix.shape[1] // 2, returned.shape[1]
    return pl.pallas_call(
        mix_quarter_kernel,
        out_shape=(
            jax.ShapeDtypeStruct((rows, cols), jnp.float32),
            jax.ShapeDtypeStruct((rows, cols), jnp.bfloat16),
        ),
        compiler_params=PARAMS,
        cost_estimate=cost(2 * mix.size * cols, 2 * (mix.size + returned.size)),
    )(mix, hot_mix, returned, hot)


def exchange(send):
    return lax.all_to_all(send, ("y", "x"), 0, 0, tiled=True)


def to_t(groups, *shifts):
    pairs = range(len(groups))
    return tuple(lax.ppermute(groups[k], "t", [(i, i ^ k) for i in pairs]) for k in shifts)


def total_of(parts):
    return sum(part.astype(jnp.float32) for part in parts).astype(jnp.bfloat16)


def per_device(tokens, expert_ids, gate_values, hot_ids, w_gate, w_up, w_down):
    y, zh, x, c, t = (lax.axis_index(name) for name in ("y", "zh", "x", "c", "t"))
    n_t = lax.axis_size("t")
    tok_dev, width = tokens.shape
    place = jnp.stack([(y * 2 + zh) * 4 + x, zh, c, t, 0]).astype(jnp.int32)
    info = jnp.concatenate([hot_ids, place])
    experts = (w_gate, w_up, w_down)

    own = pack(tokens, expert_ids, gate_values)
    own_z = lax.ppermute(own, "zh", SWAP)
    own_c = lax.ppermute(own, "c", SWAP)
    rows, near_mix, near_hot_mix = route(info, own, own_c, tok_dev, 0)
    n_slot = near_mix.shape[0]

    chunks = first_chunks(info, hot_ids, experts)
    own_zc = lax.ppermute(own_z, "c", SWAP)
    rows, far_mix, far_hot_mix = route(info, own_z, own_zc, tok_dev, 1, (rows,))
    rows, chunks = lax.optimization_barrier((rows, chunks))
    rows = exchange(rows)
    hot_w = along_y(own_span(info, chunks, c))
    rows, hot_w = lax.optimization_barrier((rows, hot_w))
    (near,) = ffn(info, rows, *experts, 0, 1)
    near, rows = lax.optimization_barrier((near, rows))
    near = exchange(near)
    far = ffn(info, rows, *experts, 1, n_t)
    far, hot_w = lax.optimization_barrier((tuple(far), hot_w))
    hot_w = (hot_w, shift_x(hot_w, 1), shift_x(hot_w, -1))
    summands = (far[0], *to_t(far, 1, 2))
    hot_w, summands = lax.optimization_barrier((hot_w, summands))
    half = hot_w[0].shape[0] // 2
    hot_w += (shift_x(hot_w[1][:half], 1), shift_x(hot_w[2][half:], -1))
    far = total_of(summands + to_t(far, 3))
    near_hot, far_hot = hot_ffn(info, (own_z, own_zc, own, own_c), hot_w, tok_dev // SPANS)
    mine, other = mix_rows(info, near_mix, near_hot_mix, near.reshape(n_slot, width), near_hot)
    got = lax.ppermute(other, "c", SWAP)
    mine, got, far, far_hot = lax.optimization_barrier((mine, got, far, far_hot))

    far = exchange(far).reshape(n_slot, width // n_t)
    pieces = [mine[k].astype(jnp.float32) + got[k].astype(jnp.float32) for k in range(n_t)]
    parts = to_t(
        [jnp.concatenate([p.astype(jnp.bfloat16), h]) for p, h in zip(pieces, far_hot)], 1, 2, 3
    )
    total = pieces[0] + sum(part[:tok_dev].astype(jnp.float32) for part in parts)
    far_hot = total_of((far_hot[0], *(part[tok_dev:] for part in parts)))
    far, total = lax.optimization_barrier((far, total))
    mine, other = mix_quarter(far_mix, far_hot_mix, far, far_hot)
    mine += lax.ppermute(other, "c", SWAP).astype(jnp.float32)
    got = lax.ppermute(mine.astype(jnp.bfloat16), "zh", SWAP)
    return (total + got.astype(jnp.float32)).astype(jnp.bfloat16)


def solution(mesh):
    fine = Mesh(mesh.devices.reshape(4, 2, 4, 2, 4), ("y", "zh", "x", "c", "t"))
    owner = ("y", "zh", "x", "c")
    in_specs = (
        P(owner, None),
        P(owner, None),
        P(owner, None),
        P(),
        P(owner, "t", None),
        P(owner, "t", None),
        P(owner, "t", None),
    )
    return jax.shard_map(
        per_device, mesh=fine, in_specs=in_specs, out_specs=P(owner, "t"), check_vma=False
    )
```

```python
import jax
import jax.numpy as jnp
from jax import lax
from jax.experimental import pallas as pl
from jax.experimental.pallas import tpu as pltpu
from jax.sharding import Mesh, PartitionSpec as P

SPANS = 4
CAPACITY = 2
TOP_K = 8
SWAP = ((0, 1), (1, 0))
VMEM_LIMIT = 32 * 1024 * 1024


def dot(a, b, contract_a, contract_b):
    dims = (((contract_a,), (contract_b,)), ((), ()))
    return lax.dot_general(a, b, dims, preferred_element_type=jnp.float32)


def iota(shape, dim):
    return lax.broadcasted_iota(jnp.int32, shape, dim)


def cost(flops, moved):
    return pl.CostEstimate(flops=flops, bytes_accessed=moved, transcendentals=0)


PARAMS = pltpu.CompilerParams(vmem_limit_bytes=VMEM_LIMIT)


def whole(shape):
    return pl.BlockSpec(shape, lambda *_: (0,) * len(shape))


CHIP, Z_HI, CORE, TENSOR, TURN = 4, 5, 6, 7, 8


def chip_of(expert):
    return expert >> 2


def order_of(info, span):
    chip = chip_of(info[span])
    return sum(((chip_of(info[s]) == chip) & (s < span)).astype(jnp.int32) for s in range(SPANS))


def my_turn(info):
    return sum(
        jnp.where((chip_of(info[s]) == info[CHIP]) & (order_of(info, s) == info[TURN]), info[s], 0)
        for s in range(SPANS)
    )


def chunk_kernel(info, gate_ref, up_ref, down_ref, keep_ref, give_ref):
    units = gate_ref.shape[1]
    mid = units // 2
    n_chunk, _, lane = keep_ref.shape

    def first(out):
        for n in range(n_chunk):
            at = slice(n * lane, (n + 1) * lane)
            out[n, :units] = gate_ref[0, :, at]
            out[n, units:] = up_ref[0, :mid, at]

    def second(out):
        for n in range(n_chunk):
            at = slice(n * lane, (n + 1) * lane)
            out[n, :mid] = up_ref[0, mid:, at]
            out[n, mid:] = down_ref[0, :, at]

    @pl.when(info[CORE] == 0)
    def _():
        first(keep_ref)
        second(give_ref)

    @pl.when(info[CORE] == 1)
    def _():
        second(keep_ref)
        first(give_ref)


def cut_chunks(info, held):
    _, units, width = held[0].shape
    steps = 4
    half, lane = 3 * units // 2, width // 16
    spec = pl.BlockSpec((1, units, width // steps), lambda n, info: (my_turn(info) & 1, 0, n))
    out = pl.BlockSpec((16 // steps, half, lane), lambda n, info: (n, 0, 0))
    shape = jax.ShapeDtypeStruct((16, half, lane), jnp.bfloat16)
    return pl.pallas_call(
        chunk_kernel,
        out_shape=(shape, shape),
        grid_spec=pltpu.PrefetchScalarGridSpec(
            num_scalar_prefetch=1, grid=(steps,), in_specs=[spec] * 3, out_specs=(out, out)
        ),
        compiler_params=PARAMS,
        cost_estimate=cost(0, 4 * 3 * units * width),
    )(info, *held)


def choose_kernel(info, keep_ref, got_ref, out_ref):
    held_here = ((my_turn(info) >> 1) & 1) == info[CORE]

    @pl.when(held_here)
    def _():
        out_ref[...] = keep_ref[...]

    @pl.when(jnp.logical_not(held_here))
    def _():
        out_ref[...] = got_ref[...]


def choose(info, keep, got):
    return pl.pallas_call(
        choose_kernel,
        out_shape=jax.ShapeDtypeStruct(keep.shape, keep.dtype),
        grid_spec=pltpu.PrefetchScalarGridSpec(
            num_scalar_prefetch=1,
            grid=(1,),
            in_specs=[whole(keep.shape)] * 2,
            out_specs=whole(keep.shape),
        ),
        compiler_params=PARAMS,
        cost_estimate=cost(0, 6 * keep.size),
    )(info, keep, got)


def span_at(info, i):
    return (2 * info[Z_HI] + info[CORE]) ^ i


def take_kernel(info, part_ref, *refs):
    *old_refs, out_ref = refs
    span = span_at(info, pl.program_id(0))
    expert = info[span]
    here = (((expert >> 4) & 1) == info[Z_HI]) & (order_of(info, span) == info[TURN])
    if old_refs:
        out_ref[...] = jnp.where(here, part_ref[...], old_refs[0][...])
    else:
        out_ref[...] = part_ref[...]


def take(info, part, *old):
    block = (1, *part.shape[1:])

    def source(i, info):
        expert = info[span_at(info, i)]
        return ((expert >> 5) * 4 + ((expert >> 2) & 3), 0, 0)

    def same(i, info):
        return (i, 0, 0)

    return pl.pallas_call(
        take_kernel,
        out_shape=jax.ShapeDtypeStruct((SPANS, *part.shape[1:]), part.dtype),
        grid_spec=pltpu.PrefetchScalarGridSpec(
            num_scalar_prefetch=1,
            grid=(SPANS,),
            in_specs=[pl.BlockSpec(block, source)] + [pl.BlockSpec(block, same)] * len(old),
            out_specs=pl.BlockSpec(block, same),
        ),
        compiler_params=PARAMS,
        cost_estimate=cost(0, 16 * block[1] * block[2]),
    )(info, part, *old)


def hot_round(info, held, *old):
    keep, give = cut_chunks(info, held)
    part = choose(info, keep, lax.ppermute(give, "c", SWAP))
    part = lax.all_to_all(part, ("y", "x"), 0, 0, tiled=True)
    return take(info, part, *old)


def pair_kernel(info, chunk_ref, got_ref, mine_ref, give_ref):
    for i, out_ref in enumerate((mine_ref, give_ref)):
        here = ((info[span_at(info, i)] >> 4) & 1) == info[Z_HI]
        out_ref[...] = jnp.where(here, chunk_ref[i], got_ref[i])


def pair(info, chunks, got):
    shape = jax.ShapeDtypeStruct(chunks.shape[1:], chunks.dtype)
    return pl.pallas_call(
        pair_kernel,
        out_shape=(shape, shape),
        grid_spec=pltpu.PrefetchScalarGridSpec(
            num_scalar_prefetch=1,
            grid=(1,),
            in_specs=[whole(got.shape)] * 2,
            out_specs=(whole(shape.shape), whole(shape.shape)),
        ),
        compiler_params=PARAMS,
        cost_estimate=cost(0, 12 * shape.size),
    )(info, chunks, got)


def first_chunks(info, hot_ids, held):
    chips = chip_of(hot_ids)
    before = jnp.arange(SPANS)[None, :] < jnp.arange(SPANS)[:, None]
    turns = 1 + jnp.max(jnp.sum((chips[:, None] == chips[None, :]) & before, axis=1))
    chunks = hot_round(info, held)
    return lax.fori_loop(
        1, turns, lambda turn, old: hot_round(info.at[TURN].set(turn), held, old), chunks
    )


def own_span(info, chunks, c):
    got = lax.ppermute(chunks[2:], "zh", SWAP)
    mine, give = pair(info, chunks, got)
    got = lax.ppermute(give, "c", SWAP)
    first, second = jnp.where(c == 0, mine, got), jnp.where(c == 0, got, mine)
    return jnp.concatenate([first, second], axis=0)


def along_y(chunk):
    n_y = lax.axis_size("y")
    column = [chunk]
    for k in range(1, n_y):
        column.append(lax.ppermute(chunk, "y", [(i, i ^ k) for i in range(n_y)]))
    return jnp.stack(column)


def shift_x(array, step):
    n_x = lax.axis_size("x")
    return lax.ppermute(array, "x", [(i, (i + step) % n_x) for i in range(n_x)])


def hot_kernel(info, *refs):
    *refs, near_ref, far_rows = refs
    tok_refs, w_refs, far_refs = refs[:4], refs[4:9], refs[9:]
    n_y, rows, lane = w_refs[0].shape
    units = rows // 3
    half = near_ref.shape[0]
    cols = far_refs[0].shape[1]
    pieces = [(0, i, w_refs[0], i) for i in range(n_y)]
    pieces += [(3, i, w_refs[1], i) for i in range(n_y)]
    pieces += [(1, i, w_refs[2], i) for i in range(n_y)]
    pieces += [(2, i, w_refs[3 + i // 2], i % 2) for i in range(n_y)]

    def columns(far, i):
        start = ((info[CHIP] >> 3 ^ i) * 4 + ((info[CHIP] + far) & 3)) * lane
        return pl.ds(pl.multiple_of(start, lane), lane)

    proj = jnp.zeros((2 * half, 2 * units), jnp.float32)
    for far, i, w_ref, at in pieces:
        tok = jnp.concatenate([r[:, columns(far, i)] for r in tok_refs], axis=0)
        proj += dot(tok, w_ref[at, : 2 * units], 1, 1)
    hidden = (jax.nn.silu(proj[:, :units]) * proj[:, units:]).astype(jnp.bfloat16)
    for far, i, w_ref, at in pieces:
        out = dot(hidden, w_ref[at, 2 * units :], 1, 0).astype(jnp.bfloat16)
        far_rows[:, columns(far, i)] = out[:half]
        near_ref[:, columns(far, i)] = out[half:]
    for i, far_ref in enumerate(far_refs):
        start = pl.multiple_of((info[TENSOR] ^ i) * cols, cols)
        far_ref[...] = far_rows[:, pl.ds(start, cols)]


def hot_ffn(info, blocks, hot_w, rows):
    width = blocks[0].shape[1]
    w_size = sum(w.size for w in hot_w)
    spec = pl.BlockSpec((rows, width), lambda i, info: (span_at(info, 0), 0))
    n_t = lax.axis_size("t")
    shapes = [jax.ShapeDtypeStruct((2 * rows, width // n_t), jnp.bfloat16)] * n_t
    shapes.append(jax.ShapeDtypeStruct((2 * rows, width), jnp.bfloat16))
    *far, near = pl.pallas_call(
        hot_kernel,
        out_shape=shapes,
        grid_spec=pltpu.PrefetchScalarGridSpec(
            num_scalar_prefetch=1,
            grid=(1,),
            in_specs=[spec] * 4 + [whole(w.shape) for w in hot_w],
            out_specs=[whole(shape.shape) for shape in shapes],
            scratch_shapes=[pltpu.VMEM((2 * rows, width), jnp.bfloat16)],
        ),
        compiler_params=PARAMS,
        cost_estimate=cost(8 * rows * w_size, 2 * w_size + 16 * rows * width),
    )(info, *blocks, *hot_w)
    return near, far


def pack(tokens, expert_ids, gate_values):
    tok_dev, width = tokens.shape
    meta = jnp.concatenate([expert_ids.astype(jnp.bfloat16), gate_values.astype(jnp.bfloat16)], axis=1)
    meta = meta.T.reshape(1, -1)
    meta = jnp.pad(meta, ((0, 7), (0, width - meta.shape[1])))
    return jnp.concatenate([tokens, meta], axis=0)


def route_kernel(info, a_ref, b_ref, *refs):
    send_ref, mix_ref, hot_mix_ref = refs[-3:]
    zh, c = info[Z_HI], info[CORE]
    n_slot, n_tok = mix_ref.shape
    tok_dev = n_tok // 2
    span_rows = tok_dev // SPANS

    def entry(k):
        at = slice(k * tok_dev, (k + 1) * tok_dev)
        row = jnp.concatenate(
            [a_ref[tok_dev : tok_dev + 8, at], b_ref[tok_dev : tok_dev + 8, at]], axis=1
        )
        return row.astype(jnp.float32)[:1]

    row = iota((1, n_tok), 1)
    group = row // span_rows
    span = group % SPANS
    hot = sum(jnp.where(span == s, info[s], 0) for s in range(SPANS)).astype(jnp.float32)

    slot = pl.program_id(0) * n_slot + iota((n_slot, 1), 0)
    dest, local = slot // 32, slot // 16 % 2
    expert = ((dest // 4 * 2 + zh) * 4 + dest % 4) * 4 + c * 2 + local
    expert = expert.astype(jnp.float32)
    gate = jnp.zeros((n_slot, n_tok), jnp.float32)
    hits = jnp.zeros((n_slot, n_tok), jnp.float32)
    hot_gate = jnp.zeros((1, n_tok), jnp.float32)
    for k in range(TOP_K):
        ids, gates = entry(k), entry(TOP_K + k)
        same = expert == ids
        gate = jnp.where(same, gates, gate)
        hits = jnp.where(same, 1.0, hits)
        hot_gate += jnp.where(ids == hot, gates, 0.0)
    named = jnp.where(expert == hot, 0.0, hits)
    before, after = iota((n_tok, n_tok), 0), iota((n_tok, n_tok), 1)
    earlier = (before // span_rows == after // span_rows) & (before < after)
    earlier = jnp.where(earlier, 1.0, 0.0).astype(jnp.bfloat16)
    rank = dot(named.astype(jnp.bfloat16), earlier, 1, 0)
    at = (slot // CAPACITY % (2 * SPANS)) == group
    chosen = (named > 0.5) & at & (rank == (slot % CAPACITY).astype(jnp.float32))
    pick = jnp.where(chosen, 1.0, 0.0).astype(jnp.bfloat16)
    sent = dot(pick[:, :tok_dev], a_ref[:tok_dev], 1, 0)
    sent += dot(pick[:, tok_dev:], b_ref[:tok_dev], 1, 0)
    send_ref[...] = sent.astype(jnp.bfloat16).reshape(send_ref.shape)
    mix_ref[...] = jnp.where(chosen, gate, 0.0).astype(jnp.bfloat16)
    hot_row = iota((2 * span_rows, 1), 0)
    hot_row = hot_row // span_rows * tok_dev + (2 * zh + c) * span_rows + hot_row % span_rows
    hot_mix_ref[...] = jnp.where(hot_row == row, hot_gate, 0.0).astype(jnp.bfloat16)


def route(info, a, b, tok_dev, half, base=()):
    width = a.shape[1]
    n_slot = 32 * 2 * SPANS * CAPACITY
    n_dest = 16
    steps = 4
    span_rows = tok_dev // SPANS
    rows = n_slot // n_dest
    shapes = (
        jax.ShapeDtypeStruct((n_dest, 2 * rows, width), jnp.bfloat16),
        jax.ShapeDtypeStruct((n_slot, 2 * tok_dev), jnp.bfloat16),
        jax.ShapeDtypeStruct((2 * span_rows, 2 * tok_dev), jnp.bfloat16),
    )
    return pl.pallas_call(
        route_kernel,
        out_shape=shapes,
        grid_spec=pltpu.PrefetchScalarGridSpec(
            num_scalar_prefetch=1,
            grid=(steps,),
            in_specs=[whole(a.shape), whole(b.shape)]
            + [pl.BlockSpec(memory_space=pl.ANY)] * len(base),
            out_specs=(
                pl.BlockSpec((n_dest // steps, rows, width), lambda i, info: (i, half, 0)),
                pl.BlockSpec((n_slot // steps, 2 * tok_dev), lambda i, info: (i, 0)),
                whole(shapes[2].shape),
            ),
        ),
        input_output_aliases={3: 0} if base else {},
        compiler_params=PARAMS,
        cost_estimate=cost(4 * n_slot * tok_dev * width, 2 * width * (n_slot + 2 * tok_dev)),
    )(info, a, b, *base)


def ffn_kernel(info, x_ref, gate_ref, up_ref, down_ref, *out_refs):
    n_src, rows, width = x_ref.shape
    x = x_ref[...].reshape(n_src * rows, width)
    gate = dot(x, gate_ref[0], 1, 1)
    up = dot(x, up_ref[0], 1, 1)
    hidden = (jax.nn.silu(gate) * up).astype(jnp.bfloat16)
    if len(out_refs) == 1:
        out = dot(hidden, down_ref[0], 1, 0).astype(jnp.bfloat16)
        out_refs[0][...] = out.reshape(n_src, rows, width)
        return
    cols = width // len(out_refs)
    for i, out_ref in enumerate(out_refs):
        start = pl.multiple_of((info[TENSOR] ^ i) * cols, cols)
        out = dot(hidden, down_ref[0, :, pl.ds(start, cols)], 1, 0).astype(jnp.bfloat16)
        out_ref[...] = out.reshape(n_src, rows, cols)


def ffn(info, x, w_gate, w_up, w_down, half, groups):
    n_src, rows, width = x.shape
    exp_dev, units, _ = w_gate.shape
    rows //= 2
    cols = width // groups
    block = (n_src, rows // exp_dev)
    w_spec = pl.BlockSpec((1, units, width), lambda e, info: (e, 0, 0))
    return pl.pallas_call(
        ffn_kernel,
        out_shape=[jax.ShapeDtypeStruct((n_src, rows, cols), jnp.bfloat16)] * groups,
        grid_spec=pltpu.PrefetchScalarGridSpec(
            num_scalar_prefetch=1,
            grid=(exp_dev,),
            in_specs=[
                pl.BlockSpec((*block, width), lambda e, info: (0, half * exp_dev + e, 0)),
                w_spec,
                w_spec,
                w_spec,
            ],
            out_specs=[pl.BlockSpec((*block, cols), lambda e, info: (0, e, 0))] * groups,
        ),
        compiler_params=PARAMS,
        cost_estimate=cost(6 * n_src * rows * units * width, 2 * x.size + 6 * w_gate.size),
    )(info, x, w_gate, w_up, w_down)


def mix_kernel(info, mix_ref, hot_mix_ref, ret_ref, hot_ref, own_ref, other_ref):
    out = dot(mix_ref[...], ret_ref[...], 0, 0) + dot(hot_mix_ref[...], hot_ref[...], 0, 0)
    out = out.astype(jnp.bfloat16)
    half = out.shape[0] // 2
    own_ref[0] = out[:half]
    other_ref[0] = out[half:]


def mix_rows(info, mix, hot_mix, returned, hot):
    n_slot, n_tok = mix.shape
    width = returned.shape[1]
    n_group = lax.axis_size("t")
    cols = width // n_group
    shape = jax.ShapeDtypeStruct((n_group, n_tok // 2, cols), jnp.bfloat16)
    out = pl.BlockSpec((1, n_tok // 2, cols), lambda i, info: (i, 0, 0))
    return pl.pallas_call(
        mix_kernel,
        out_shape=(shape, shape),
        grid_spec=pltpu.PrefetchScalarGridSpec(
            num_scalar_prefetch=1,
            grid=(n_group,),
            in_specs=[
                whole(mix.shape),
                whole(hot_mix.shape),
                pl.BlockSpec((n_slot, cols), lambda i, info: (0, i ^ info[TENSOR])),
                pl.BlockSpec((hot.shape[0], cols), lambda i, info: (0, i ^ info[TENSOR])),
            ],
            out_specs=(out, out),
        ),
        compiler_params=PARAMS,
        cost_estimate=cost(2 * n_slot * n_tok * width, 2 * width * (n_slot + n_tok)),
    )(info, mix, hot_mix, returned, hot)


def mix_quarter_kernel(mix_ref, hot_mix_ref, ret_ref, hot_ref, own_ref, other_ref):
    out = dot(mix_ref[...], ret_ref[...], 0, 0) + dot(hot_mix_ref[...], hot_ref[...], 0, 0)
    half = out.shape[0] // 2
    own_ref[...] = out[:half]
    other_ref[...] = out[half:].astype(jnp.bfloat16)


def mix_quarter(mix, hot_mix, returned, hot):
    rows, cols = mix.shape[1] // 2, returned.shape[1]
    return pl.pallas_call(
        mix_quarter_kernel,
        out_shape=(
            jax.ShapeDtypeStruct((rows, cols), jnp.float32),
            jax.ShapeDtypeStruct((rows, cols), jnp.bfloat16),
        ),
        compiler_params=PARAMS,
        cost_estimate=cost(2 * mix.size * cols, 2 * (mix.size + returned.size)),
    )(mix, hot_mix, returned, hot)


def exchange(send):
    return lax.all_to_all(send, ("y", "x"), 0, 0, tiled=True)


def to_t(groups, *shifts):
    pairs = range(len(groups))
    return tuple(lax.ppermute(groups[k], "t", [(i, i ^ k) for i in pairs]) for k in shifts)


def total_of(parts):
    return sum(part.astype(jnp.float32) for part in parts).astype(jnp.bfloat16)


def per_device(tokens, expert_ids, gate_values, hot_ids, w_gate, w_up, w_down):
    y, zh, x, c, t = (lax.axis_index(name) for name in ("y", "zh", "x", "c", "t"))
    n_t = lax.axis_size("t")
    tok_dev, width = tokens.shape
    place = jnp.stack([(y * 2 + zh) * 4 + x, zh, c, t, 0]).astype(jnp.int32)
    info = jnp.concatenate([hot_ids, place])
    experts = (w_gate, w_up, w_down)

    own = pack(tokens, expert_ids, gate_values)
    own_z = lax.ppermute(own, "zh", SWAP)
    own_c = lax.ppermute(own, "c", SWAP)
    rows, near_mix, near_hot_mix = route(info, own, own_c, tok_dev, 0)
    n_slot = near_mix.shape[0]

    chunks = first_chunks(info, hot_ids, experts)
    own_zc = lax.ppermute(own_z, "c", SWAP)
    rows, far_mix, far_hot_mix = route(info, own_z, own_zc, tok_dev, 1, (rows,))
    rows, chunks = lax.optimization_barrier((rows, chunks))
    rows = exchange(rows)
    hot_w = along_y(own_span(info, chunks, c))
    rows, hot_w = lax.optimization_barrier((rows, hot_w))
    hot_w = (hot_w, shift_x(hot_w, 1), shift_x(hot_w, -1))
    far = ffn(info, rows, *experts, 1, n_t)
    far, rows = lax.optimization_barrier((tuple(far), rows))
    (near,) = ffn(info, rows, *experts, 0, 1)
    near, hot_w = lax.optimization_barrier((near, hot_w))
    near = exchange(near)
    half = hot_w[0].shape[0] // 2
    hot_w += (shift_x(hot_w[1][:half], 1), shift_x(hot_w[2][half:], -1))
    far = total_of((far[0], *to_t(far, 1, 2, 3)))
    near_hot, far_hot = hot_ffn(info, (own_z, own_zc, own, own_c), hot_w, tok_dev // SPANS)
    mine, other = mix_rows(info, near_mix, near_hot_mix, near.reshape(n_slot, width), near_hot)
    got = lax.ppermute(other, "c", SWAP)
    mine, got, far, far_hot = lax.optimization_barrier((mine, got, far, far_hot))

    far = exchange(far).reshape(n_slot, width // n_t)
    pieces = [mine[k].astype(jnp.float32) + got[k].astype(jnp.float32) for k in range(n_t)]
    parts = to_t(
        [jnp.concatenate([p.astype(jnp.bfloat16), h]) for p, h in zip(pieces, far_hot)], 1, 2, 3
    )
    total = pieces[0] + sum(part[:tok_dev].astype(jnp.float32) for part in parts)
    far_hot = total_of((far_hot[0], *(part[tok_dev:] for part in parts)))
    far, total = lax.optimization_barrier((far, total))
    mine, other = mix_quarter(far_mix, far_hot_mix, far, far_hot)
    mine += lax.ppermute(other, "c", SWAP).astype(jnp.float32)
    got = lax.ppermute(mine.astype(jnp.bfloat16), "zh", SWAP)
    return (total + got.astype(jnp.float32)).astype(jnp.bfloat16)


def solution(mesh):
    fine = Mesh(mesh.devices.reshape(4, 2, 4, 2, 4), ("y", "zh", "x", "c", "t"))
    owner = ("y", "zh", "x", "c")
    in_specs = (
        P(owner, None),
        P(owner, None),
        P(owner, None),
        P(),
        P(owner, "t", None),
        P(owner, "t", None),
        P(owner, "t", None),
    )
    return jax.shard_map(
        per_device, mesh=fine, in_specs=in_specs, out_specs=P(owner, "t"), check_vma=False
    )
```

```python
import jax
import jax.numpy as jnp
from jax import lax
from jax.experimental import pallas as pl
from jax.experimental.pallas import tpu as pltpu
from jax.sharding import Mesh, PartitionSpec as P

SPANS = 4
CAPACITY = 2
TOP_K = 8
SWAP = ((0, 1), (1, 0))
VMEM_LIMIT = 32 * 1024 * 1024


def dot(a, b, contract_a, contract_b):
    dims = (((contract_a,), (contract_b,)), ((), ()))
    return lax.dot_general(a, b, dims, preferred_element_type=jnp.float32)


def iota(shape, dim):
    return lax.broadcasted_iota(jnp.int32, shape, dim)


def cost(flops, moved):
    return pl.CostEstimate(flops=flops, bytes_accessed=moved, transcendentals=0)


PARAMS = pltpu.CompilerParams(vmem_limit_bytes=VMEM_LIMIT)


def whole(shape):
    return pl.BlockSpec(shape, lambda *_: (0,) * len(shape))


CHIP, Z_HI, CORE, TENSOR, TURN = 4, 5, 6, 7, 8


def chip_of(expert):
    return expert >> 2


def order_of(info, span):
    chip = chip_of(info[span])
    return sum(((chip_of(info[s]) == chip) & (s < span)).astype(jnp.int32) for s in range(SPANS))


def my_turn(info):
    return sum(
        jnp.where((chip_of(info[s]) == info[CHIP]) & (order_of(info, s) == info[TURN]), info[s], 0)
        for s in range(SPANS)
    )


def chunk_kernel(info, gate_ref, up_ref, down_ref, keep_ref, give_ref):
    units = gate_ref.shape[1]
    mid = units // 2
    n_chunk, _, lane = keep_ref.shape

    def first(out):
        for n in range(n_chunk):
            at = slice(n * lane, (n + 1) * lane)
            out[n, :units] = gate_ref[0, :, at]
            out[n, units:] = up_ref[0, :mid, at]

    def second(out):
        for n in range(n_chunk):
            at = slice(n * lane, (n + 1) * lane)
            out[n, :mid] = up_ref[0, mid:, at]
            out[n, mid:] = down_ref[0, :, at]

    @pl.when(info[CORE] == 0)
    def _():
        first(keep_ref)
        second(give_ref)

    @pl.when(info[CORE] == 1)
    def _():
        second(keep_ref)
        first(give_ref)


def cut_chunks(info, held):
    _, units, width = held[0].shape
    steps = 4
    half, lane = 3 * units // 2, width // 16
    spec = pl.BlockSpec((1, units, width // steps), lambda n, info: (my_turn(info) & 1, 0, n))
    out = pl.BlockSpec((16 // steps, half, lane), lambda n, info: (n, 0, 0))
    shape = jax.ShapeDtypeStruct((16, half, lane), jnp.bfloat16)
    return pl.pallas_call(
        chunk_kernel,
        out_shape=(shape, shape),
        grid_spec=pltpu.PrefetchScalarGridSpec(
            num_scalar_prefetch=1, grid=(steps,), in_specs=[spec] * 3, out_specs=(out, out)
        ),
        compiler_params=PARAMS,
        cost_estimate=cost(0, 4 * 3 * units * width),
    )(info, *held)


def choose_kernel(info, keep_ref, got_ref, out_ref):
    held_here = ((my_turn(info) >> 1) & 1) == info[CORE]

    @pl.when(held_here)
    def _():
        out_ref[...] = keep_ref[...]

    @pl.when(jnp.logical_not(held_here))
    def _():
        out_ref[...] = got_ref[...]


def choose(info, keep, got):
    return pl.pallas_call(
        choose_kernel,
        out_shape=jax.ShapeDtypeStruct(keep.shape, keep.dtype),
        grid_spec=pltpu.PrefetchScalarGridSpec(
            num_scalar_prefetch=1,
            grid=(1,),
            in_specs=[whole(keep.shape)] * 2,
            out_specs=whole(keep.shape),
        ),
        compiler_params=PARAMS,
        cost_estimate=cost(0, 6 * keep.size),
    )(info, keep, got)


def span_at(info, i):
    return (2 * info[Z_HI] + info[CORE]) ^ i


def take_kernel(info, part_ref, *refs):
    *old_refs, out_ref = refs
    span = span_at(info, pl.program_id(0))
    expert = info[span]
    here = (((expert >> 4) & 1) == info[Z_HI]) & (order_of(info, span) == info[TURN])
    if old_refs:
        out_ref[...] = jnp.where(here, part_ref[...], old_refs[0][...])
    else:
        out_ref[...] = part_ref[...]


def take(info, part, *old):
    block = (1, *part.shape[1:])

    def source(i, info):
        expert = info[span_at(info, i)]
        return ((expert >> 5) * 4 + ((expert >> 2) & 3), 0, 0)

    def same(i, info):
        return (i, 0, 0)

    return pl.pallas_call(
        take_kernel,
        out_shape=jax.ShapeDtypeStruct((SPANS, *part.shape[1:]), part.dtype),
        grid_spec=pltpu.PrefetchScalarGridSpec(
            num_scalar_prefetch=1,
            grid=(SPANS,),
            in_specs=[pl.BlockSpec(block, source)] + [pl.BlockSpec(block, same)] * len(old),
            out_specs=pl.BlockSpec(block, same),
        ),
        compiler_params=PARAMS,
        cost_estimate=cost(0, 16 * block[1] * block[2]),
    )(info, part, *old)


def hot_round(info, held, *old):
    keep, give = cut_chunks(info, held)
    part = choose(info, keep, lax.ppermute(give, "c", SWAP))
    part = lax.all_to_all(part, ("y", "x"), 0, 0, tiled=True)
    return take(info, part, *old)


def pair_kernel(info, chunk_ref, got_ref, mine_ref, give_ref):
    for i, out_ref in enumerate((mine_ref, give_ref)):
        here = ((info[span_at(info, i)] >> 4) & 1) == info[Z_HI]
        out_ref[...] = jnp.where(here, chunk_ref[i], got_ref[i])


def pair(info, chunks, got):
    shape = jax.ShapeDtypeStruct(chunks.shape[1:], chunks.dtype)
    return pl.pallas_call(
        pair_kernel,
        out_shape=(shape, shape),
        grid_spec=pltpu.PrefetchScalarGridSpec(
            num_scalar_prefetch=1,
            grid=(1,),
            in_specs=[whole(got.shape)] * 2,
            out_specs=(whole(shape.shape), whole(shape.shape)),
        ),
        compiler_params=PARAMS,
        cost_estimate=cost(0, 12 * shape.size),
    )(info, chunks, got)


def first_chunks(info, hot_ids, held):
    chips = chip_of(hot_ids)
    before = jnp.arange(SPANS)[None, :] < jnp.arange(SPANS)[:, None]
    turns = 1 + jnp.max(jnp.sum((chips[:, None] == chips[None, :]) & before, axis=1))
    chunks = hot_round(info, held)
    return lax.fori_loop(
        1, turns, lambda turn, old: hot_round(info.at[TURN].set(turn), held, old), chunks
    )


def own_span(info, chunks, c):
    got = lax.ppermute(chunks[2:], "zh", SWAP)
    mine, give = pair(info, chunks, got)
    got = lax.ppermute(give, "c", SWAP)
    first, second = jnp.where(c == 0, mine, got), jnp.where(c == 0, got, mine)
    return jnp.concatenate([first, second], axis=0)


def along_y(chunk):
    n_y = lax.axis_size("y")
    column = [chunk]
    for k in range(1, n_y):
        column.append(lax.ppermute(chunk, "y", [(i, i ^ k) for i in range(n_y)]))
    return jnp.stack(column)


def shift_x(array, step):
    n_x = lax.axis_size("x")
    return lax.ppermute(array, "x", [(i, (i + step) % n_x) for i in range(n_x)])


def hot_kernel(info, *refs):
    *refs, near_ref, far_rows = refs
    tok_refs, w_refs, far_refs = refs[:4], refs[4:9], refs[9:]
    n_y, rows, lane = w_refs[0].shape
    units = rows // 3
    half = near_ref.shape[0]
    cols = far_refs[0].shape[1]
    pieces = [(0, i, w_refs[0], i) for i in range(n_y)]
    pieces += [(3, i, w_refs[1], i) for i in range(n_y)]
    pieces += [(1, i, w_refs[2], i) for i in range(n_y)]
    pieces += [(2, i, w_refs[3 + i // 2], i % 2) for i in range(n_y)]

    def columns(far, i):
        start = ((info[CHIP] >> 3 ^ i) * 4 + ((info[CHIP] + far) & 3)) * lane
        return pl.ds(pl.multiple_of(start, lane), lane)

    proj = jnp.zeros((2 * half, 2 * units), jnp.float32)
    for far, i, w_ref, at in pieces:
        tok = jnp.concatenate([r[:, columns(far, i)] for r in tok_refs], axis=0)
        proj += dot(tok, w_ref[at, : 2 * units], 1, 1)
    hidden = (jax.nn.silu(proj[:, :units]) * proj[:, units:]).astype(jnp.bfloat16)
    for far, i, w_ref, at in pieces:
        out = dot(hidden, w_ref[at, 2 * units :], 1, 0).astype(jnp.bfloat16)
        far_rows[:, columns(far, i)] = out[:half]
        near_ref[:, columns(far, i)] = out[half:]
    for i, far_ref in enumerate(far_refs):
        start = pl.multiple_of((info[TENSOR] ^ i) * cols, cols)
        far_ref[...] = far_rows[:, pl.ds(start, cols)]


def hot_ffn(info, blocks, hot_w, rows):
    width = blocks[0].shape[1]
    w_size = sum(w.size for w in hot_w)
    spec = pl.BlockSpec((rows, width), lambda i, info: (span_at(info, 0), 0))
    n_t = lax.axis_size("t")
    shapes = [jax.ShapeDtypeStruct((2 * rows, width // n_t), jnp.bfloat16)] * n_t
    shapes.append(jax.ShapeDtypeStruct((2 * rows, width), jnp.bfloat16))
    *far, near = pl.pallas_call(
        hot_kernel,
        out_shape=shapes,
        grid_spec=pltpu.PrefetchScalarGridSpec(
            num_scalar_prefetch=1,
            grid=(1,),
            in_specs=[spec] * 4 + [whole(w.shape) for w in hot_w],
            out_specs=[whole(shape.shape) for shape in shapes],
            scratch_shapes=[pltpu.VMEM((2 * rows, width), jnp.bfloat16)],
        ),
        compiler_params=PARAMS,
        cost_estimate=cost(8 * rows * w_size, 2 * w_size + 16 * rows * width),
    )(info, *blocks, *hot_w)
    return near, far


def pack(tokens, expert_ids, gate_values):
    tok_dev, width = tokens.shape
    meta = jnp.concatenate([expert_ids.astype(jnp.bfloat16), gate_values.astype(jnp.bfloat16)], axis=1)
    meta = meta.T.reshape(1, -1)
    meta = jnp.pad(meta, ((0, 7), (0, width - meta.shape[1])))
    return jnp.concatenate([tokens, meta], axis=0)


def route_kernel(info, a_ref, b_ref, *refs):
    send_ref, mix_ref, hot_mix_ref = refs[-3:]
    zh, c = info[Z_HI], info[CORE]
    n_slot, n_tok = mix_ref.shape
    tok_dev = n_tok // 2
    span_rows = tok_dev // SPANS

    def entry(k):
        at = slice(k * tok_dev, (k + 1) * tok_dev)
        row = jnp.concatenate(
            [a_ref[tok_dev : tok_dev + 8, at], b_ref[tok_dev : tok_dev + 8, at]], axis=1
        )
        return row.astype(jnp.float32)[:1]

    row = iota((1, n_tok), 1)
    group = row // span_rows
    span = group % SPANS
    hot = sum(jnp.where(span == s, info[s], 0) for s in range(SPANS)).astype(jnp.float32)

    slot = pl.program_id(0) * n_slot + iota((n_slot, 1), 0)
    dest, local = slot // 32, slot // 16 % 2
    expert = ((dest // 4 * 2 + zh) * 4 + dest % 4) * 4 + c * 2 + local
    expert = expert.astype(jnp.float32)
    gate = jnp.zeros((n_slot, n_tok), jnp.float32)
    hits = jnp.zeros((n_slot, n_tok), jnp.float32)
    hot_gate = jnp.zeros((1, n_tok), jnp.float32)
    for k in range(TOP_K):
        ids, gates = entry(k), entry(TOP_K + k)
        same = expert == ids
        gate = jnp.where(same, gates, gate)
        hits = jnp.where(same, 1.0, hits)
        hot_gate += jnp.where(ids == hot, gates, 0.0)
    named = jnp.where(expert == hot, 0.0, hits)
    before, after = iota((n_tok, n_tok), 0), iota((n_tok, n_tok), 1)
    earlier = (before // span_rows == after // span_rows) & (before < after)
    earlier = jnp.where(earlier, 1.0, 0.0).astype(jnp.bfloat16)
    rank = dot(named.astype(jnp.bfloat16), earlier, 1, 0)
    at = (slot // CAPACITY % (2 * SPANS)) == group
    chosen = (named > 0.5) & at & (rank == (slot % CAPACITY).astype(jnp.float32))
    pick = jnp.where(chosen, 1.0, 0.0).astype(jnp.bfloat16)
    sent = dot(pick[:, :tok_dev], a_ref[:tok_dev], 1, 0)
    sent += dot(pick[:, tok_dev:], b_ref[:tok_dev], 1, 0)
    send_ref[...] = sent.astype(jnp.bfloat16).reshape(send_ref.shape)
    mix_ref[...] = jnp.where(chosen, gate, 0.0).astype(jnp.bfloat16)
    hot_row = iota((2 * span_rows, 1), 0)
    hot_row = hot_row // span_rows * tok_dev + (2 * zh + c) * span_rows + hot_row % span_rows
    hot_mix_ref[...] = jnp.where(hot_row == row, hot_gate, 0.0).astype(jnp.bfloat16)


def route(info, a, b, tok_dev, half, base=()):
    width = a.shape[1]
    n_slot = 32 * 2 * SPANS * CAPACITY
    n_dest = 16
    steps = 4
    span_rows = tok_dev // SPANS
    rows = n_slot // n_dest
    shapes = (
        jax.ShapeDtypeStruct((n_dest, 2 * rows, width), jnp.bfloat16),
        jax.ShapeDtypeStruct((n_slot, 2 * tok_dev), jnp.bfloat16),
        jax.ShapeDtypeStruct((2 * span_rows, 2 * tok_dev), jnp.bfloat16),
    )
    return pl.pallas_call(
        route_kernel,
        out_shape=shapes,
        grid_spec=pltpu.PrefetchScalarGridSpec(
            num_scalar_prefetch=1,
            grid=(steps,),
            in_specs=[whole(a.shape), whole(b.shape)]
            + [pl.BlockSpec(memory_space=pl.ANY)] * len(base),
            out_specs=(
                pl.BlockSpec((n_dest // steps, rows, width), lambda i, info: (i, half, 0)),
                pl.BlockSpec((n_slot // steps, 2 * tok_dev), lambda i, info: (i, 0)),
                whole(shapes[2].shape),
            ),
        ),
        input_output_aliases={3: 0} if base else {},
        compiler_params=PARAMS,
        cost_estimate=cost(4 * n_slot * tok_dev * width, 2 * width * (n_slot + 2 * tok_dev)),
    )(info, a, b, *base)


def ffn_kernel(info, x_ref, gate_ref, up_ref, down_ref, *out_refs):
    n_src, rows, width = x_ref.shape
    x = x_ref[...].reshape(n_src * rows, width)
    gate = dot(x, gate_ref[0], 1, 1)
    up = dot(x, up_ref[0], 1, 1)
    hidden = (jax.nn.silu(gate) * up).astype(jnp.bfloat16)
    if len(out_refs) == 1:
        out = dot(hidden, down_ref[0], 1, 0).astype(jnp.bfloat16)
        out_refs[0][...] = out.reshape(n_src, rows, width)
        return
    cols = width // len(out_refs)
    for i, out_ref in enumerate(out_refs):
        start = pl.multiple_of((info[TENSOR] ^ i) * cols, cols)
        out = dot(hidden, down_ref[0, :, pl.ds(start, cols)], 1, 0).astype(jnp.bfloat16)
        out_ref[...] = out.reshape(n_src, rows, cols)


def ffn(info, x, w_gate, w_up, w_down, half, groups):
    n_src, rows, width = x.shape
    exp_dev, units, _ = w_gate.shape
    rows //= 2
    cols = width // groups
    block = (n_src, rows // exp_dev)
    w_spec = pl.BlockSpec((1, units, width), lambda e, info: (e, 0, 0))
    return pl.pallas_call(
        ffn_kernel,
        out_shape=[jax.ShapeDtypeStruct((n_src, rows, cols), jnp.bfloat16)] * groups,
        grid_spec=pltpu.PrefetchScalarGridSpec(
            num_scalar_prefetch=1,
            grid=(exp_dev,),
            in_specs=[
                pl.BlockSpec((*block, width), lambda e, info: (0, half * exp_dev + e, 0)),
                w_spec,
                w_spec,
                w_spec,
            ],
            out_specs=[pl.BlockSpec((*block, cols), lambda e, info: (0, e, 0))] * groups,
        ),
        compiler_params=PARAMS,
        cost_estimate=cost(6 * n_src * rows * units * width, 2 * x.size + 6 * w_gate.size),
    )(info, x, w_gate, w_up, w_down)


def mix_kernel(info, mix_ref, hot_mix_ref, ret_ref, hot_ref, own_ref, other_ref):
    out = dot(mix_ref[...], ret_ref[...], 0, 0) + dot(hot_mix_ref[...], hot_ref[...], 0, 0)
    out = out.astype(jnp.bfloat16)
    half = out.shape[0] // 2
    own_ref[0] = out[:half]
    other_ref[0] = out[half:]


def mix_rows(info, mix, hot_mix, returned, hot):
    n_slot, n_tok = mix.shape
    width = returned.shape[1]
    n_group = lax.axis_size("t")
    cols = width // n_group
    shape = jax.ShapeDtypeStruct((n_group, n_tok // 2, cols), jnp.bfloat16)
    out = pl.BlockSpec((1, n_tok // 2, cols), lambda i, info: (i, 0, 0))
    return pl.pallas_call(
        mix_kernel,
        out_shape=(shape, shape),
        grid_spec=pltpu.PrefetchScalarGridSpec(
            num_scalar_prefetch=1,
            grid=(n_group,),
            in_specs=[
                whole(mix.shape),
                whole(hot_mix.shape),
                pl.BlockSpec((n_slot, cols), lambda i, info: (0, i ^ info[TENSOR])),
                pl.BlockSpec((hot.shape[0], cols), lambda i, info: (0, i ^ info[TENSOR])),
            ],
            out_specs=(out, out),
        ),
        compiler_params=PARAMS,
        cost_estimate=cost(2 * n_slot * n_tok * width, 2 * width * (n_slot + n_tok)),
    )(info, mix, hot_mix, returned, hot)


def mix_quarter_kernel(mix_ref, hot_mix_ref, ret_ref, hot_ref, own_ref, other_ref):
    out = dot(mix_ref[...], ret_ref[...], 0, 0) + dot(hot_mix_ref[...], hot_ref[...], 0, 0)
    half = out.shape[0] // 2
    own_ref[...] = out[:half]
    other_ref[...] = out[half:].astype(jnp.bfloat16)


def mix_quarter(mix, hot_mix, returned, hot):
    rows, cols = mix.shape[1] // 2, returned.shape[1]
    return pl.pallas_call(
        mix_quarter_kernel,
        out_shape=(
            jax.ShapeDtypeStruct((rows, cols), jnp.float32),
            jax.ShapeDtypeStruct((rows, cols), jnp.bfloat16),
        ),
        compiler_params=PARAMS,
        cost_estimate=cost(2 * mix.size * cols, 2 * (mix.size + returned.size)),
    )(mix, hot_mix, returned, hot)


def exchange(send):
    return lax.all_to_all(send, ("y", "x"), 0, 0, tiled=True)


def to_t(groups, *shifts):
    pairs = range(len(groups))
    return tuple(lax.ppermute(groups[k], "t", [(i, i ^ k) for i in pairs]) for k in shifts)


def total_of(parts):
    return sum(part.astype(jnp.float32) for part in parts).astype(jnp.bfloat16)


def per_device(tokens, expert_ids, gate_values, hot_ids, w_gate, w_up, w_down):
    y, zh, x, c, t = (lax.axis_index(name) for name in ("y", "zh", "x", "c", "t"))
    n_t = lax.axis_size("t")
    tok_dev, width = tokens.shape
    place = jnp.stack([(y * 2 + zh) * 4 + x, zh, c, t, 0]).astype(jnp.int32)
    info = jnp.concatenate([hot_ids, place])
    experts = (w_gate, w_up, w_down)

    own = pack(tokens, expert_ids, gate_values)
    own_z = lax.ppermute(own, "zh", SWAP)
    own_c = lax.ppermute(own, "c", SWAP)
    rows, near_mix, near_hot_mix = route(info, own, own_c, tok_dev, 0)
    n_slot = near_mix.shape[0]

    chunks = first_chunks(info, hot_ids, experts)
    own_zc = lax.ppermute(own_z, "c", SWAP)
    rows, far_mix, far_hot_mix = route(info, own_z, own_zc, tok_dev, 1, (rows,))
    rows, chunks = lax.optimization_barrier((rows, chunks))
    rows = exchange(rows)
    hot_w = along_y(own_span(info, chunks, c))
    rows, hot_w = lax.optimization_barrier((rows, hot_w))
    hot_w = (hot_w, shift_x(hot_w, 1), shift_x(hot_w, -1))
    far = ffn(info, rows, *experts, 1, n_t)
    far, rows = lax.optimization_barrier((tuple(far), rows))
    (near,) = ffn(info, rows, *experts, 0, 1)
    near, hot_w = lax.optimization_barrier((near, hot_w))
    near = exchange(near)
    half = hot_w[0].shape[0] // 2
    hot_w += (shift_x(hot_w[1][:half], 1), shift_x(hot_w[2][half:], -1))
    summands = (far[0], *to_t(far, 2))
    hot_w, summands = lax.optimization_barrier((hot_w, summands))
    far = total_of(summands + to_t(far, 3, 1))
    near_hot, far_hot = hot_ffn(info, (own_z, own_zc, own, own_c), hot_w, tok_dev // SPANS)
    mine, other = mix_rows(info, near_mix, near_hot_mix, near.reshape(n_slot, width), near_hot)
    got = lax.ppermute(other, "c", SWAP)
    mine, got, far, far_hot = lax.optimization_barrier((mine, got, far, far_hot))

    far = exchange(far).reshape(n_slot, width // n_t)
    pieces = [mine[k].astype(jnp.float32) + got[k].astype(jnp.float32) for k in range(n_t)]
    parts = to_t(
        [jnp.concatenate([p.astype(jnp.bfloat16), h]) for p, h in zip(pieces, far_hot)], 1, 2, 3
    )
    total = pieces[0] + sum(part[:tok_dev].astype(jnp.float32) for part in parts)
    far_hot = total_of((far_hot[0], *(part[tok_dev:] for part in parts)))
    far, total = lax.optimization_barrier((far, total))
    mine, other = mix_quarter(far_mix, far_hot_mix, far, far_hot)
    mine += lax.ppermute(other, "c", SWAP).astype(jnp.float32)
    got = lax.ppermute(mine.astype(jnp.bfloat16), "zh", SWAP)
    return (total + got.astype(jnp.float32)).astype(jnp.bfloat16)


def solution(mesh):
    fine = Mesh(mesh.devices.reshape(4, 2, 4, 2, 4), ("y", "zh", "x", "c", "t"))
    owner = ("y", "zh", "x", "c")
    in_specs = (
        P(owner, None),
        P(owner, None),
        P(owner, None),
        P(),
        P(owner, "t", None),
        P(owner, "t", None),
        P(owner, "t", None),
    )
    return jax.shard_map(
        per_device, mesh=fine, in_specs=in_specs, out_specs=P(owner, "t"), check_vma=False
    )
```
